32 devices in a mesh: fsdp: 2 (over x), ctx: 4 (over y, core), tp: 4 (over z).
Axes of the slice: x: 2, y: 2, z: 4, core: 2. Of those that a mesh axis runs over, the one named last changes fastest.
Arguments:
- inputs: bfloat16 [4, 16, 196, 768], P('fsdp', 'ctx', 'tp'), may hold values from -6 to 6
- cotangent: bfloat16 [4, 16, 196, 768], P('fsdp', 'ctx', 'tp'), may hold values from -6 to 6
- norm_gain: float32 [3, 768], replicated, may hold values from 0.5 to 1.5
- norm_bias: float32 [3, 768], replicated, may hold values from -1 to 1
- attn_weight: bfloat16 [2, 3, 768, 768], P(None, None, 'fsdp', 'tp'), may hold values from -0.21875 to 0.21875
- attn_bias: float32 [2, 2, 768], P(None, None, 'tp'), may hold values from -1 to 1
- out_weight: bfloat16 [2, 768, 768], P(None, 'tp', 'fsdp'), may hold values from -0.625 to 0.625
- out_bias: float32 [2, 768], replicated, may hold values from -1 to 1
- up_weight: bfloat16 [768, 3072], P('fsdp', 'tp'), may hold values from -0.21875 to 0.21875
- up_bias: float32 [3072], replicated, may hold values from -1 to 1
- down_weight: bfloat16 [3072, 768], P('tp', 'fsdp'), may hold values from -0.109375 to 0.109375
- down_bias: float32 [768], replicated, may hold values from -1 to 1
Outputs:
- outputs: bfloat16 [4, 16, 196, 768], P('fsdp', 'ctx', 'tp')
- input_grad: bfloat16 [4, 16, 196, 768], P('fsdp', 'ctx', 'tp')
- grad_norm_gain: float32 [3, 768], replicated
- grad_norm_bias: float32 [3, 768], replicated
- grad_attn_weight: float32 [2, 3, 768, 768], P(None, None, ('fsdp', 'ctx'), 'tp')
- grad_attn_bias: float32 [2, 2, 768], P(None, None, 'tp')
- grad_out_weight: float32 [2, 768, 768], P(None, 'tp', ('fsdp', 'ctx'))
- grad_out_bias: float32 [2, 768], replicated
- grad_up_weight: float32 [768, 3072], P(('fsdp', 'ctx'), 'tp')
- grad_up_bias: float32 [3072], replicated
- grad_down_weight: float32 [3072, 768], P('tp', ('fsdp', 'ctx'))
- grad_down_bias: float32 [768], replicated
The draws below stay inside these ranges and needn't reach their ends.
All inputs are finite; a program needn't handle non-finite values.
Results may differ from the reference program's by a relative error of at most 0.025.
Values may be sent and summed in bfloat16 or wider, within the bound.
A program may use at most 128 MiB of HBM per device.

```python
import jax
import jax.numpy as jnp
from jax import lax

D = 768
HEADS = 12
HEAD = 64
FF = 3072
FRAMES = 16
PLACES = 196
CLIPS = 4


def block_scale(rng, shape, pieces, low, top_value):
    level, own = 1.0, jax.random.fold_in(rng, 6)
    for position, blocks in pieces:
        draws = jnp.exp(jax.random.uniform(jax.random.fold_in(own, position), (blocks,), jnp.float32, low / len(pieces), top_value / len(pieces)))
        level = level * jnp.repeat(draws, shape[position] // blocks).reshape([-1 if axis == position else 1 for axis in range(len(shape))])
    return level


def normal_values(stream_key, extent, scale, limit, split=(), dtype=jnp.bfloat16):
    values = jax.random.normal(stream_key, extent, jnp.float32) * scale
    if len(split) > 0:
        values = block_scale(stream_key, extent, split, -0.22, 0.18) * values
    return jnp.clip(values, min=-limit, max=limit).astype(dtype)


def setup_inputs(seed: int = 0) -> dict:
    key_of = jax.random.split(jax.random.key(seed), 13)
    inputs = normal_values(key_of[0], (CLIPS, FRAMES, PLACES, D), 1.0, 6.0, ((0, 2), (1, 4), (2, 4)))
    cotangent = normal_values(key_of[1], (CLIPS, FRAMES, PLACES, D), 1.0, 6.0, ((0, 2), (1, 4), (2, 4)))
    norm_gain = jnp.clip(1.0 + 0.1 * jax.random.normal(key_of[2], (3, D), jnp.float32), 0.5, 1.5)
    norm_bias = normal_values(key_of[3], (3, D), 0.2, 1.0, (), jnp.float32)
    attn_weight = normal_values(key_of[4], (2, 3, D, D), D ** -0.5, 0.21875, ((2, 2), (3, 4)))
    attn_bias = normal_values(key_of[5], (2, 2, D), 0.2, 1.0, ((2, 4),), jnp.float32)
    out_weight = normal_values(key_of[6], (2, D, D), (D // 8) ** -0.5, 0.625, ((1, 4), (2, 2)))
    out_bias = normal_values(key_of[7], (2, D), 0.2, 1.0, (), jnp.float32)
    up_weight = normal_values(key_of[8], (D, FF), D ** -0.5, 0.21875, ((0, 2), (1, 4)))
    up_bias = normal_values(key_of[9], (FF,), 0.2, 1.0, (), jnp.float32)
    down_weight = normal_values(key_of[10], (FF, D), FF ** -0.5, 0.109375, ((0, 4), (1, 2)))
    down_bias = normal_values(key_of[11], (D,), 0.2, 1.0, (), jnp.float32)
    return dict(inputs=inputs, cotangent=cotangent, norm_gain=norm_gain, norm_bias=norm_bias, attn_weight=attn_weight, attn_bias=attn_bias, out_weight=out_weight, out_bias=out_bias, up_weight=up_weight, up_bias=up_bias, down_weight=down_weight, down_bias=down_bias)


@jax.custom_vjp
def low(v):
    return lax.optimization_barrier(v.astype(jnp.bfloat16)).astype(jnp.float32)

@jax.custom_vjp
def low_back(v):
    return v

def low_keep(v):
    return (low(v), None)

def low_pass(kept, grad):
    return (grad,)

def back_keep(v):
    return (v, None)

def back_low(kept, grad):
    return (low(grad),)
low.defvjp(low_keep, low_pass)
low_back.defvjp(back_keep, back_low)
EPSILON = 1e-06
HIGH = lax.Precision.HIGHEST

def layer_norm(rows, gain, shift):
    centre = rows - lax.optimization_barrier(jnp.mean(rows, axis=-1, keepdims=True))
    spread = lax.optimization_barrier(jnp.mean(centre * centre, axis=-1, keepdims=True))
    return centre * lax.rsqrt(spread + EPSILON) * gain + shift

def attention(triple, temporal):
    shaped = triple.reshape(triple.shape[:3] + (HEADS, HEAD))
    if temporal:
        score_form = 'qbhe,kbhe->bhqk'
        mix_form = 'bhqk,kbhe->qbhe'
    else:
        score_form = 'bqhe,bkhe->bhqk'
        mix_form = 'bhqk,bkhe->bqhe'
    scores = low_back(jnp.einsum(score_form, shaped[0], shaped[1], precision=HIGH) * 0.125)
    weights = low(jax.nn.softmax(scores, axis=-1))
    mixed = jnp.einsum(mix_form, weights, shaped[2], precision=HIGH)
    return low(low_back(mixed.reshape(triple.shape[1:])))

def sublayer(stream, index, gain, shift, attn_w, attn_b, out_w, out_b, temporal):
    normed = low(layer_norm(stream, gain[index], shift[index]))
    zero_row = jnp.zeros_like(attn_b[index, 0])
    bias_rows = jnp.stack([attn_b[index, 0], zero_row, attn_b[index, 1]])
    triple = jnp.einsum('fpd,jdc->jfpc', normed, attn_w[index], precision=HIGH) + bias_rows[:, None, None, :]
    triple = low(low_back(triple))
    mixed = attention(triple, temporal)
    branch = low_back(jnp.einsum('fpc,cd->fpd', mixed, out_w[index], precision=HIGH) + out_b[index])
    return stream + branch

def block(clip, norm_gain, norm_bias, attn_weight, attn_bias, out_weight, out_bias, up_weight, up_bias, down_weight, down_bias):
    spatial = sublayer(clip, 0, norm_gain, norm_bias, attn_weight, attn_bias, out_weight, out_bias, False)
    across = sublayer(spatial, 1, norm_gain, norm_bias, attn_weight, attn_bias, out_weight, out_bias, True)
    normed = low(layer_norm(across, norm_gain[2], norm_bias[2]))
    hidden = low_back(jnp.einsum('fpd,dc->fpc', normed, up_weight, precision=HIGH) + up_bias)
    active = low(jax.nn.gelu(hidden, approximate=False))
    branch = low_back(jnp.einsum('fpc,cd->fpd', active, down_weight, precision=HIGH) + down_bias)
    return across + branch

def reference(inputs, cotangent, norm_gain, norm_bias, attn_weight, attn_bias, out_weight, out_bias, up_weight, up_bias, down_weight, down_bias):
    params = (norm_gain, norm_bias, attn_weight.astype(jnp.float32), attn_bias, out_weight.astype(jnp.float32), out_bias, up_weight.astype(jnp.float32), up_bias, down_weight.astype(jnp.float32), down_bias)

    def step(totals, pair):
        clip, grad_clip = pair
        result, pull = jax.vjp(block, clip.astype(jnp.float32), *params)
        grads = pull(grad_clip.astype(jnp.float32))
        totals = tuple((total + extra for total, extra in zip(totals, grads[1:])))
        return (totals, (result.astype(jnp.bfloat16), grads[0].astype(jnp.bfloat16)))
    start = tuple((jnp.zeros_like(param) for param in params))
    totals, stacked = lax.scan(step, start, (inputs, cotangent))
    return (stacked[0], stacked[1], totals[0], totals[1], totals[2], totals[3], totals[4], totals[5], totals[6], totals[7], totals[8], totals[9])
```

```python
import jax
import jax.numpy as jnp
from jax import lax
from jax.sharding import PartitionSpec as P

HEAD = 64
EPSILON = 1e-06
BF = jnp.bfloat16
F32 = jnp.float32


def layer_norm(rows, gain, shift):
    centre = rows - jnp.mean(rows, axis=-1, keepdims=True)
    spread = jnp.mean(centre * centre, axis=-1, keepdims=True)
    return centre * lax.rsqrt(spread + EPSILON) * gain + shift


def gelu_exact(values):
    return jax.nn.gelu(values, approximate=False)


def dot(form, a, b):
    return jnp.einsum(form, a, b, preferred_element_type=F32)


def attend(q, k, v):
    scores = dot("hgqe,hgke->hgqk", q, k) * 0.125
    highest = jnp.max(scores, axis=-1, keepdims=True)
    log_total = highest + jnp.log(jnp.sum(jnp.exp(scores - highest), axis=-1, keepdims=True))
    weights = jnp.exp(scores - log_total).astype(BF)
    return dot("hgqk,hgke->hgqe", weights, v).astype(BF), log_total


def attend_back(q, k, v, log_total, grad):
    probs = jnp.exp(dot("hgqe,hgke->hgqk", q, k) * 0.125 - log_total)
    grad_probs = dot("hgqe,hgke->hgqk", grad, v)
    inner = jnp.sum(probs * grad_probs, axis=-1, keepdims=True)
    grad_scores = (probs * (grad_probs - inner)).astype(BF)
    grad_q = dot("hgqk,hgke->hgqe", grad_scores, k) * 0.125
    grad_k = dot("hgqk,hgqe->hgke", grad_scores, q) * 0.125
    grad_v = dot("hgqk,hgqe->hgke", probs.astype(BF), grad)
    return jnp.stack([grad_q, grad_k, grad_v]).astype(BF)


def local(
    inputs,
    cotangent,
    norm_gain,
    norm_bias,
    attn_weight,
    attn_bias,
    out_weight,
    out_bias,
    up_weight,
    up_bias,
    down_weight,
    down_bias,
):
    ranks_f, ranks_c, ranks_t = (lax.axis_size("fsdp"), lax.axis_size("ctx"), lax.axis_size("tp"))
    everyone = ("fsdp", "ctx", "tp")
    ctx_rank = lax.axis_index("ctx")
    tp_rank = lax.axis_index("tp")
    clips, frames, places, model = inputs.shape
    width = attn_weight.shape[3]
    hidden = up_weight.shape[1]
    heads = model // HEAD
    shards = ranks_f * ranks_c

    def gather_rows(shard):
        rows = shard.shape[0] // ranks_c
        part = lax.dynamic_slice_in_dim(shard, ctx_rank * rows, rows, 0)
        return lax.all_gather(part, everyone, axis=0, tiled=False).reshape(
            (ranks_f, ranks_c, ranks_t, rows, shard.shape[1])
        )

    def full_in(shard):
        whole = gather_rows(shard)
        return whole.transpose(0, 1, 3, 2, 4).reshape(shard.shape[0] * ranks_f, -1)

    def full_out(shard):
        whole = gather_rows(shard)
        return whole.transpose(2, 1, 3, 0, 4).reshape(shard.shape[0] * ranks_t, -1)

    qkv_full = []
    out_full = []
    for layer in range(2):
        packed = attn_weight[layer].transpose(1, 0, 2).reshape(attn_weight.shape[2], 3 * width)
        whole = full_in(packed).reshape(model, ranks_t, 3, width)
        qkv_full.append(whole.transpose(2, 0, 1, 3).reshape(3, model, ranks_t * width))
        out_full.append(full_out(out_weight[layer]))
    up_full = full_in(up_weight)
    down_full = full_out(down_weight)
    attn_bias_full = lax.all_gather(attn_bias, "tp", axis=2, tiled=True)

    total_frames = frames * ranks_c
    pairs = clips * places
    share = -(-pairs // ranks_c)

    def home_to_spatial(values):
        return lax.all_to_all(values, "tp", split_axis=1, concat_axis=2, tiled=True)

    def spatial_to_home(values):
        return lax.all_to_all(values, "tp", split_axis=2, concat_axis=1, tiled=True)

    def home_to_temporal(values):
        rows = values.transpose(1, 0, 2, 3).reshape(frames, pairs, model)
        rows = jnp.pad(rows, ((0, 0), (0, share * ranks_c - pairs), (0, 0)))
        return lax.all_to_all(rows, "ctx", split_axis=1, concat_axis=0, tiled=True)

    def temporal_to_home(values):
        rows = lax.all_to_all(values, "ctx", split_axis=0, concat_axis=1, tiled=True)[:, :pairs]
        return rows.reshape(frames, clips, places, model).transpose(1, 0, 2, 3)

    def heads_apart(values, temporal):
        apart = values.reshape(values.shape[:2] + (heads, HEAD))
        return apart.transpose(2, 1, 0, 3) if temporal else apart.transpose(2, 0, 1, 3)

    def heads_joined(values, temporal):
        joined = values.transpose(2, 1, 0, 3) if temporal else values.transpose(1, 2, 0, 3)
        return joined.reshape(joined.shape[:2] + (model,))

    def attn_forward(stream, index, temporal):
        normed = layer_norm(stream, norm_gain[index], norm_bias[index]).astype(BF)
        biases = (attn_bias_full[index, 0], 0.0, attn_bias_full[index, 1])
        triple = [
            heads_apart((dot("abd,dc->abc", normed, qkv_full[index][j]) + biases[j]).astype(BF), temporal)
            for j in range(3)
        ]
        mixed, log_total = attend(*triple)
        mixed = heads_joined(mixed, temporal)
        stream_next = stream + (dot("abc,cd->abd", mixed, out_full[index]) + out_bias[index])
        return stream_next, (normed, triple, log_total, mixed)

    def attn_backward(stream, index, kept, grad_stream, temporal):
        normed, triple, log_total, mixed = kept
        grad_branch = grad_stream.astype(BF)
        grad_bias_out = jnp.sum(grad_branch.astype(F32), axis=(0, 1))
        grad_weight_out = dot("abc,abd->cd", mixed, grad_branch)
        grad_mixed = dot("abd,cd->abc", grad_branch, out_full[index]).astype(BF)
        grad_triple = attend_back(*triple, log_total, heads_apart(grad_mixed, temporal))
        grad_triple = [heads_joined(grad_triple[j], temporal) for j in range(3)]
        grad_weight_attn = [dot("abd,abc->dc", normed, g) for g in grad_triple]
        sums = [jnp.sum(g.astype(F32), axis=(0, 1)) for g in grad_triple]
        grad_normed = sum(
            dot("abc,dc->abd", grad_triple[j], qkv_full[index][j]) for j in range(3)
        )
        unused, pull = jax.vjp(layer_norm, stream, norm_gain[index], norm_bias[index])
        grad_input, grad_gain, grad_shift = pull(grad_normed)
        return grad_stream + grad_input, (
            grad_gain,
            grad_shift,
            grad_weight_attn,
            jnp.stack([sums[0], sums[2]]),
            grad_weight_out,
            grad_bias_out,
        )

    first = home_to_spatial(inputs)
    spatial_shape = first.shape
    first = first.reshape((-1,) + first.shape[2:]).astype(F32)
    second, kept_spatial = attn_forward(first, 0, False)
    second = home_to_temporal(
        spatial_to_home(second.astype(BF).reshape(spatial_shape))
    ).astype(F32)
    third, kept_temporal = attn_forward(second, 1, True)
    normed = layer_norm(third, norm_gain[2], norm_bias[2]).astype(BF)
    units = dot("abd,dc->abc", normed, up_full) + up_bias
    active = gelu_exact(units).astype(BF)
    result = third + (dot("abc,cd->abd", active, down_full) + down_bias)
    outputs = temporal_to_home(result.astype(BF))

    grad_out = home_to_temporal(cotangent)
    grad_bias_down = jnp.sum(grad_out.astype(F32), axis=(0, 1))
    grad_weight_down = dot("abc,abd->cd", active, grad_out)
    grad_active = dot("abd,cd->abc", grad_out, down_full)
    unused, pull_gelu = jax.vjp(gelu_exact, units)
    grad_units = pull_gelu(grad_active)[0].astype(BF)
    grad_bias_up = jnp.sum(grad_units.astype(F32), axis=(0, 1))
    grad_weight_up = dot("abd,abc->dc", normed, grad_units)
    grad_normed = dot("abc,dc->abd", grad_units, up_full)
    unused, pull = jax.vjp(layer_norm, third, norm_gain[2], norm_bias[2])
    grad_third, gain_mlp, shift_mlp = pull(grad_normed)
    grad_third = grad_third + grad_out.astype(F32)

    def scatter(blocks):
        return lax.psum_scatter(blocks.astype(BF), everyone, scatter_dimension=0, tiled=False).astype(F32)

    def blocks_in(grad):
        rows, columns = grad.shape
        parts = grad.reshape(shards, rows // shards, ranks_t, columns // ranks_t)
        return parts.transpose(0, 2, 1, 3).reshape(shards * ranks_t, rows // shards, columns // ranks_t)

    def blocks_out(grad):
        rows, columns = grad.shape
        parts = grad.reshape(ranks_t, rows // ranks_t, shards, columns // shards)
        return parts.transpose(2, 0, 1, 3).reshape(shards * ranks_t, rows // ranks_t, columns // shards)

    own_up = scatter(blocks_in(grad_weight_up.astype(BF)))
    own_down = scatter(blocks_out(grad_weight_down.astype(BF)))

    grad_second, temporal_terms = attn_backward(second, 1, kept_temporal, grad_third, True)
    grad_second = home_to_spatial(temporal_to_home(grad_second.astype(BF)))
    grad_second = grad_second.reshape(first.shape).astype(F32)
    grad_first, spatial_terms = attn_backward(first, 0, kept_spatial, grad_second, False)
    input_grad = spatial_to_home(grad_first.astype(BF).reshape(spatial_shape))

    own_attn = []
    own_out = []
    for terms in (spatial_terms, temporal_terms):
        own_attn.append(
            scatter(jnp.stack([blocks_in(g.astype(BF)) for g in terms[2]], axis=1))
        )
        own_out.append(scatter(blocks_out(terms[4].astype(BF))))

    vectors = lax.psum(
        (
            jnp.stack([spatial_terms[0], temporal_terms[0], gain_mlp]),
            jnp.stack([spatial_terms[1], temporal_terms[1], shift_mlp]),
            jnp.stack([spatial_terms[3], temporal_terms[3]]),
            jnp.stack([spatial_terms[5], temporal_terms[5]]),
            grad_bias_up,
            grad_bias_down,
        ),
        everyone,
    )
    attn_bias_part = lax.dynamic_slice_in_dim(vectors[2], tp_rank * width, width, 2)
    return (
        outputs,
        input_grad,
        vectors[0],
        vectors[1],
        jnp.stack(own_attn),
        attn_bias_part,
        jnp.stack(own_out),
        vectors[3],
        own_up,
        vectors[4],
        own_down,
        vectors[5],
    )


def solution(mesh):
    return jax.shard_map(
        local,
        mesh=mesh,
        in_specs=(
            P("fsdp", "ctx", "tp", None),
            P("fsdp", "ctx", "tp", None),
            P(),
            P(),
            P(None, None, "fsdp", "tp"),
            P(None, None, "tp"),
            P(None, "tp", "fsdp"),
            P(),
            P("fsdp", "tp"),
            P(),
            P("tp", "fsdp"),
            P(),
        ),
        out_specs=(
            P("fsdp", "ctx", "tp", None),
            P("fsdp", "ctx", "tp", None),
            P(),
            P(),
            P(None, None, ("fsdp", "ctx"), "tp"),
            P(None, None, "tp"),
            P(None, "tp", ("fsdp", "ctx")),
            P(),
            P(("fsdp", "ctx"), "tp"),
            P(),
            P("tp", ("fsdp", "ctx")),
            P(),
        ),
        check_vma=False,
    )
```

```python
import jax
import jax.numpy as jnp
from jax import lax
from jax.experimental import pallas as pl
from jax.experimental.pallas import tpu as pltpu
from jax.sharding import PartitionSpec as P

HEAD = 64
EPSILON = 1e-06
BF = jnp.bfloat16
F32 = jnp.float32
MESH = pl.DeviceIdType.MESH
PIECES = 4
ALL = ("fsdp", "ctx", "tp")


def places_of(x, y, k, z):
    return {
        "x": (1 - x, y * 2 + k, z),
        "y": (x, (1 - y) * 2 + k, z),
        "core": (x, y * 2 + 1 - k, z),
        "up": (x, y * 2 + k, z + 1),
        "down": (x, y * 2 + k, z - 1),
        "z1": (x, y * 2 + k, (z // 2) * 2 + 1 - z % 2),
        "z2": (x, y * 2 + k, (z + 2) % 4),
    }


def meet(places, sides, z, last):
    barrier = pltpu.get_barrier_semaphore()
    for side in sides:
        pl.semaphore_signal(barrier, inc=1, device_id=places[side], device_id_type=MESH)

    @pl.when(z < last)
    def _():
        pl.semaphore_signal(barrier, inc=1, device_id=places["up"], device_id_type=MESH)

    @pl.when(z > 0)
    def _():
        pl.semaphore_signal(barrier, inc=1, device_id=places["down"], device_id_type=MESH)

    inner = (z > 0).astype(jnp.int32) + (z < last).astype(jnp.int32)
    pl.semaphore_wait(barrier, len(sides) + inner)


def maybe(when, action):
    if when is None:
        action()
    else:
        pl.when(when)(action)


def gather_kernel(shard, whole, send_sem, recv_sem, local_sem):
    x, c, z = lax.axis_index("fsdp"), lax.axis_index("ctx"), lax.axis_index("tp")
    y, k = c // 2, c % 2
    rows = shard.shape[1] // 4
    width = shard.shape[2]
    last = 3
    places = places_of(x, y, k, z)

    def spot(ref, piece, f, cc, t):
        row = pl.multiple_of((f * 4 + cc) * rows, 16)
        return ref.at[piece, pl.ds(row, rows), pl.ds(pl.multiple_of(t * width, 128), width)]

    meet(places, ("x", "y", "core"), z, last)
    local = []
    for piece in range(PIECES):
        row = pl.multiple_of(x * rows * 4, 16)
        copy = pltpu.make_async_copy(
            shard.at[piece],
            whole.at[piece, pl.ds(row, rows * 4), pl.ds(pl.multiple_of(z * width, 128), width)],
            local_sem.at[piece],
        )
        copy.start()
        local.append(copy)

    sent = []

    def send(side, unit, mine=False, pieces=range(PIECES), when=None):
        f, cc, t = unit
        copies = []
        for piece in pieces:
            target = spot(whole, piece, f, cc, t)
            source = shard.at[piece, pl.ds(pl.multiple_of(cc * rows, 16), rows)] if mine else target
            number = sum(len(c) for w, c in sent) + len(copies)
            copies.append(
                pltpu.make_async_remote_copy(
                    src_ref=source,
                    dst_ref=target,
                    send_sem=send_sem.at[number],
                    recv_sem=recv_sem.at[(f * 4 + cc) * 4 + t, piece],
                    device_id=places[side],
                    device_id_type=MESH,
                )
            )
        sent.append((when, copies))

        def start():
            for copy in copies:
                copy.start()

        maybe(when, start)

    def arrived(unit, when=None):
        f, cc, t = unit

        def wait():
            for piece in range(PIECES):
                ref = spot(whole, piece, f, cc, t)
                pltpu.make_async_copy(ref, ref, recv_sem.at[(f * 4 + cc) * 4 + t, piece]).wait()

        maybe(when, wait)

    other_y = (1 - y) * 2 + k
    first, second = (0, 1), (2, 3)
    me = (x, c, z)
    send("up", me, True, when=z < last)
    send("down", me, True, when=z > 0)
    send("x", me, True)
    send("x", (x, other_y, z), True)

    def at(sign, d):
        t = z + sign * d
        return t, ((t >= 0) if sign < 0 else (t <= last))

    def from_line(sign, d):
        t, have = at(sign, d)
        unit = (x, c, t)
        arrived(unit, have)
        if d < last:
            if sign < 0:
                send("up", unit, when=have & (z < last))
            else:
                send("down", unit, when=have & (z > 0))
        for side in ("x", "y", "core"):
            send(side, unit, when=have)

    def from_plane(sign, d):
        t, have = at(sign, d)
        arrived((1 - x, c, t), have)
        send("y", (1 - x, c, t), pieces=second, when=have)
        send("core", (1 - x, c, t), when=have)
        arrived((x, other_y, t), have)
        send("x", (x, other_y, t), pieces=first, when=have)
        send("core", (x, other_y, t), when=have)

    def from_diagonal(sign, d):
        t, have = at(sign, d)
        arrived((1 - x, other_y, t), have)
        send("core", (1 - x, other_y, t), when=have)

    def both(action, d):
        action(-1, d)
        action(1, d)

    both(from_line, 1)
    arrived((1 - x, c, z))
    send("core", (1 - x, c, z))
    both(from_line, 2)
    arrived((1 - x, other_y, z))
    send("core", (1 - x, other_y, z))
    both(from_plane, 1)
    both(from_line, 3)
    both(from_plane, 2)
    both(from_diagonal, 1)
    both(from_plane, 3)
    both(from_diagonal, 2)
    both(from_diagonal, 3)
    for sign, d in ((-1, 1), (1, 1), (-1, 2), (1, 2), (-1, 3), (1, 3)):
        t, have = at(sign, d)
        for f in (x, 1 - x):
            for yy in (y, 1 - y):
                arrived((f, yy * 2 + 1 - k, t), have)
    for yy in (y, 1 - y):
        arrived((1 - x, yy * 2 + 1 - k, z))
    for when, copies in sent:

        def wait():
            for copy in copies:
                copy.wait_send()

        maybe(when, wait)
    for copy in local:
        copy.wait()


def gather(shard):
    ranks = (lax.axis_size("fsdp"), lax.axis_size("ctx"), lax.axis_size("tp"))
    rows, width = shard.shape[1:]
    if ranks != (2, 4, 4):
        part = rows // ranks[1]
        mine = lax.dynamic_slice_in_dim(shard, lax.axis_index("ctx") * part, part, 1)
        tall = lax.all_gather(mine, ("fsdp", "ctx"), axis=1, tiled=True)
        return lax.all_gather(tall, "tp", axis=2, tiled=True)
    return pl.pallas_call(
        gather_kernel,
        out_shape=jax.ShapeDtypeStruct((PIECES, rows * 2, width * 4), BF),
        in_specs=[pl.BlockSpec(memory_space=pltpu.VMEM)],
        out_specs=pl.BlockSpec(memory_space=pl.ANY),
        scratch_shapes=[
            pltpu.SemaphoreType.DMA((260,)),
            pltpu.SemaphoreType.DMA((32, PIECES)),
            pltpu.SemaphoreType.DMA((PIECES,)),
        ],
        compiler_params=pltpu.CompilerParams(collective_id=0, has_side_effects=True),
        name="gather_weights",
    )(shard)


STEPS = 16


def scatter_kernel(
    g_ref, v_ref, out_ref, vout_ref, own, r1, r2, r3x, r3y, rup, rdn, vr, va,
    own_sem, s1, q1, s2, q2, s3a, s3b, q3x, q3y, sz, qup, qdn, vs, vq,
):
    x, c, z = lax.axis_index("fsdp"), lax.axis_index("ctx"), lax.axis_index("tp")
    y, k = c // 2, c % 2
    rows, width = out_ref.shape[1:]
    last = 3
    places = places_of(x, y, k, z)
    meet(places, ("x", "y", "core", "z2"), z, last)

    def tp_of(s):
        return (3 * s) % 4

    def spot(f, yy, kk, s):
        row = pl.multiple_of((f * 4 + yy * 2 + kk) * rows, 16)
        column = pl.multiple_of(tp_of(s) * width, 128)
        return g_ref.at[s // 4, pl.ds(row, rows), pl.ds(column, width)]

    def remote(src, dst, send, recv, side):
        return pltpu.make_async_remote_copy(
            src_ref=src, dst_ref=dst, send_sem=send, recv_sem=recv,
            device_id=places[side], device_id_type=MESH,
        )

    def core_copy(s, f, yy):
        return remote(
            spot(f, yy, 1 - k, s), r1.at[s, f, yy], s1.at[s, f, yy], q1.at[s, f, yy], "core"
        )

    def own_copy(s, f, yy):
        return pltpu.make_async_copy(spot(f, yy, k, s), own.at[s, f, yy], own_sem.at[s, f, yy])

    def diag_copy(s, side):
        return remote(r1.at[s, 1 - x, 1 - y], r2.at[s], s2.at[s], q2.at[s], side)

    def x_copy(s):
        return remote(r1.at[s, 1 - x, y], r3x.at[s], s3a.at[s], q3x.at[s], "x")

    def y_copy(s):
        return remote(r1.at[s, x, 1 - y], r3y.at[s], s3b.at[s], q3y.at[s], "y")

    def up_copy(s):
        return remote(r1.at[s, x, y], rup.at[s], sz.at[s], qup.at[s], "up")

    def down_copy(s):
        return remote(r1.at[s, x, y], rdn.at[s], sz.at[s], qdn.at[s], "down")

    sides = ("core", "x", "y", "z1", "z2")

    def v_copy(j):
        return remote(va.at[j], vr.at[j], vs.at[j], vq.at[j], sides[j])

    quads = [(f, yy) for f in range(2) for yy in range(2)]

    def start(s, carry):
        for f, yy in quads:
            core_copy(s, f, yy).start()
            own_copy(s, f, yy).start()
        return carry

    lax.fori_loop(0, STEPS, start, 0)
    va[0] = v_ref[...]
    v_copy(0).start()

    def chip_sum(s):
        for f, yy in quads:
            core_copy(s, f, yy).wait_recv()
            own_copy(s, f, yy).wait()
            r1[s, f, yy] = r1[s, f, yy] + own[s, f, yy]

        @pl.when(s % 2 == 0)
        def _():
            diag_copy(s, "x").start()
            x_copy(s).start()

        @pl.when(s % 2 == 1)
        def _():
            diag_copy(s, "y").start()
            y_copy(s).start()

    def turn(s):
        diag_copy(s, "x").wait_recv()

        @pl.when(s % 2 == 0)
        def _():
            r1[s, x, 1 - y] = r1[s, x, 1 - y] + r2[s]
            y_copy(s).start()

        @pl.when(s % 2 == 1)
        def _():
            r1[s, 1 - x, y] = r1[s, 1 - x, y] + r2[s]
            x_copy(s).start()

    def plane_sum(s):
        x_copy(s).wait_recv()
        y_copy(s).wait_recv()
        total = r1[s, x, y].astype(F32) + r3x[s].astype(F32) + r3y[s].astype(F32)
        r1[s, x, y] = total.astype(BF)

    def line(s, hop):
        t = tp_of(s)

        @pl.when((z < t) & (z == hop))
        def _():
            if hop > 0:
                up_copy(s).wait_recv()
                r1[s, x, y] = r1[s, x, y] + rup[s]
            up_copy(s).start()

        @pl.when((z > t) & (last - z == hop))
        def _():
            if hop > 0:
                down_copy(s).wait_recv()
                r1[s, x, y] = r1[s, x, y] + rdn[s]
            down_copy(s).start()

        far = z + (last - 2 * z) * ((last - 2 * z) > 0).astype(jnp.int32)

        @pl.when((z == t) & (far == hop))
        def _():
            out_ref[s // 4] = r1[s, x, y].astype(F32)

            @pl.when(z > 0)
            def _():
                up_copy(s).wait_recv()
                out_ref[s // 4] = out_ref[s // 4] + rup[s].astype(F32)

            @pl.when(z < last)
            def _():
                down_copy(s).wait_recv()
                out_ref[s // 4] = out_ref[s // 4] + rdn[s].astype(F32)

    def guard(action, s, *rest):
        @pl.when((s >= 0) & (s < STEPS))
        def _():
            action(s, *rest)

    def step(s, carry):
        guard(chip_sum, s)
        guard(turn, s - 1)
        guard(plane_sum, s - 3)
        for hop in range(4):
            guard(line, s - 3 - hop, hop)
        for j in range(5):

            @pl.when(s == 2 + j)
            def _():
                v_copy(j).wait()
                if j < 4:
                    va[j + 1] = va[j] + vr[j]
                    v_copy(j + 1).start()
                else:
                    vout_ref[...] = va[j] + vr[j]

        return carry

    lax.fori_loop(0, STEPS + 6, step, 0)

    def finish(s, carry):
        for f, yy in quads:
            core_copy(s, f, yy).wait_send()
        diag_copy(s, "x").wait_send()
        x_copy(s).wait_send()
        y_copy(s).wait_send()

        @pl.when(z != tp_of(s))
        def _():
            up_copy(s).wait_send()

        return carry

    lax.fori_loop(0, STEPS, finish, 0)


def scatter(grads, vectors):
    ranks = (lax.axis_size("fsdp"), lax.axis_size("ctx"), lax.axis_size("tp"))
    rows = grads.shape[1] // (ranks[0] * ranks[1])
    width = grads.shape[2] // ranks[2]
    if ranks != (2, 4, 4):
        tall = lax.psum_scatter(grads, ("fsdp", "ctx"), scatter_dimension=1, tiled=True)
        own = lax.psum_scatter(tall, "tp", scatter_dimension=2, tiled=True)
        return own.astype(F32), lax.psum(vectors, ALL)
    sub = (rows, width)
    dma = pltpu.SemaphoreType.DMA
    return pl.pallas_call(
        scatter_kernel,
        out_shape=(
            jax.ShapeDtypeStruct((PIECES,) + sub, F32),
            jax.ShapeDtypeStruct(vectors.shape, F32),
        ),
        in_specs=[pl.BlockSpec(memory_space=pl.ANY), pl.BlockSpec(memory_space=pltpu.VMEM)],
        out_specs=[pl.BlockSpec(memory_space=pltpu.VMEM)] * 2,
        scratch_shapes=[pltpu.VMEM((STEPS, 2, 2) + sub, BF)] * 2
        + [pltpu.VMEM((STEPS,) + sub, BF)] * 5
        + [pltpu.VMEM((5,) + vectors.shape, F32)] * 2
        + [dma((STEPS, 2, 2))] * 3
        + [dma((STEPS,))] * 9
        + [dma((5,))] * 2,
        compiler_params=pltpu.CompilerParams(
            collective_id=1, has_side_effects=True, vmem_limit_bytes=48 * 2**20
        ),
        name="scatter_grads",
    )(grads, vectors)


def layer_norm(rows, gain, shift):
    centre = rows - jnp.mean(rows, axis=-1, keepdims=True)
    spread = jnp.mean(centre * centre, axis=-1, keepdims=True)
    return centre * lax.rsqrt(spread + EPSILON) * gain + shift


def gelu_exact(values):
    return jax.nn.gelu(values, approximate=False)


def dot(form, a, b):
    return jnp.einsum(form, a, b, preferred_element_type=F32)


def attend(q, k, v):
    scores = dot("hgqe,hgke->hgqk", q, k) * 0.125
    highest = jnp.max(scores, axis=-1, keepdims=True)
    log_total = highest + jnp.log(jnp.sum(jnp.exp(scores - highest), axis=-1, keepdims=True))
    weights = jnp.exp(scores - log_total).astype(BF)
    return dot("hgqk,hgke->hgqe", weights, v).astype(BF), log_total


def attend_back(q, k, v, log_total, grad):
    probs = jnp.exp(dot("hgqe,hgke->hgqk", q, k) * 0.125 - log_total)
    grad_probs = dot("hgqe,hgke->hgqk", grad, v)
    inner = jnp.sum(probs * grad_probs, axis=-1, keepdims=True)
    grad_scores = (probs * (grad_probs - inner)).astype(BF)
    grad_q = dot("hgqk,hgke->hgqe", grad_scores, k) * 0.125
    grad_k = dot("hgqk,hgqe->hgke", grad_scores, q) * 0.125
    grad_v = dot("hgqk,hgqe->hgke", probs.astype(BF), grad)
    return jnp.stack([grad_q, grad_k, grad_v]).astype(BF)


def local(
    inputs,
    cotangent,
    norm_gain,
    norm_bias,
    attn_weight,
    attn_bias,
    out_weight,
    out_bias,
    up_weight,
    up_bias,
    down_weight,
    down_bias,
):
    ranks_c, ranks_t = lax.axis_size("ctx"), lax.axis_size("tp")
    tp_rank = lax.axis_index("tp")
    clips, frames, places, model = inputs.shape
    width = attn_weight.shape[3]
    heads = model // HEAD

    shard = jnp.concatenate(
        [
            jnp.concatenate(
                [
                    attn_weight.transpose(0, 2, 1, 3).reshape(2, attn_weight.shape[2], 3 * width),
                    out_weight.transpose(0, 2, 1),
                ],
                axis=2,
            ),
            up_weight[None],
            down_weight.T[None],
        ]
    )
    whole = gather(shard)
    qkv_full, out_full = [], []
    for layer in range(2):
        blocks = whole[layer].reshape(model, ranks_t, 4, width)
        qkv_full.append([blocks[:, :, j].reshape(model, model) for j in range(3)])
        out_full.append(blocks[:, :, 3].reshape(model, model))
    up_full = whole[2]
    down_full = whole[3]
    attn_bias_full = lax.all_gather(attn_bias, "tp", axis=2, tiled=True)

    pairs = clips * places
    share = -(-pairs // ranks_c)

    def home_to_spatial(values):
        return lax.all_to_all(values, "tp", split_axis=1, concat_axis=2, tiled=True)

    def spatial_to_home(values):
        return lax.all_to_all(values, "tp", split_axis=2, concat_axis=1, tiled=True)

    def home_to_temporal(values):
        rows = values.transpose(1, 0, 2, 3).reshape(frames, pairs, model)
        rows = jnp.pad(rows, ((0, 0), (0, share * ranks_c - pairs), (0, 0)))
        return lax.all_to_all(rows, "ctx", split_axis=1, concat_axis=0, tiled=True)

    def temporal_to_home(values):
        rows = lax.all_to_all(values, "ctx", split_axis=0, concat_axis=1, tiled=True)[:, :pairs]
        return rows.reshape(frames, clips, places, model).transpose(1, 0, 2, 3)

    def heads_apart(values, temporal):
        apart = values.reshape(values.shape[:2] + (heads, HEAD))
        return apart.transpose(2, 1, 0, 3) if temporal else apart.transpose(2, 0, 1, 3)

    def heads_joined(values, temporal):
        joined = values.transpose(2, 1, 0, 3) if temporal else values.transpose(1, 2, 0, 3)
        return joined.reshape(joined.shape[:2] + (model,))

    def attn_forward(stream, index, temporal):
        normed = layer_norm(stream, norm_gain[index], norm_bias[index]).astype(BF)
        biases = (attn_bias_full[index, 0], 0.0, attn_bias_full[index, 1])
        triple = [
            heads_apart((dot("abd,dc->abc", normed, qkv_full[index][j]) + biases[j]).astype(BF), temporal)
            for j in range(3)
        ]
        mixed, log_total = attend(*triple)
        mixed = heads_joined(mixed, temporal)
        stream_next = stream + (dot("abc,dc->abd", mixed, out_full[index]) + out_bias[index])
        return stream_next, (normed, triple, log_total, mixed)

    def attn_backward(stream, index, kept, grad_stream, temporal):
        normed, triple, log_total, mixed = kept
        grad_branch = grad_stream.astype(BF)
        grad_bias_out = jnp.sum(grad_branch.astype(F32), axis=(0, 1))
        grad_weight_out = dot("abc,abd->dc", mixed, grad_branch)
        grad_mixed = dot("abd,dc->abc", grad_branch, out_full[index]).astype(BF)
        grad_triple = attend_back(*triple, log_total, heads_apart(grad_mixed, temporal))
        grad_triple = [heads_joined(grad_triple[j], temporal) for j in range(3)]
        grad_weight_attn = [dot("abd,abc->dc", normed, g) for g in grad_triple]
        sums = [jnp.sum(g.astype(F32), axis=(0, 1)) for g in grad_triple]
        grad_normed = sum(
            dot("abc,dc->abd", grad_triple[j], qkv_full[index][j]) for j in range(3)
        )
        unused, pull = jax.vjp(layer_norm, stream, norm_gain[index], norm_bias[index])
        grad_input, grad_gain, grad_shift = pull(grad_normed)
        return grad_stream + grad_input, (
            grad_gain,
            grad_shift,
            grad_weight_attn,
            jnp.stack([sums[0], sums[2]]),
            grad_weight_out,
            grad_bias_out,
        )

    first = home_to_spatial(inputs)
    spatial_shape = first.shape
    first = first.reshape((-1,) + first.shape[2:]).astype(F32)
    second, kept_spatial = attn_forward(first, 0, False)
    second = home_to_temporal(
        spatial_to_home(second.astype(BF).reshape(spatial_shape))
    ).astype(F32)
    third, kept_temporal = attn_forward(second, 1, True)
    normed = layer_norm(third, norm_gain[2], norm_bias[2]).astype(BF)
    units = dot("abd,dc->abc", normed, up_full) + up_bias
    active = gelu_exact(units).astype(BF)
    result = third + (dot("abc,dc->abd", active, down_full) + down_bias)
    outputs = temporal_to_home(result.astype(BF))

    grad_out = home_to_temporal(cotangent)
    grad_bias_down = jnp.sum(grad_out.astype(F32), axis=(0, 1))
    grad_weight_down = dot("abc,abd->dc", active, grad_out)
    grad_active = dot("abd,dc->abc", grad_out, down_full)
    unused, pull_gelu = jax.vjp(gelu_exact, units)
    grad_units = pull_gelu(grad_active)[0].astype(BF)
    grad_bias_up = jnp.sum(grad_units.astype(F32), axis=(0, 1))
    grad_weight_up = dot("abd,abc->dc", normed, grad_units)
    grad_normed = dot("abc,dc->abd", grad_units, up_full)
    unused, pull = jax.vjp(layer_norm, third, norm_gain[2], norm_bias[2])
    grad_third, gain_mlp, shift_mlp = pull(grad_normed)
    grad_third = grad_third + grad_out.astype(F32)

    grad_second, temporal_terms = attn_backward(second, 1, kept_temporal, grad_third, True)
    grad_second = home_to_spatial(temporal_to_home(grad_second.astype(BF)))
    grad_second = grad_second.reshape(first.shape).astype(F32)
    grad_first, spatial_terms = attn_backward(first, 0, kept_spatial, grad_second, False)
    input_grad = spatial_to_home(grad_first.astype(BF).reshape(spatial_shape))

    def joined(terms):
        parts = [g.astype(BF).reshape(model, ranks_t, width) for g in terms[2] + [terms[4]]]
        return jnp.stack(parts, axis=2).reshape(model, -1)

    grads = jnp.stack(
        [
            grad_weight_up.astype(BF),
            grad_weight_down.astype(BF),
            joined(temporal_terms),
            joined(spatial_terms),
        ]
    )
    parts = [
        jnp.stack([spatial_terms[0], temporal_terms[0], gain_mlp]),
        jnp.stack([spatial_terms[1], temporal_terms[1], shift_mlp]),
        jnp.stack([spatial_terms[3], temporal_terms[3]]),
        jnp.stack([spatial_terms[5], temporal_terms[5]]),
        grad_bias_up,
        grad_bias_down,
    ]
    lines = [p.reshape(-1, model) for p in parts]
    used = sum(line.shape[0] for line in lines)
    vectors = jnp.pad(jnp.concatenate(lines), ((0, -used % 8), (0, 0)))
    own, vectors = scatter(grads, vectors)
    sums, start = [], 0
    for part, line in zip(parts, lines):
        sums.append(vectors[start : start + line.shape[0]].reshape(part.shape))
        start += line.shape[0]
    attn = own[jnp.array([3, 2])].reshape(2, own.shape[1], 4, width)
    return (
        outputs,
        input_grad,
        sums[0],
        sums[1],
        attn[:, :, :3].transpose(0, 2, 1, 3),
        lax.dynamic_slice_in_dim(sums[2], tp_rank * width, width, 2),
        attn[:, :, 3].transpose(0, 2, 1),
        sums[3],
        own[0],
        sums[4],
        own[1].T,
        sums[5],
    )


def solution(mesh):
    return jax.shard_map(
        local,
        mesh=mesh,
        in_specs=(
            P("fsdp", "ctx", "tp", None),
            P("fsdp", "ctx", "tp", None),
            P(),
            P(),
            P(None, None, "fsdp", "tp"),
            P(None, None, "tp"),
            P(None, "tp", "fsdp"),
            P(),
            P("fsdp", "tp"),
            P(),
            P("tp", "fsdp"),
            P(),
        ),
        out_specs=(
            P("fsdp", "ctx", "tp", None),
            P("fsdp", "ctx", "tp", None),
            P(),
            P(),
            P(None, None, ("fsdp", "ctx"), "tp"),
            P(None, None, "tp"),
            P(None, "tp", ("fsdp", "ctx")),
            P(),
            P(("fsdp", "ctx"), "tp"),
            P(),
            P("tp", ("fsdp", "ctx")),
            P(),
        ),
        check_vma=False,
    )
```

```python
import jax
import jax.numpy as jnp
from jax import lax
from jax.experimental import pallas as pl
from jax.experimental.pallas import tpu as pltpu
from jax.sharding import PartitionSpec as P

HEAD = 64
EPSILON = 1e-06
BF = jnp.bfloat16
F32 = jnp.float32
MESH = pl.DeviceIdType.MESH
PIECES = 4
ALL = ("fsdp", "ctx", "tp")


def places_of(x, y, k, z):
    return {
        "x": (1 - x, y * 2 + k, z),
        "y": (x, (1 - y) * 2 + k, z),
        "core": (x, y * 2 + 1 - k, z),
        "up": (x, y * 2 + k, z + 1),
        "down": (x, y * 2 + k, z - 1),
        "z1": (x, y * 2 + k, (z // 2) * 2 + 1 - z % 2),
        "z2": (x, y * 2 + k, (z + 2) % 4),
    }


def meet(places, sides, z, last):
    barrier = pltpu.get_barrier_semaphore()
    for side in sides:
        pl.semaphore_signal(barrier, inc=1, device_id=places[side], device_id_type=MESH)

    @pl.when(z < last)
    def _():
        pl.semaphore_signal(barrier, inc=1, device_id=places["up"], device_id_type=MESH)

    @pl.when(z > 0)
    def _():
        pl.semaphore_signal(barrier, inc=1, device_id=places["down"], device_id_type=MESH)

    inner = (z > 0).astype(jnp.int32) + (z < last).astype(jnp.int32)
    pl.semaphore_wait(barrier, len(sides) + inner)


def maybe(when, action):
    if when is None:
        action()
    else:
        pl.when(when)(action)


def gather_kernel(shard, bias, whole, bias_all, send_sem, recv_sem, local_sem, bias_send, bias_recv):
    x, c, z = lax.axis_index("fsdp"), lax.axis_index("ctx"), lax.axis_index("tp")
    y, k = c // 2, c % 2
    rows = shard.shape[1] // 4
    width = shard.shape[2]
    last = 3
    places = places_of(x, y, k, z)

    def spot(ref, piece, f, cc, t):
        row = pl.multiple_of((f * 4 + cc) * rows, 16)
        return ref.at[piece, pl.ds(row, rows), pl.ds(pl.multiple_of(t * width, 128), width)]

    line = [(x, c, (z + i) % 4) for i in range(1, 4)]
    barrier = pltpu.get_barrier_semaphore()
    for place in [places[side] for side in ("x", "y", "core")] + line:
        pl.semaphore_signal(barrier, inc=1, device_id=place, device_id_type=MESH)
    pl.semaphore_wait(barrier, 6)
    small = []
    for i, place in enumerate(line):
        copy = pltpu.make_async_remote_copy(
            src_ref=bias,
            dst_ref=bias_all.at[z],
            send_sem=bias_send.at[i],
            recv_sem=bias_recv.at[i],
            device_id=place,
            device_id_type=MESH,
        )
        copy.start()
        small.append(copy)
    bias_all[z] = bias[...]
    local = []
    for piece in range(PIECES):
        row = pl.multiple_of(x * rows * 4, 16)
        copy = pltpu.make_async_copy(
            shard.at[piece],
            whole.at[piece, pl.ds(row, rows * 4), pl.ds(pl.multiple_of(z * width, 128), width)],
            local_sem.at[piece],
        )
        copy.start()
        local.append(copy)

    sent = []

    def send(side, unit, mine=False, pieces=range(PIECES), when=None):
        f, cc, t = unit
        copies = []
        for piece in pieces:
            target = spot(whole, piece, f, cc, t)
            source = shard.at[piece, pl.ds(pl.multiple_of(cc * rows, 16), rows)] if mine else target
            number = sum(len(c) for w, c in sent) + len(copies)
            copies.append(
                pltpu.make_async_remote_copy(
                    src_ref=source,
                    dst_ref=target,
                    send_sem=send_sem.at[number],
                    recv_sem=recv_sem.at[(f * 4 + cc) * 4 + t, piece],
                    device_id=places[side],
                    device_id_type=MESH,
                )
            )
        sent.append((when, copies))

        def start():
            for copy in copies:
                copy.start()

        maybe(when, start)

    def arrived(unit, when=None):
        f, cc, t = unit

        def wait():
            for piece in range(PIECES):
                ref = spot(whole, piece, f, cc, t)
                pltpu.make_async_copy(ref, ref, recv_sem.at[(f * 4 + cc) * 4 + t, piece]).wait()

        maybe(when, wait)

    other_y = (1 - y) * 2 + k
    first, second = (0, 1), (2, 3)
    me = (x, c, z)
    send("up", me, True, when=z < last)
    send("down", me, True, when=z > 0)
    send("x", me, True)
    send("x", (x, other_y, z), True)

    def at(sign, d):
        t = z + sign * d
        return t, ((t >= 0) if sign < 0 else (t <= last))

    def from_line(sign, d):
        t, have = at(sign, d)
        unit = (x, c, t)
        arrived(unit, have)
        if d < last:
            if sign < 0:
                send("up", unit, when=have & (z < last))
            else:
                send("down", unit, when=have & (z > 0))
        for side in ("x", "y", "core"):
            send(side, unit, when=have)

    def from_plane(sign, d):
        t, have = at(sign, d)
        arrived((1 - x, c, t), have)
        send("y", (1 - x, c, t), pieces=second, when=have)
        send("core", (1 - x, c, t), when=have)
        arrived((x, other_y, t), have)
        send("x", (x, other_y, t), pieces=first, when=have)
        send("core", (x, other_y, t), when=have)

    def from_diagonal(sign, d):
        t, have = at(sign, d)
        arrived((1 - x, other_y, t), have)
        send("core", (1 - x, other_y, t), when=have)

    def both(action, d):
        action(-1, d)
        action(1, d)

    both(from_line, 1)
    arrived((1 - x, c, z))
    send("core", (1 - x, c, z))
    both(from_line, 2)
    arrived((1 - x, other_y, z))
    send("core", (1 - x, other_y, z))
    both(from_plane, 1)
    both(from_line, 3)
    both(from_plane, 2)
    both(from_diagonal, 1)
    both(from_plane, 3)
    both(from_diagonal, 2)
    both(from_diagonal, 3)
    for sign, d in ((-1, 1), (1, 1), (-1, 2), (1, 2), (-1, 3), (1, 3)):
        t, have = at(sign, d)
        for f in (x, 1 - x):
            for yy in (y, 1 - y):
                arrived((f, yy * 2 + 1 - k, t), have)
    for yy in (y, 1 - y):
        arrived((1 - x, yy * 2 + 1 - k, z))
    for when, copies in sent:

        def wait():
            for copy in copies:
                copy.wait_send()

        maybe(when, wait)
    for copy in local + small:
        copy.wait()


def gather(shard, bias):
    ranks = (lax.axis_size("fsdp"), lax.axis_size("ctx"), lax.axis_size("tp"))
    rows, width = shard.shape[1:]
    if ranks != (2, 4, 4):
        part = rows // ranks[1]
        mine = lax.dynamic_slice_in_dim(shard, lax.axis_index("ctx") * part, part, 1)
        tall = lax.all_gather(mine, ("fsdp", "ctx"), axis=1, tiled=True)
        return lax.all_gather(tall, "tp", axis=2, tiled=True), lax.all_gather(bias, "tp")
    return pl.pallas_call(
        gather_kernel,
        out_shape=(
            jax.ShapeDtypeStruct((PIECES, rows * 2, width * 4), BF),
            jax.ShapeDtypeStruct((4,) + bias.shape, F32),
        ),
        in_specs=[pl.BlockSpec(memory_space=pltpu.VMEM)] * 2,
        out_specs=[pl.BlockSpec(memory_space=pl.ANY), pl.BlockSpec(memory_space=pltpu.VMEM)],
        scratch_shapes=[
            pltpu.SemaphoreType.DMA((260,)),
            pltpu.SemaphoreType.DMA((32, PIECES)),
            pltpu.SemaphoreType.DMA((PIECES,)),
            pltpu.SemaphoreType.DMA((3,)),
            pltpu.SemaphoreType.DMA((3,)),
        ],
        compiler_params=pltpu.CompilerParams(collective_id=0, has_side_effects=True),
        name="gather_weights",
    )(shard, bias)


STEPS = 16


def scatter_kernel(
    g0, g1, g2, g3, v_ref, out_ref, vout_ref, own, r1, r2, r3x, r3y, rup, rdn, vr, va,
    own_sem, s1, q1, s2, q2, s3a, s3b, q3x, q3y, sz, qup, qdn, vs, vq,
):
    x, c, z = lax.axis_index("fsdp"), lax.axis_index("ctx"), lax.axis_index("tp")
    y, k = c // 2, c % 2
    rows, width = out_ref.shape[1:]
    last = 3
    places = places_of(x, y, k, z)
    meet(places, ("x", "y", "core", "z2"), z, last)

    def tp_of(s):
        return (3 * s) % 4

    pieces = (g0, g1, g2, g3)

    def spot(f, yy, kk, s, piece=0):
        row = pl.multiple_of((f * 4 + yy * 2 + kk) * rows, 16)
        column = pl.multiple_of(tp_of(s) * width, 128)
        return pieces[piece].at[0, pl.ds(row, rows), pl.ds(column, width)]

    def remote(src, dst, send, recv, side):
        return pltpu.make_async_remote_copy(
            src_ref=src, dst_ref=dst, send_sem=send, recv_sem=recv,
            device_id=places[side], device_id_type=MESH,
        )

    def core_copy(s, f, yy, piece=0):
        return remote(
            spot(f, yy, 1 - k, s, piece), r1.at[s, f, yy], s1.at[s, f, yy], q1.at[s, f, yy], "core"
        )

    def own_copy(s, f, yy, piece=0):
        return pltpu.make_async_copy(spot(f, yy, k, s, piece), own.at[s, f, yy], own_sem.at[s, f, yy])

    def diag_copy(s, side):
        return remote(r1.at[s, 1 - x, 1 - y], r2.at[s], s2.at[s], q2.at[s], side)

    def x_copy(s):
        return remote(r1.at[s, 1 - x, y], r3x.at[s], s3a.at[s], q3x.at[s], "x")

    def y_copy(s):
        return remote(r1.at[s, x, 1 - y], r3y.at[s], s3b.at[s], q3y.at[s], "y")

    def up_copy(s):
        return remote(r1.at[s, x, y], rup.at[s], sz.at[s], qup.at[s], "up")

    def down_copy(s):
        return remote(r1.at[s, x, y], rdn.at[s], sz.at[s], qdn.at[s], "down")

    sides = ("core", "x", "y", "z1", "z2")

    def v_copy(j):
        return remote(va.at[j], vr.at[j], vs.at[j], vq.at[j], sides[j])

    quads = [(f, yy) for f in range(2) for yy in range(2)]

    for piece in range(PIECES):

        def start(s, carry):
            for f, yy in quads:
                core_copy(s, f, yy, piece).start()
                own_copy(s, f, yy, piece).start()
            return carry

        lax.fori_loop(piece * 4, piece * 4 + 4, start, 0)
    va[0] = v_ref[...]
    v_copy(0).start()

    def chip_sum(s):
        for f, yy in quads:
            core_copy(s, f, yy).wait_recv()
            own_copy(s, f, yy).wait()
            r1[s, f, yy] = r1[s, f, yy] + own[s, f, yy]

        @pl.when(s % 2 == 0)
        def _():
            diag_copy(s, "x").start()
            x_copy(s).start()

        @pl.when(s % 2 == 1)
        def _():
            diag_copy(s, "y").start()
            y_copy(s).start()

    def turn(s):
        diag_copy(s, "x").wait_recv()

        @pl.when(s % 2 == 0)
        def _():
            r1[s, x, 1 - y] = r1[s, x, 1 - y] + r2[s]
            y_copy(s).start()

        @pl.when(s % 2 == 1)
        def _():
            r1[s, 1 - x, y] = r1[s, 1 - x, y] + r2[s]
            x_copy(s).start()

    def plane_sum(s):
        x_copy(s).wait_recv()
        y_copy(s).wait_recv()
        total = r1[s, x, y].astype(F32) + r3x[s].astype(F32) + r3y[s].astype(F32)
        r1[s, x, y] = total.astype(BF)

    def line(s, hop):
        t = tp_of(s)

        @pl.when((z < t) & (z == hop))
        def _():
            if hop > 0:
                up_copy(s).wait_recv()
                r1[s, x, y] = r1[s, x, y] + rup[s]
            up_copy(s).start()

        @pl.when((z > t) & (last - z == hop))
        def _():
            if hop > 0:
                down_copy(s).wait_recv()
                r1[s, x, y] = r1[s, x, y] + rdn[s]
            down_copy(s).start()

        far = z + (last - 2 * z) * ((last - 2 * z) > 0).astype(jnp.int32)

        @pl.when((z == t) & (far == hop))
        def _():
            out_ref[s // 4] = r1[s, x, y].astype(F32)

            @pl.when(z > 0)
            def _():
                up_copy(s).wait_recv()
                out_ref[s // 4] = out_ref[s // 4] + rup[s].astype(F32)

            @pl.when(z < last)
            def _():
                down_copy(s).wait_recv()
                out_ref[s // 4] = out_ref[s // 4] + rdn[s].astype(F32)

    def guard(action, s, *rest):
        @pl.when((s >= 0) & (s < STEPS))
        def _():
            action(s, *rest)

    def step(s, carry):
        guard(chip_sum, s)
        guard(turn, s - 1)
        guard(plane_sum, s - 3)
        for hop in range(4):
            guard(line, s - 3 - hop, hop)
        for j in range(5):

            @pl.when(s == 2 + j)
            def _():
                v_copy(j).wait()
                if j < 4:
                    va[j + 1] = va[j] + vr[j]
                    v_copy(j + 1).start()
                else:
                    vout_ref[...] = va[j] + vr[j]

        return carry

    lax.fori_loop(0, STEPS + 6, step, 0)

    def finish(s, carry):
        for f, yy in quads:
            core_copy(s, f, yy).wait_send()
        diag_copy(s, "x").wait_send()
        x_copy(s).wait_send()
        y_copy(s).wait_send()

        @pl.when(z != tp_of(s))
        def _():
            up_copy(s).wait_send()

        return carry

    lax.fori_loop(0, STEPS, finish, 0)


def scatter(grads, vectors):
    ranks = (lax.axis_size("fsdp"), lax.axis_size("ctx"), lax.axis_size("tp"))
    rows = grads[0].shape[1] // (ranks[0] * ranks[1])
    width = grads[0].shape[2] // ranks[2]
    if ranks != (2, 4, 4):
        tall = lax.psum_scatter(jnp.concatenate(grads), ("fsdp", "ctx"), scatter_dimension=1, tiled=True)
        own = lax.psum_scatter(tall, "tp", scatter_dimension=2, tiled=True)
        return own.astype(F32), lax.psum(vectors, ALL)
    sub = (rows, width)
    dma = pltpu.SemaphoreType.DMA
    return pl.pallas_call(
        scatter_kernel,
        out_shape=(
            jax.ShapeDtypeStruct((PIECES,) + sub, F32),
            jax.ShapeDtypeStruct(vectors.shape, F32),
        ),
        in_specs=[pl.BlockSpec(memory_space=pl.ANY)] * 4 + [pl.BlockSpec(memory_space=pltpu.VMEM)],
        out_specs=[pl.BlockSpec(memory_space=pltpu.VMEM)] * 2,
        scratch_shapes=[pltpu.VMEM((STEPS, 2, 2) + sub, BF)] * 2
        + [pltpu.VMEM((STEPS,) + sub, BF)] * 5
        + [pltpu.VMEM((5,) + vectors.shape, F32)] * 2
        + [dma((STEPS, 2, 2))] * 3
        + [dma((STEPS,))] * 9
        + [dma((5,))] * 2,
        compiler_params=pltpu.CompilerParams(
            collective_id=1, has_side_effects=True, vmem_limit_bytes=48 * 2**20
        ),
        name="scatter_grads",
    )(*grads, vectors)


def nn(a, b):
    return lax.dot_general(a, b, (((1,), (0,)), ((), ())), preferred_element_type=F32)


def nt(a, b):
    return lax.dot_general(a, b, (((1,), (1,)), ((), ())), preferred_element_type=F32)


def tn(a, b):
    return lax.dot_general(a, b, (((0,), (0,)), ((), ())), preferred_element_type=F32)


def normalise(rows):
    centre = rows - jnp.mean(rows, axis=-1, keepdims=True)
    scale = lax.rsqrt(jnp.mean(centre * centre, axis=-1, keepdims=True) + EPSILON)
    return centre * scale, scale


def norm_back(rows, gain, grad):
    unit, scale = normalise(rows)
    inner = grad * gain
    mean = jnp.mean(inner, axis=-1, keepdims=True)
    along = jnp.mean(inner * unit, axis=-1, keepdims=True)
    return scale * (inner - mean - unit * along), jnp.sum(grad * unit, axis=0, keepdims=True), jnp.sum(
        grad, axis=0, keepdims=True
    )


def lanes_in(low, high):
    lane = lax.broadcasted_iota(jnp.int32, (1, 256), 1)
    return jnp.where((lane >= low) & (lane < high), 1.0, 0.0)


def stack_heads(values):
    return jnp.concatenate(
        [values * lanes_in(i * HEAD, i * HEAD + HEAD).astype(BF) for i in range(3)], axis=0
    )


def pick_heads(stacked):
    rows = stacked.shape[0] // 3
    return sum(
        stacked[i * rows : (i + 1) * rows] * lanes_in(i * HEAD, i * HEAD + HEAD) for i in range(3)
    )


def shifted(values):
    return pltpu.roll(values, 64, axis=1)


def unshifted(values):
    return pltpu.roll(values, 192, axis=1)


def block(w_ref, t, start, size):
    return w_ref[:, pl.ds(pl.multiple_of(t * (w_ref.shape[1] // 4) + start, 128), size)]


class Attention:
    def __init__(self, groups, rows, penalty, w, bias, q, k, v, o, p):
        self.groups, self.rows, self.penalty = groups, rows, penalty
        self.w, self.bias, self.q, self.k, self.v, self.o, self.p = w, bias, q, k, v, o, p

    def spans(self):
        return [(g, pl.ds(g * self.rows, self.rows)) for g in range(self.groups)]

    def forward(self, normed, total):
        used = lanes_in(0, 192)

        def body(t, carry):
            mixed = nn(normed[...], block(self.w, t, 0, 640))
            self.q[t] = ((mixed[:, :256] + self.bias[t, 0:1]) * used).astype(BF)
            self.k[t] = (unshifted(mixed[:, 128:384]) * used).astype(BF)
            self.v[t] = ((mixed[:, 384:] + self.bias[t, 1:2]) * used).astype(BF)
            for g, span in self.spans():
                scores = nt(stack_heads(self.q[t, span]), self.k[t, span]) * 0.125 + self.penalty()
                weights = jnp.exp(scores - jnp.max(scores, axis=-1, keepdims=True))
                weights = weights * (1.0 / jnp.sum(weights, axis=-1, keepdims=True))
                weights = weights.astype(BF)
                self.p[t, g] = weights
                out = pick_heads(nn(weights, self.v[t, span]))
                self.o[t, span] = shifted(out).astype(BF)
            total[...] += nt(self.o[t], block(self.w, t, 512, 256))
            return carry

        lax.fori_loop(0, 4, body, 0)

    def backward(self, normed_t, branch, branch_t, dk, dv, grad_normed, grad_w, grad_bias):
        used = lanes_in(0, 192)

        def body(t, carry):
            grad_o = (unshifted(nn(branch[...], block(self.w, t, 512, 256))) * used).astype(BF)
            dq = []
            for g, span in self.spans():
                stacked = stack_heads(grad_o[g * self.rows : (g + 1) * self.rows])
                weights = self.p[t, g]
                probs = weights.astype(F32)
                grad_p = nt(stacked, self.v[t, span])
                inner = jnp.sum(probs * grad_p, axis=-1, keepdims=True)
                grad_s = (probs * (grad_p - inner)).astype(BF)
                dq.append((pick_heads(nn(grad_s, self.k[t, span])) * 0.125).astype(BF))
                dk[span] = shifted(tn(grad_s, stack_heads(self.q[t, span])) * 0.125).astype(BF)
                dv[span] = tn(weights, stacked).astype(BF)
            dq = jnp.concatenate(dq, axis=0)
            grad_normed[...] += (
                nt(dq, block(self.w, t, 0, 256))
                + nt(dk[...], block(self.w, t, 128, 256))
                + nt(dv[...], block(self.w, t, 384, 256))
            )
            for start, low, high in (
                (0, nn(normed_t[...], dq), nn(normed_t[...], dk[...])),
                (384, nn(normed_t[...], dv[...]), nn(branch_t[...], self.o[t])),
            ):
                columns = pl.multiple_of(t * (self.w.shape[1] // 4) + start, 128)
                grad_w[:, pl.ds(columns, 128)] = low[:, :128].astype(BF)
                grad_w[:, pl.ds(columns + 128, 128)] = (low[:, 128:] + high[:, :128]).astype(BF)
                grad_w[:, pl.ds(columns + 256, 128)] = high[:, 128:].astype(BF)
            grad_bias[t, 0:1] = jnp.sum(dq.astype(F32), axis=0, keepdims=True)
            grad_bias[t, 1:2] = jnp.sum(dv[...].astype(F32), axis=0, keepdims=True)
            return carry

        lax.fori_loop(0, 4, body, 0)


SP = 208


def spatial_penalty(places):
    def penalty():
        lane = lax.broadcasted_iota(jnp.int32, (1, SP), 1)
        return jnp.where(lane < places, 0.0, -1e30)
    return penalty


def spatial_forward_kernel(x_ref, w_ref, bias_ref, norm_ref, ob_ref, h_out, q, k, v, o, p, total, normed):
    clips, places, model = x_ref.shape
    for g in range(clips):
        total[pl.ds(g * SP, places)] = x_ref[g].astype(F32)
        total[pl.ds(g * SP + places, SP - places)] = jnp.zeros((SP - places, model), F32)
        span = pl.ds(g * SP, SP)
        unit, _ = normalise(total[span])
        normed[span] = (unit * norm_ref[0:1] + norm_ref[1:2]).astype(BF)
        total[span] += ob_ref[...]
    att = Attention(clips, SP, spatial_penalty(places), w_ref.at[0], bias_ref, q, k, v, o, p)
    att.forward(normed, total)
    for g in range(clips):
        h_out[g] = total[pl.ds(g * SP, places)].astype(BF)


def spatial_back_kernel(x_ref, g_ref, w_ref, norm_ref, q, k, v, o, p,
                        gx_out, gw, gbias, gvec, total, normed_t, branch, branch_t, dk, dv, gn, rows_in):
    clips, places, model = x_ref.shape
    for g in range(clips):
        for ref, source in ((rows_in, x_ref), (total, g_ref)):
            ref[pl.ds(g * SP, places)] = source[g].astype(F32)
            ref[pl.ds(g * SP + places, SP - places)] = jnp.zeros((SP - places, model), F32)
    attention_back(Attention(clips, SP, None, w_ref.at[0], None, q, k, v, o, p),
                   rows_in, total, norm_ref, normed_t, branch, branch_t, dk, dv, gn, gw.at[0], gbias, gvec)
    for g in range(clips):
        gx_out[g] = total[pl.ds(g * SP, places)].astype(BF)


def attention_back(att, rows_in, total, norm_ref, normed_t, branch, branch_t, dk, dv, gn, gw, gbias, gvec):
    rounded = total[...].astype(BF)
    branch[...] = rounded
    branch_t[...] = total[...].T.astype(BF)
    gvec[2:3] = jnp.sum(rounded.astype(F32), axis=0, keepdims=True)
    unit, _ = normalise(rows_in[...])
    normed_t[...] = (unit * norm_ref[0:1] + norm_ref[1:2]).T.astype(BF)
    gn[...] = jnp.zeros_like(gn)
    att.backward(normed_t, branch, branch_t, dk, dv, gn, gw, gbias)
    grad, gain, shift = norm_back(rows_in[...], norm_ref[0:1], gn[...])
    total[...] += grad
    gvec[0:1] = gain
    gvec[1:2] = shift


def by_pair(source, target, mix):
    frames, pairs, model = source.shape
    for f in range(frames):
        values = source[f].astype(F32)
        for i in range(model // 128):
            mix[i, pl.ds(f, pairs, stride=frames)] = values[:, i * 128 : i * 128 + 128]
    for i in range(model // 128):
        target[:, i * 128 : i * 128 + 128] = mix[i]


def by_frame(source, target, mix):
    frames, pairs, model = target.shape
    for i in range(model // 128):
        mix[i] = source[:, i * 128 : i * 128 + 128]
    for f in range(frames):
        for i in range(model // 128):
            target[f, :, i * 128 : i * 128 + 128] = mix[i, pl.ds(f, pairs, stride=frames)].astype(BF)


TG = 5


def temporal_kernel(h_ref, g_ref, w_ref, u_ref, d_ref, bias_ref, norm_ref, norm2_ref, ob_ref, ub_ref, db_ref, pen_ref,
                    y_out, g_out, gw, gu, gd, gbias, gvec, gvec2, gub,
                    q, k, v, o, p, rows_in, total, third, grad, normed, normed_t, branch, branch_t, dk, dv, gn, mix):
    frames, pairs, model = h_ref.shape
    rows = frames * pairs
    by_pair(h_ref, rows_in, mix)
    by_pair(g_ref, grad, mix)
    unit, _ = normalise(rows_in[...])
    normed[...] = (unit * norm_ref[0:1] + norm_ref[1:2]).astype(BF)
    third[...] = rows_in[...] + ob_ref[...]
    group = TG * frames
    att = Attention(pairs // TG, group, lambda: pen_ref[...], w_ref.at[0], bias_ref, q, k, v, o, p)
    att.forward(normed, third)
    unit, _ = normalise(third[...])
    n2 = unit * norm2_ref[0:1] + norm2_ref[1:2]
    normed[...] = n2.astype(BF)
    normed_t[...] = n2.T.astype(BF)
    branch[...] = grad[...].astype(BF)
    branch_t[...] = grad[...].T.astype(BF)
    gvec2[2:3] = jnp.sum(grad[...], axis=0, keepdims=True)
    total[...] = third[...] + db_ref[...]
    gn[...] = jnp.zeros_like(gn)
    size = 384
    def mlp(j, carry):
        columns = pl.ds(pl.multiple_of(j * size, 128), size)
        up = u_ref[0, :, columns]
        down = d_ref[0, :, columns]
        hidden = nn(normed[...], up) + ub_ref[j]
        half = 0.5 + 0.5 * lax.erf(hidden * (2.0 ** -0.5))
        active = (hidden * half).astype(BF)
        slope = half + hidden * (jnp.exp(-0.5 * hidden * hidden) * ((2.0 * jnp.pi) ** -0.5))
        grad_hidden = nn(branch[...], down) * slope
        rounded = grad_hidden.astype(BF)
        gub[j] = jnp.sum(rounded.astype(F32), axis=0, keepdims=True)
        total[...] += nt(active, down)
        gn[...] += nt(rounded, up)
        gd[0, :, columns] = nn(branch_t[...], active).astype(BF)
        gu[0, :, columns] = nn(normed_t[...], rounded).astype(BF)
        return carry
    lax.fori_loop(0, u_ref.shape[2] // size, mlp, 0)
    by_frame(total, y_out, mix)
    back, gain, shift = norm_back(third[...], norm2_ref[0:1], gn[...])
    grad[...] += back
    gvec2[0:1] = gain
    gvec2[1:2] = shift
    attention_back(att, rows_in, grad, norm_ref, normed_t, branch, branch_t, dk, dv, gn, gw.at[0], gbias, gvec)
    by_frame(grad, g_out, mix)


def piece_spec(piece, whole):
    return pl.BlockSpec((1,) + whole.shape[1:], lambda i: (piece, 0, 0))


def full_spec(value):
    return pl.BlockSpec(value.shape, lambda i: (0,) * len(value.shape))


def run(kernel, args, specs, outs, scratch, name):
    return pl.pallas_call(
        kernel, grid=(1,),
        out_shape=outs, in_specs=specs, out_specs=[full_spec(out) for out in outs], scratch_shapes=scratch,
        compiler_params=pltpu.CompilerParams(vmem_limit_bytes=63 * 2**20),
        name=name,
    )(*args)


def shape(*size, dtype=BF):
    return jax.ShapeDtypeStruct(size, dtype)


def spatial_forward(x, whole, bias, norm, out_bias):
    clips, places, model = x.shape
    rows = clips * SP
    args = (x, whole, bias, norm, out_bias)
    specs = [full_spec(a) for a in args]
    specs[1] = piece_spec(0, whole)
    outs = [shape(clips, places, model)] + [shape(4, rows, 256)] * 4 + [shape(4, clips, 3 * SP, SP)]
    return run(spatial_forward_kernel, args, specs, outs,
               [pltpu.VMEM((rows, model), F32), pltpu.VMEM((rows, model), BF)], "spatial_forward")


def spatial_back(x, g, whole, norm, kept):
    clips, places, model = x.shape
    rows = clips * SP
    args = (x, g, whole, norm) + tuple(kept)
    specs = [full_spec(a) for a in args]
    specs[2] = piece_spec(0, whole)
    outs = [shape(clips, places, model), shape(1, *whole.shape[1:]), shape(4, 2, 256, dtype=F32), shape(3, model, dtype=F32)]
    scratch = [pltpu.VMEM((rows, model), F32), pltpu.VMEM((model, rows), BF), pltpu.VMEM((rows, model), BF),
               pltpu.VMEM((model, rows), BF), pltpu.VMEM((rows, 256), BF), pltpu.VMEM((rows, 256), BF),
               pltpu.VMEM((rows, model), F32), pltpu.VMEM((rows, model), F32)]
    return run(spatial_back_kernel, args, specs, outs, scratch, "spatial_back")


def temporal(h, g, whole, bias, norm, norm2, out_bias, up_bias, down_bias):
    frames, pairs, model = h.shape
    rows = frames * pairs
    group = TG * frames
    row = jnp.arange(3 * group)[:, None] % group // frames
    column = jnp.arange(group)[None] // frames
    penalty = jnp.where(row == column, 0.0, -1e30).astype(F32)
    args = (h, g, whole, whole, whole, bias, norm, norm2, out_bias, up_bias.reshape(-1, 1, 384), down_bias, penalty)
    specs = [full_spec(a) for a in args]
    for i, piece in ((2, 1), (3, 2), (4, 3)):
        specs[i] = piece_spec(piece, whole)
    hidden = whole.shape[2]
    outs = [shape(frames, pairs, model), shape(frames, pairs, model), shape(1, model, hidden), shape(1, model, hidden),
            shape(1, model, hidden), shape(4, 2, 256, dtype=F32), shape(3, model, dtype=F32), shape(3, model, dtype=F32),
            shape(hidden // 384, 1, 384, dtype=F32)]
    big = pltpu.VMEM((rows, model), F32)
    low = pltpu.VMEM((rows, model), BF)
    flip = pltpu.VMEM((model, rows), BF)
    part = pltpu.VMEM((rows, 256), BF)
    scratch = [pltpu.VMEM((4, rows, 256), BF)] * 4 + [pltpu.VMEM((4, pairs // TG, 3 * group, group), BF)] + [
        big, big, big, big, low, flip, low, flip, part, part, big, pltpu.VMEM((model // 128, rows, 128), F32)]
    return run(temporal_kernel, args, specs, outs, scratch, "temporal_and_mlp")


def local(
    inputs,
    cotangent,
    norm_gain,
    norm_bias,
    attn_weight,
    attn_bias,
    out_weight,
    out_bias,
    up_weight,
    up_bias,
    down_weight,
    down_bias,
):
    ranks_c = lax.axis_size("ctx")
    tp_rank = lax.axis_index("tp")
    clips, frames, places, model = inputs.shape
    width = attn_weight.shape[3]

    shard = jnp.concatenate(
        [
            jnp.concatenate(
                [
                    attn_weight.transpose(0, 2, 1, 3).reshape(2, attn_weight.shape[2], 3 * width),
                    out_weight.transpose(0, 2, 1),
                ],
                axis=2,
            ),
            up_weight[None],
            down_weight.T[None],
        ]
    )
    bias = jnp.pad(attn_bias.reshape(4, width), ((0, 4), (0, 256 - width)))
    whole, bias = gather(shard, bias)
    bias = bias[:, :4].reshape(4, 2, 2, 256).transpose(1, 0, 2, 3)
    norm = jnp.stack([norm_gain, norm_bias], axis=1)

    pairs = clips * places
    share = -(-pairs // ranks_c)
    share += -share % TG

    def home_to_spatial(values):
        return lax.all_to_all(values, "tp", split_axis=1, concat_axis=2, tiled=True)

    def spatial_to_home(values):
        return lax.all_to_all(values, "tp", split_axis=2, concat_axis=1, tiled=True)

    def home_to_temporal(values):
        rows = values.transpose(1, 0, 2, 3).reshape(frames, pairs, model)
        rows = jnp.pad(rows, ((0, 0), (0, share * ranks_c - pairs), (0, 0)))
        return lax.all_to_all(rows, "ctx", split_axis=1, concat_axis=0, tiled=True)

    def temporal_to_home(values):
        rows = lax.all_to_all(values, "ctx", split_axis=0, concat_axis=1, tiled=True)[:, :pairs]
        return rows.reshape(frames, clips, places, model).transpose(1, 0, 2, 3)

    first = home_to_spatial(inputs)
    spatial_shape = first.shape
    first = first.reshape((-1,) + first.shape[2:])
    second, *kept = spatial_forward(first, whole, bias[0], norm[0], out_bias[0:1])
    second = home_to_temporal(spatial_to_home(second.reshape(spatial_shape)))
    grad_out = home_to_temporal(cotangent)
    result, grad_second, grad_attn1, grad_up, grad_down, bias1, vec1, vec2, grad_up_bias = temporal(
        second, grad_out, whole, bias[1], norm[1], norm[2], out_bias[1:2], up_bias, down_bias[None]
    )
    outputs = temporal_to_home(result)
    grad_second = home_to_spatial(temporal_to_home(grad_second)).reshape(first.shape)
    grad_first, grad_attn0, bias0, vec0 = spatial_back(first, grad_second, whole, norm[0], kept)
    input_grad = spatial_to_home(grad_first.reshape(spatial_shape))

    attn_bias_sums = jnp.stack([bias0, bias1])[..., :width].transpose(0, 2, 1, 3)
    lines = [vec0, vec1, vec2, grad_up_bias, attn_bias_sums]
    flat = jnp.concatenate([line.reshape(-1, model) for line in lines])
    vectors = jnp.pad(flat, ((0, -flat.shape[0] % 8), (0, 0)))
    own, vectors = scatter([grad_up, grad_down, grad_attn1, grad_attn0], vectors)
    triples = vectors[:9].reshape(3, 3, model)
    ups = up_bias.shape[0] // model
    attn_bias_sums = vectors[9 + ups : 13 + ups].reshape(2, 2, model)
    attn = jnp.stack([own[3], own[2]]).reshape(2, own.shape[1], 4, width)
    return (
        outputs,
        input_grad,
        triples[:, 0],
        triples[:, 1],
        attn[:, :, :3].transpose(0, 2, 1, 3),
        lax.dynamic_slice_in_dim(attn_bias_sums, tp_rank * width, width, 2),
        attn[:, :, 3].transpose(0, 2, 1),
        triples[:2, 2],
        own[0],
        vectors[9 : 9 + ups].reshape(-1),
        own[1].T,
        triples[2, 2],
    )


def solution(mesh):
    return jax.shard_map(
        local,
        mesh=mesh,
        in_specs=(
            P("fsdp", "ctx", "tp", None),
            P("fsdp", "ctx", "tp", None),
            P(),
            P(),
            P(None, None, "fsdp", "tp"),
            P(None, None, "tp"),
            P(None, "tp", "fsdp"),
            P(),
            P("fsdp", "tp"),
            P(),
            P("tp", "fsdp"),
            P(),
        ),
        out_specs=(
            P("fsdp", "ctx", "tp", None),
            P("fsdp", "ctx", "tp", None),
            P(),
            P(),
            P(None, None, ("fsdp", "ctx"), "tp"),
            P(None, None, "tp"),
            P(None, "tp", ("fsdp", "ctx")),
            P(),
            P(("fsdp", "ctx"), "tp"),
            P(),
            P("tp", ("fsdp", "ctx")),
            P(),
        ),
        check_vma=False,
    )
```

```python
import jax
import jax.numpy as jnp
from jax import lax
from jax.experimental import pallas as pl
from jax.experimental.pallas import tpu as pltpu
from jax.sharding import PartitionSpec as P

HEAD = 64
EPSILON = 1e-06
BF = jnp.bfloat16
F32 = jnp.float32
MESH = pl.DeviceIdType.MESH
PIECES = 4
ALL = ("fsdp", "ctx", "tp")


def places_of(x, y, k, z):
    return {
        "x": (1 - x, y * 2 + k, z),
        "y": (x, (1 - y) * 2 + k, z),
        "core": (x, y * 2 + 1 - k, z),
        "up": (x, y * 2 + k, z + 1),
        "down": (x, y * 2 + k, z - 1),
        "z1": (x, y * 2 + k, (z // 2) * 2 + 1 - z % 2),
        "z2": (x, y * 2 + k, (z + 2) % 4),
    }


def maybe(when, action):
    if when is None:
        action()
    else:
        pl.when(when)(action)


def gather_kernel(shard, bias, whole, bias_all, send_sem, recv_sem, local_sem, bias_send, bias_recv):
    x, c, z = lax.axis_index("fsdp"), lax.axis_index("ctx"), lax.axis_index("tp")
    y, k = c // 2, c % 2
    rows = shard.shape[1] // 4
    width = shard.shape[2]
    last = 3
    places = places_of(x, y, k, z)

    def spot(ref, piece, f, cc, t):
        row = pl.multiple_of((f * 4 + cc) * rows, 16)
        return ref.at[piece, pl.ds(row, rows), pl.ds(pl.multiple_of(t * width, 128), width)]

    line = [(x, c, (z + i) % 4) for i in range(1, 4)]
    barrier = pltpu.get_barrier_semaphore()
    for place in [places[side] for side in ("x", "y", "core")] + line:
        pl.semaphore_signal(barrier, inc=1, device_id=place, device_id_type=MESH)
    pl.semaphore_wait(barrier, 6)
    small = []
    for i, place in enumerate(line):
        copy = pltpu.make_async_remote_copy(
            src_ref=bias,
            dst_ref=bias_all.at[z],
            send_sem=bias_send.at[i],
            recv_sem=bias_recv.at[i],
            device_id=place,
            device_id_type=MESH,
        )
        copy.start()
        small.append(copy)
    bias_all[z] = bias[...]
    local = []
    for piece in range(PIECES):
        row = pl.multiple_of(x * rows * 4, 16)
        copy = pltpu.make_async_copy(
            shard.at[piece],
            whole.at[piece, pl.ds(row, rows * 4), pl.ds(pl.multiple_of(z * width, 128), width)],
            local_sem.at[piece],
        )
        copy.start()
        local.append(copy)

    sent = []

    def send(side, unit, mine=False, pieces=range(PIECES), when=None):
        f, cc, t = unit
        copies = []
        for piece in pieces:
            target = spot(whole, piece, f, cc, t)
            source = shard.at[piece, pl.ds(pl.multiple_of(cc * rows, 16), rows)] if mine else target
            number = sum(len(c) for w, c in sent) + len(copies)
            copies.append(
                pltpu.make_async_remote_copy(
                    src_ref=source,
                    dst_ref=target,
                    send_sem=send_sem.at[number],
                    recv_sem=recv_sem.at[(f * 4 + cc) * 4 + t, piece],
                    device_id=places[side],
                    device_id_type=MESH,
                )
            )
        sent.append((when, copies))

        def start():
            for copy in copies:
                copy.start()

        maybe(when, start)

    def arrived(unit, when=None):
        f, cc, t = unit

        def wait():
            for piece in range(PIECES):
                ref = spot(whole, piece, f, cc, t)
                pltpu.make_async_copy(ref, ref, recv_sem.at[(f * 4 + cc) * 4 + t, piece]).wait()

        maybe(when, wait)

    other_y = (1 - y) * 2 + k
    first, second = (0, 1), (2, 3)
    me = (x, c, z)
    send("up", me, True, when=z < last)
    send("down", me, True, when=z > 0)
    send("x", me, True)
    send("x", (x, other_y, z), True)

    def at(sign, d):
        t = z + sign * d
        return t, ((t >= 0) if sign < 0 else (t <= last))

    def from_line(sign, d):
        t, have = at(sign, d)
        unit = (x, c, t)
        arrived(unit, have)
        if d < last:
            if sign < 0:
                send("up", unit, when=have & (z < last))
            else:
                send("down", unit, when=have & (z > 0))
        for side in ("x", "y", "core"):
            send(side, unit, when=have)

    def from_plane(sign, d):
        t, have = at(sign, d)
        arrived((1 - x, c, t), have)
        send("y", (1 - x, c, t), pieces=second, when=have)
        send("core", (1 - x, c, t), when=have)
        arrived((x, other_y, t), have)
        send("x", (x, other_y, t), pieces=first, when=have)
        send("core", (x, other_y, t), when=have)

    def from_diagonal(sign, d):
        t, have = at(sign, d)
        arrived((1 - x, other_y, t), have)
        send("core", (1 - x, other_y, t), when=have)

    def both(action, d):
        action(-1, d)
        action(1, d)

    both(from_line, 1)
    arrived((1 - x, c, z))
    send("core", (1 - x, c, z))
    both(from_line, 2)
    arrived((1 - x, other_y, z))
    send("core", (1 - x, other_y, z))
    both(from_plane, 1)
    both(from_line, 3)
    both(from_plane, 2)
    both(from_diagonal, 1)
    both(from_plane, 3)
    both(from_diagonal, 2)
    both(from_diagonal, 3)
    for sign, d in ((-1, 1), (1, 1), (-1, 2), (1, 2), (-1, 3), (1, 3)):
        t, have = at(sign, d)
        for f in (x, 1 - x):
            for yy in (y, 1 - y):
                arrived((f, yy * 2 + 1 - k, t), have)
    for yy in (y, 1 - y):
        arrived((1 - x, yy * 2 + 1 - k, z))
    for when, copies in sent:

        def wait():
            for copy in copies:
                copy.wait_send()

        maybe(when, wait)
    for copy in local + small:
        copy.wait()


def gather(shard, bias):
    ranks = (lax.axis_size("fsdp"), lax.axis_size("ctx"), lax.axis_size("tp"))
    rows, width = shard.shape[1:]
    if ranks != (2, 4, 4):
        part = rows // ranks[1]
        mine = lax.dynamic_slice_in_dim(shard, lax.axis_index("ctx") * part, part, 1)
        tall = lax.all_gather(mine, ("fsdp", "ctx"), axis=1, tiled=True)
        return lax.all_gather(tall, "tp", axis=2, tiled=True), lax.all_gather(bias, "tp")
    return pl.pallas_call(
        gather_kernel,
        out_shape=(
            jax.ShapeDtypeStruct((PIECES, rows * 2, width * 4), BF),
            jax.ShapeDtypeStruct((4,) + bias.shape, F32),
        ),
        in_specs=[pl.BlockSpec(memory_space=pltpu.VMEM)] * 2,
        out_specs=[pl.BlockSpec(memory_space=pl.ANY), pl.BlockSpec(memory_space=pltpu.VMEM)],
        scratch_shapes=[
            pltpu.SemaphoreType.DMA((260,)),
            pltpu.SemaphoreType.DMA((32, PIECES)),
            pltpu.SemaphoreType.DMA((PIECES,)),
            pltpu.SemaphoreType.DMA((3,)),
            pltpu.SemaphoreType.DMA((3,)),
        ],
        compiler_params=pltpu.CompilerParams(collective_id=0, has_side_effects=True),
        name="gather_weights",
    )(shard, bias)


def scatter(grads, vectors):
    tall = lax.psum_scatter(jnp.concatenate(grads), ("fsdp", "ctx"), scatter_dimension=1, tiled=True)
    own = lax.psum_scatter(tall, "tp", scatter_dimension=2, tiled=True)
    return own.astype(F32), lax.psum(vectors, ALL)


def nn(a, b):
    return lax.dot_general(a, b, (((1,), (0,)), ((), ())), preferred_element_type=F32)


def nt(a, b):
    return lax.dot_general(a, b, (((1,), (1,)), ((), ())), preferred_element_type=F32)


def tn(a, b):
    return lax.dot_general(a, b, (((0,), (0,)), ((), ())), preferred_element_type=F32)


def normalise(rows):
    centre = rows - jnp.mean(rows, axis=-1, keepdims=True)
    scale = lax.rsqrt(jnp.mean(centre * centre, axis=-1, keepdims=True) + EPSILON)
    return centre * scale, scale


def chunks(count):
    size = 80 if count % 80 == 0 else 208
    return size, count // size


def norm_into(source, norm, target):
    size, number = chunks(source.shape[0])

    def body(i, carry):
        span = pl.ds(pl.multiple_of(i * size, 16), size)
        unit, _ = normalise(source[span])
        target[span] = (unit * norm[0:1] + norm[1:2]).astype(BF)
        return carry

    lax.fori_loop(0, number, body, 0)


def norm_back_into(source, norm, grad, total, vec, line):
    size, number = chunks(source.shape[0])
    vec[line : line + 2] = jnp.zeros((2, source.shape[1]), F32)

    def body(i, carry):
        span = pl.ds(pl.multiple_of(i * size, 16), size)
        back, gain, shift = norm_back(source[span], norm[0:1], grad[span])
        total[span] += back
        vec[line : line + 1] += gain
        vec[line + 1 : line + 2] += shift
        return carry

    lax.fori_loop(0, number, body, 0)


def round_into(source, target, vec, line):
    size, number = chunks(source.shape[0])
    vec[line : line + 1] = jnp.zeros((1, source.shape[1]), F32)

    def body(i, carry):
        span = pl.ds(pl.multiple_of(i * size, 16), size)
        rounded = source[span].astype(BF)
        target[span] = rounded
        vec[line : line + 1] += jnp.sum(rounded.astype(F32), axis=0, keepdims=True)
        return carry

    lax.fori_loop(0, number, body, 0)


def flip_into(source, target):
    rows = source.shape[0]
    for low in range(0, rows, 128):
        high = min(rows, low + 128)
        target[:, low:high] = source[low:high].T


def norm_back(rows, gain, grad):
    unit, scale = normalise(rows)
    inner = grad * gain
    mean = jnp.mean(inner, axis=-1, keepdims=True)
    along = jnp.mean(inner * unit, axis=-1, keepdims=True)
    return scale * (inner - mean - unit * along), jnp.sum(grad * unit, axis=0, keepdims=True), jnp.sum(
        grad, axis=0, keepdims=True
    )


def lanes_in(low, high):
    lane = lax.broadcasted_iota(jnp.int32, (1, 256), 1)
    return jnp.where((lane >= low) & (lane < high), 1.0, 0.0)


def stack_heads(values):
    return jnp.concatenate(
        [values * lanes_in(i * HEAD, i * HEAD + HEAD).astype(BF) for i in range(3)], axis=0
    )


def pick_heads(stacked):
    rows = stacked.shape[0] // 3
    return sum(
        stacked[i * rows : (i + 1) * rows] * lanes_in(i * HEAD, i * HEAD + HEAD) for i in range(3)
    )


def shifted(values):
    return pltpu.roll(values, 64, axis=1)


def unshifted(values):
    return pltpu.roll(values, 192, axis=1)


def block(w_ref, t, start, size):
    return w_ref[:, pl.ds(pl.multiple_of(t * (w_ref.shape[1] // 4) + start, 128), size)]


def spatial_probs(ref):
    return lambda t, g: ref.at[t, g]


def small_probs(ref, size):
    def find(t, g):
        row, lane = ((g % 2) * 3 * size, 0) if g < 4 else (0, 128)
        return ref.at[t, g // 2 % 2, pl.ds(row, 3 * size), pl.ds(lane, size)]

    return find


class Attention:
    def __init__(self, groups, rows, penalty, w, bias, q, k, v, o, p):
        self.groups, self.rows, self.penalty = groups, rows, penalty
        self.w, self.bias, self.q, self.k, self.v, self.o, self.p = w, bias, q, k, v, o, p

    def spans(self):
        return [(g, pl.ds(g * self.rows, self.rows)) for g in range(self.groups)]

    def forward(self, normed, total):
        used = lanes_in(0, 192)

        def body(t, carry):
            mixed = nn(normed[...], block(self.w, t, 0, 640))
            self.q[t] = ((mixed[:, :256] + self.bias[t, 0:1]) * used).astype(BF)
            self.k[t] = (unshifted(mixed[:, 128:384]) * used).astype(BF)
            self.v[t] = ((mixed[:, 384:] + self.bias[t, 1:2]) * used).astype(BF)
            for g, span in self.spans():
                scores = nt(stack_heads(self.q[t, span]), self.k[t, span]) * 0.125 + self.penalty()
                weights = jnp.exp(scores - jnp.max(scores, axis=-1, keepdims=True))
                weights = weights * (1.0 / jnp.sum(weights, axis=-1, keepdims=True))
                weights = weights.astype(BF)
                self.p(t, g)[...] = weights
                out = pick_heads(nn(weights, self.v[t, span]))
                self.o[t, span] = shifted(out).astype(BF)
            total[...] += nt(self.o[t, pl.ds(0, self.groups * self.rows)], block(self.w, t, 512, 256))
            return carry

        lax.fori_loop(0, 4, body, 0)

    def backward(self, normed_t, branch, branch_t, dk, dv, grad_normed, grad_w, grad_bias, after):
        used = lanes_in(0, 192)

        def body(i, carry):
            t = (3 * i) % 4
            grad_o = (unshifted(nn(branch[...], block(self.w, t, 512, 256))) * used).astype(BF)
            dq = []
            for g, span in self.spans():
                stacked = stack_heads(grad_o[g * self.rows : (g + 1) * self.rows])
                weights = self.p(t, g)[...]
                probs = weights.astype(F32)
                grad_p = nt(stacked, self.v[t, span])
                inner = jnp.sum(probs * grad_p, axis=-1, keepdims=True)
                grad_s = (probs * (grad_p - inner)).astype(BF)
                dq.append((pick_heads(nn(grad_s, self.k[t, span])) * 0.125).astype(BF))
                dk[span] = shifted(tn(grad_s, stack_heads(self.q[t, span])) * 0.125).astype(BF)
                dv[span] = tn(weights, stacked).astype(BF)
            extra = normed_t.shape[1] - self.groups * self.rows
            if extra:
                dq.append(jnp.zeros((extra, 256), BF))
            dq = jnp.concatenate(dq, axis=0)
            grad_normed[...] += (
                nt(dq, block(self.w, t, 0, 256))
                + nt(dk[...], block(self.w, t, 128, 256))
                + nt(dv[...], block(self.w, t, 384, 256))
            )
            for start, low, high in (
                (0, nn(normed_t[...], dq), nn(normed_t[...], dk[...])),
                (384, nn(normed_t[...], dv[...]), nn(branch_t[...], self.o[t])),
            ):
                columns = pl.multiple_of(t * (self.w.shape[1] // 4) + start, 128)
                grad_w[:, pl.ds(columns, 128)] = low[:, :128].astype(BF)
                grad_w[:, pl.ds(columns + 128, 128)] = (low[:, 128:] + high[:, :128]).astype(BF)
                grad_w[:, pl.ds(columns + 256, 128)] = high[:, 128:].astype(BF)
            grad_bias[t, 0:1] = jnp.sum(dq.astype(F32), axis=0, keepdims=True)
            grad_bias[t, 1:2] = jnp.sum(dv[...].astype(F32), axis=0, keepdims=True)
            after(i)
            return carry

        lax.fori_loop(0, 4, body, 0)


SP = 208


def spatial_penalty(places):
    def penalty():
        lane = lax.broadcasted_iota(jnp.int32, (1, SP), 1)
        return jnp.where(lane < places, 0.0, -1e30)
    return penalty


def spatial_forward_kernel(x_ref, w_ref, bias_ref, norm_ref, ob_ref, h_out, q, k, v, o, p, total, normed):
    clips, places, model = x_ref.shape
    for g in range(clips):
        total[pl.ds(g * SP, places)] = x_ref[g].astype(F32)
        total[pl.ds(g * SP + places, SP - places)] = jnp.zeros((SP - places, model), F32)
        span = pl.ds(g * SP, SP)
        unit, _ = normalise(total[span])
        normed[span] = (unit * norm_ref[0:1] + norm_ref[1:2]).astype(BF)
        total[span] += ob_ref[...]
    att = Attention(clips, SP, spatial_penalty(places), w_ref.at[0], bias_ref, q, k, v, o, spatial_probs(p))
    att.forward(normed, total)
    for g in range(clips):
        h_out[g] = total[pl.ds(g * SP, places)].astype(BF)


def spatial_back_kernel(x_ref, g_ref, w_ref, norm_ref, q, k, v, o, p,
                        gx_out, gw, gbias, gvec, total, normed, normed_t, branch, branch_t, dk, dv, gn, rows_in):
    clips, places, model = x_ref.shape
    for g in range(clips):
        for ref, source in ((rows_in, x_ref), (total, g_ref)):
            ref[pl.ds(g * SP, places)] = source[g].astype(F32)
            ref[pl.ds(g * SP + places, SP - places)] = jnp.zeros((SP - places, model), F32)
    attention_back(Attention(clips, SP, None, w_ref.at[0], None, q, k, v, o, spatial_probs(p)),
                   rows_in, total, norm_ref, normed, normed_t, branch, branch_t, dk, dv, gn, gw.at[0], gbias, gvec, 0, lambda i: None)
    for g in range(clips):
        gx_out[g] = total[pl.ds(g * SP, places)].astype(BF)


def attention_back(
    att, rows_in, total, norm, normed, normed_t, branch, branch_t, dk, dv, gn, grad_w, gbias, vec, line, after
):
    round_into(total, branch, vec, line + 2)
    flip_into(branch, branch_t)
    norm_into(rows_in, norm, normed)
    flip_into(normed, normed_t)
    gn[...] = jnp.zeros(gn.shape, F32)
    att.backward(normed_t, branch, branch_t, dk, dv, gn, grad_w, gbias, after)
    norm_back_into(rows_in, norm, gn, total, vec, line)


def by_pair(source, target, mix):
    frames, pairs, model = source.shape
    for f in range(frames):
        values = source[f].astype(F32)
        for i in range(model // 128):
            mix[i, pl.ds(f, pairs, stride=frames)] = values[:, i * 128 : i * 128 + 128]
    for i in range(model // 128):
        target[:, i * 128 : i * 128 + 128] = mix[i]


def by_frame(source, target, mix):
    frames, pairs, model = target.shape
    for i in range(model // 128):
        mix[i] = source[:, i * 128 : i * 128 + 128]
    for f in range(frames):
        for i in range(model // 128):
            target[f, :, i * 128 : i * 128 + 128] = mix[i, pl.ds(f, pairs, stride=frames)].astype(BF)


TG = 5


def temporal_kernel(h_ref, g_ref, w_ref, u_ref, d_ref, bias_ref, norm_ref, norm2_ref, ob_ref, ub_ref, db_ref, pen_ref,
                    y_out, g_out, gw, gu, gd, gbias, gvec, gvec2, gub,
                    q, k, v, o, p, rows_in, total, third, grad, normed, normed_t, branch, branch_t, dk, dv, gn, mix):
    frames, pairs, model = h_ref.shape
    rows = frames * pairs
    by_pair(h_ref, rows_in, mix)
    by_pair(g_ref, grad, mix)
    unit, _ = normalise(rows_in[...])
    normed[...] = (unit * norm_ref[0:1] + norm_ref[1:2]).astype(BF)
    third[...] = rows_in[...] + ob_ref[...]
    group = TG * frames
    att = Attention(pairs // TG, group, lambda: pen_ref[...], w_ref.at[0], bias_ref, q, k, v, o, spatial_probs(p))
    att.forward(normed, third)
    unit, _ = normalise(third[...])
    n2 = unit * norm2_ref[0:1] + norm2_ref[1:2]
    normed[...] = n2.astype(BF)
    normed_t[...] = n2.T.astype(BF)
    branch[...] = grad[...].astype(BF)
    branch_t[...] = grad[...].T.astype(BF)
    gvec2[2:3] = jnp.sum(grad[...], axis=0, keepdims=True)
    total[...] = third[...] + db_ref[...]
    gn[...] = jnp.zeros_like(gn)
    size = 384
    def mlp(j, carry):
        columns = pl.ds(pl.multiple_of(j * size, 128), size)
        up = u_ref[0, :, columns]
        down = d_ref[0, :, columns]
        hidden = nn(normed[...], up) + ub_ref[j]
        half = 0.5 + 0.5 * lax.erf(hidden * (2.0 ** -0.5))
        active = (hidden * half).astype(BF)
        slope = half + hidden * (jnp.exp(-0.5 * hidden * hidden) * ((2.0 * jnp.pi) ** -0.5))
        grad_hidden = nn(branch[...], down) * slope
        rounded = grad_hidden.astype(BF)
        gub[j] = jnp.sum(rounded.astype(F32), axis=0, keepdims=True)
        total[...] += nt(active, down)
        gn[...] += nt(rounded, up)
        gd[0, :, columns] = nn(branch_t[...], active).astype(BF)
        gu[0, :, columns] = nn(normed_t[...], rounded).astype(BF)
        return carry
    lax.fori_loop(0, u_ref.shape[2] // size, mlp, 0)
    by_frame(total, y_out, mix)
    back, gain, shift = norm_back(third[...], norm2_ref[0:1], gn[...])
    grad[...] += back
    gvec2[0:1] = gain
    gvec2[1:2] = shift
    attention_back(att, rows_in, grad, norm_ref, normed, normed_t, branch, branch_t, dk, dv, gn, gw.at[0], gbias, gvec, 0, lambda i: None)
    by_frame(grad, g_out, mix)


def piece_spec(piece, whole):
    return pl.BlockSpec((1,) + whole.shape[1:], lambda i: (piece, 0, 0))


def full_spec(value):
    return pl.BlockSpec(value.shape, lambda i: (0,) * len(value.shape))


def run(kernel, args, specs, outs, scratch, name):
    return pl.pallas_call(
        kernel, grid=(1,),
        out_shape=outs, in_specs=specs, out_specs=[full_spec(out) for out in outs], scratch_shapes=scratch,
        compiler_params=pltpu.CompilerParams(vmem_limit_bytes=63 * 2**20),
        name=name,
    )(*args)


def shape(*size, dtype=BF):
    return jax.ShapeDtypeStruct(size, dtype)


def spatial_forward(x, whole, bias, norm, out_bias):
    clips, places, model = x.shape
    rows = clips * SP
    args = (x, whole, bias, norm, out_bias)
    specs = [full_spec(a) for a in args]
    specs[1] = piece_spec(0, whole)
    outs = [shape(clips, places, model)] + [shape(4, rows, 256)] * 4 + [shape(4, clips, 3 * SP, SP)]
    return run(spatial_forward_kernel, args, specs, outs,
               [pltpu.VMEM((rows, model), F32), pltpu.VMEM((rows, model), BF)], "spatial_forward")


def spatial_back(x, g, whole, norm, kept):
    clips, places, model = x.shape
    rows = clips * SP
    args = (x, g, whole, norm) + tuple(kept)
    specs = [full_spec(a) for a in args]
    specs[2] = piece_spec(0, whole)
    outs = [shape(clips, places, model), shape(1, *whole.shape[1:]), shape(4, 2, 256, dtype=F32), shape(3, model, dtype=F32)]
    scratch = [pltpu.VMEM((rows, model), F32), pltpu.VMEM((rows, model), BF), pltpu.VMEM((model, rows), BF), pltpu.VMEM((rows, model), BF),
               pltpu.VMEM((model, rows), BF), pltpu.VMEM((rows, 256), BF), pltpu.VMEM((rows, 256), BF),
               pltpu.VMEM((rows, model), F32), pltpu.VMEM((rows, model), F32)]
    return run(spatial_back_kernel, args, specs, outs, scratch, "spatial_back")


def temporal(h, g, whole, bias, norm, norm2, out_bias, up_bias, down_bias):
    frames, pairs, model = h.shape
    rows = frames * pairs
    group = TG * frames
    row = jnp.arange(3 * group)[:, None] % group // frames
    column = jnp.arange(group)[None] // frames
    penalty = jnp.where(row == column, 0.0, -1e30).astype(F32)
    args = (h, g, whole, whole, whole, bias, norm, norm2, out_bias, up_bias.reshape(-1, 1, 384), down_bias, penalty)
    specs = [full_spec(a) for a in args]
    for i, piece in ((2, 1), (3, 2), (4, 3)):
        specs[i] = piece_spec(piece, whole)
    hidden = whole.shape[2]
    outs = [shape(frames, pairs, model), shape(frames, pairs, model), shape(1, model, hidden), shape(1, model, hidden),
            shape(1, model, hidden), shape(4, 2, 256, dtype=F32), shape(3, model, dtype=F32), shape(3, model, dtype=F32),
            shape(hidden // 384, 1, 384, dtype=F32)]
    big = pltpu.VMEM((rows, model), F32)
    low = pltpu.VMEM((rows, model), BF)
    flip = pltpu.VMEM((model, rows), BF)
    part = pltpu.VMEM((rows, 256), BF)
    scratch = [pltpu.VMEM((4, rows, 256), BF)] * 4 + [pltpu.VMEM((4, pairs // TG, 3 * group, group), BF)] + [
        big, big, big, big, low, flip, low, flip, part, part, big, pltpu.VMEM((model // 128, rows, 128), F32)]
    return run(temporal_kernel, args, specs, outs, scratch, "temporal_and_mlp")


STEPS = 16


class Refs:
    def __init__(self, names, refs):
        for name, ref in zip(names, refs, strict=True):
            setattr(self, name, ref)


def pair_segments(index, share, clips, places):
    found = []
    for clip in range(clips):
        low = max(index * share, clip * places)
        high = min(index * share + share, clip * places + places)
        if low < high:
            found.append((low - index * share, high - low, clip, low - clip * places))
    return found


class Reduction:
    def __init__(self, r, places, x, y, k, z, rows, width):
        self.r, self.places, self.rows, self.width = r, places, rows, width
        self.x, self.y, self.k, self.z = x, y, k, z
        self.quads = [(f, yy) for f in range(2) for yy in range(2)]
        self.last = 3

    def piece_of(self, s):
        if isinstance(s, int):
            return 2 + s % 2 if s < 8 else 1 if s < 12 else 0
        early, middle = (s < 8).astype(jnp.int32), ((s >= 8) & (s < 12)).astype(jnp.int32)
        return early * (2 + s % 2) + middle

    def tp_of(self, s):
        if isinstance(s, int):
            return 3 * (s // 2 if s < 8 else s) % 4
        early = (s < 8).astype(jnp.int32)
        return (3 * (early * (s // 2) + (1 - early) * s)) % 4

    def spot(self, f, yy, kk, s):
        row = pl.multiple_of((f * 4 + yy * 2 + kk) * self.rows, 16)
        column = pl.multiple_of(self.tp_of(s) * self.width, 128)
        return self.r.w.at[self.piece_of(s), pl.ds(row, self.rows), pl.ds(column, self.width)]

    def remote(self, src, dst, send, recv, side):
        return pltpu.make_async_remote_copy(
            src_ref=src, dst_ref=dst, send_sem=send, recv_sem=recv,
            device_id=self.places[side], device_id_type=MESH,
        )

    def core_copy(self, s, f, yy):
        r = self.r
        return self.remote(
            self.spot(f, yy, 1 - self.k, s), r.r1.at[s, f, yy], r.s1.at[s, f, yy], r.q1.at[s, f, yy], "core"
        )

    def diag_copy(self, s, side):
        r = self.r
        return self.remote(r.r1.at[s, 1 - self.x, 1 - self.y], r.r2.at[s], r.s2.at[s], r.q2.at[s], side)

    def x_copy(self, s):
        r = self.r
        return self.remote(r.r1.at[s, 1 - self.x, self.y], r.r3x.at[s], r.s3x.at[s], r.q3x.at[s], "x")

    def y_copy(self, s):
        r = self.r
        return self.remote(r.r1.at[s, self.x, 1 - self.y], r.r3y.at[s], r.s3y.at[s], r.q3y.at[s], "y")

    def up_copy(self, s):
        r = self.r
        return self.remote(r.r1.at[s, self.x, self.y], r.rz.at[s], r.sz.at[s], r.qup.at[s], "up")

    def down_copy(self, s, owner=False):
        r = self.r
        target = r.re.at[self.piece_of(s)] if owner else r.rz.at[s]
        return self.remote(r.r1.at[s, self.x, self.y], target, r.sz.at[s], r.qdn.at[s], "down")

    def start(self, s):
        for f, yy in self.quads:
            self.core_copy(s, f, yy).start()

    def even_odd(self, s, even, odd):
        if isinstance(s, int):
            (odd if s % 2 else even)()
        else:
            pl.when(s % 2 == 0)(even)
            pl.when(s % 2 == 1)(odd)

    def chip_sum(self, s):
        r1 = self.r.r1
        for f, yy in self.quads:
            self.core_copy(s, f, yy).wait_recv()
            r1[s, f, yy] = r1[s, f, yy] + self.spot(f, yy, self.k, s)[...]

        def even():
            self.diag_copy(s, "x").start()
            self.x_copy(s).start()

        def odd():
            self.diag_copy(s, "y").start()
            self.y_copy(s).start()

        self.even_odd(s, even, odd)

    def turn(self, s):
        r1, r2, x, y = self.r.r1, self.r.r2, self.x, self.y
        self.diag_copy(s, "x").wait_recv()

        def even():
            r1[s, x, 1 - y] = r1[s, x, 1 - y] + r2[s]
            self.y_copy(s).start()

        def odd():
            r1[s, 1 - x, y] = r1[s, 1 - x, y] + r2[s]
            self.x_copy(s).start()

        self.even_odd(s, even, odd)

    def plane_sum(self, s):
        r = self.r
        self.x_copy(s).wait_recv()
        self.y_copy(s).wait_recv()
        total = r.r1[s, self.x, self.y].astype(F32) + r.r3x[s].astype(F32) + r.r3y[s].astype(F32)
        r.r1[s, self.x, self.y] = total.astype(BF)

    def line(self, s, hop):
        r, x, y, z, last = self.r, self.x, self.y, self.z, self.last
        t = self.tp_of(s)

        @pl.when((z < t) & (z == hop))
        def _():
            if hop > 0:
                self.up_copy(s).wait_recv()
                r.r1[s, x, y] = r.r1[s, x, y] + r.rz[s]
            self.up_copy(s).start()

        @pl.when((z > t) & (last - z == hop))
        def _():
            if hop > 0:
                self.down_copy(s).wait_recv()
                r.r1[s, x, y] = r.r1[s, x, y] + r.rz[s]

            @pl.when(z - 1 == t)
            def _():
                self.down_copy(s, True).start()

            @pl.when(z - 1 != t)
            def _():
                self.down_copy(s).start()

        far = z + (last - 2 * z) * ((last - 2 * z) > 0).astype(jnp.int32)

        @pl.when((z == t) & (far == hop))
        def _():
            piece = self.piece_of(s)
            r.own[piece] = r.r1[s, x, y].astype(F32)

            @pl.when(z > 0)
            def _():
                self.up_copy(s).wait_recv()
                r.own[piece] = r.own[piece] + r.rz[s].astype(F32)

            @pl.when(z < last)
            def _():
                self.down_copy(s, True).wait_recv()
                r.own[piece] = r.own[piece] + r.re[piece].astype(F32)

    def guard(self, action, s, *rest):
        if isinstance(s, int):
            if 0 <= s < STEPS:
                action(s, *rest)
        else:

            @pl.when((s >= 0) & (s < STEPS))
            def _():
                action(s, *rest)

    def tick(self, n):
        self.guard(self.chip_sum, n - 1)
        self.guard(self.turn, n - 2)
        self.guard(self.plane_sum, n - 4)
        for hop in range(4):
            self.guard(self.line, n - 5 - hop, hop)

    def finish(self):
        def body(s, carry):
            for f, yy in self.quads:
                self.core_copy(s, f, yy).wait_send()
            self.diag_copy(s, "x").wait_send()
            self.x_copy(s).wait_send()
            self.y_copy(s).wait_send()

            @pl.when(self.z != self.tp_of(s))
            def _():
                self.up_copy(s).wait_send()

            return carry

        lax.fori_loop(0, STEPS, body, 0)


BACK_NAMES = [
    "h", "x", "g", "whole", "q_in", "k_in", "v_in", "o_in", "p_in", "bias", "norm", "ob", "ub", "db",
    "penalty", "y_home", "g_home", "own", "vectors", "w", "q", "k", "v", "o", "p", "rows_in", "total",
    "third", "grad", "gn", "mix", "normed", "normed_t", "branch", "branch_t", "dk", "dv", "y_send",
    "g_send", "g_recv", "home_send", "bias1", "bias0", "ups", "r1", "r2", "r3x", "r3y", "rz", "re", "va",
    "vr", "load", "s1", "q1", "s2", "q2", "s3x", "s3y", "q3x", "q3y", "sz", "qup", "qdn", "vs", "vq", "ys",
    "yq", "gs", "gq", "hs", "hq", "keep", "early",
]


def back_kernel(*refs):
    r = Refs(BACK_NAMES, refs)
    x, c, z = lax.axis_index("fsdp"), lax.axis_index("ctx"), lax.axis_index("tp")
    y, k = c // 2, c % 2
    clips, places, model = r.x.shape
    frames, share = r.h.shape[:2]
    home_places = places // 4
    me = c * 4 + z
    where = places_of(x, y, k, z)

    barrier = pltpu.get_barrier_semaphore()
    pl.semaphore_signal(barrier, inc=1, device_id=where["x"], device_id_type=MESH)

    def greet(d, carry):
        peer = (me + d) % 16
        pl.semaphore_signal(barrier, inc=1, device_id=(x, peer // 4, peer % 4), device_id_type=MESH)
        return carry

    lax.fori_loop(1, 16, greet, 0)

    loads = [pltpu.make_async_copy(r.whole.at[i], r.w.at[i], r.load.at[i]) for i in range(4)]
    for i in (1, 2, 3, 0):
        loads[i].start()
    kept = [
        pltpu.make_async_copy(source, target, r.keep.at[i])
        for i, (source, target) in enumerate(
            ((r.q_in, r.q), (r.k_in, r.k), (r.v_in, r.v), (r.o_in, r.o), (r.p_in, r.p))
        )
    ]

    early = [
        pltpu.make_async_copy(source, target, r.early.at[i])
        for i, (source, target) in enumerate(((r.h, r.y_send), (r.g, r.g_send)))
    ]
    for copy in early:
        copy.start()
    for copy in early:
        copy.wait()
    frames_in = r.rows_in.at[pl.ds(0, frames * share)]
    by_pair(r.y_send, frames_in, r.mix)
    by_pair(r.g_send, r.grad, r.mix)
    normed = r.normed.at[pl.ds(0, frames * share)]
    norm_into(frames_in, r.norm.at[1], normed)
    r.third[...] = frames_in[...] + r.ob[1:2]
    group = TG * frames
    rows = frames * share
    loads[1].wait()
    att = Attention(
        share // TG, group, lambda: r.penalty[...], r.w.at[1], r.bias.at[1],
        *(ref.at[:, pl.ds(0, rows)] for ref in (r.q, r.k, r.v)), r.o, small_probs(r.p, group),
    )
    spare = r.normed.shape[0] - rows
    for ref in (r.normed, r.branch, r.dk, r.dv):
        ref[rows:] = jnp.zeros((spare, ref.shape[1]), BF)
    for t in range(4):
        r.o[t, rows:] = jnp.zeros((spare, r.o.shape[2]), BF)
    r.total[rows:] = jnp.zeros((spare, model), F32)
    att.forward(normed, r.third)

    norm_into(r.third, r.norm.at[2], normed)
    flip_into(r.normed, r.normed_t)
    va = r.va.at[0]
    round_into(r.grad, r.branch, va, 8)
    flip_into(r.branch, r.branch_t)
    r.total[0:rows] = r.third[...] + r.db[...]
    r.gn[...] = jnp.zeros(r.gn.shape, F32)
    loads[2].wait()
    loads[3].wait()
    pl.semaphore_wait(barrier, 16)
    red = Reduction(r, where, x, y, k, z, r.own.shape[1], r.own.shape[2])
    size = r.ub.shape[2]
    halves = r.own.shape[2] // size

    def mlp(i, carry):
        t = (3 * i) % 4
        for half in range(halves):
            j = t * halves + half
            columns = pl.ds(pl.multiple_of(j * size, 128), size)
            up = r.w[2, :, columns]
            down = r.w[3, :, columns]
            hidden = nn(r.normed[...], up) + r.ub[j]
            cdf = 0.5 + 0.5 * lax.erf(hidden * (2.0**-0.5))
            active = (hidden * cdf).astype(BF)
            slope = cdf + hidden * (jnp.exp(-0.5 * hidden * hidden) * ((2.0 * jnp.pi) ** -0.5))
            rounded = (nn(r.branch[...], down) * slope).astype(BF)
            r.ups[j] = jnp.sum(rounded.astype(F32), axis=0, keepdims=True)
            r.total[...] += nt(active, down)
            r.gn[...] += nt(rounded, up)
            r.w[3, :, columns] = nn(r.branch_t[...], active).astype(BF)
            r.w[2, :, columns] = nn(r.normed_t[...], rounded).astype(BF)
        for s in (2 * i, 2 * i + 1):
            red.start(s)
        for s in (2 * i, 2 * i + 1):
            red.tick(s)
        return carry

    lax.fori_loop(0, 4, mlp, 0)

    by_frame(r.total.at[pl.ds(0, rows)], r.y_send, r.mix)
    outs = []
    for d in range(1, 4):
        peer = (c + d) % 4
        copy = pltpu.make_async_remote_copy(
            src_ref=r.y_send.at[pl.ds(peer * 4, 4)], dst_ref=r.y_home.at[c],
            send_sem=r.ys.at[d], recv_sem=r.yq.at[d], device_id=(x, peer, z), device_id_type=MESH,
        )
        copy.start()
        outs.append(copy)
    y_own = pltpu.make_async_copy(r.y_send.at[pl.ds(c * 4, 4)], r.y_home.at[c], r.ys.at[0])
    y_own.start()

    norm_back_into(r.third, r.norm.at[2], r.gn, r.grad, va, 6)

    def each(first):
        def after(i):
            red.start(first + i)
            maybe(i > 0 if first == 12 else None, lambda: red.tick(first + i))

        return after

    attention_back(
        att, frames_in, r.grad, r.norm.at[1], r.normed, r.normed_t, r.branch, r.branch_t,
        r.dk, r.dv, r.gn, r.w.at[1], r.bias1, va, 3, each(8),
    )
    for copy in kept:
        copy.start()
    by_frame(r.grad, r.g_send, r.mix)

    def to_frame(d):
        peer = (me + d) % 16
        return pltpu.make_async_remote_copy(
            src_ref=r.g_send.at[peer], dst_ref=r.g_recv.at[me],
            send_sem=r.gs.at[d], recv_sem=r.gq.at[d], device_id=(x, peer // 4, peer % 4), device_id_type=MESH,
        )

    def go(d, carry):
        to_frame(d).start()
        return carry

    lax.fori_loop(1, 16, go, 0)
    r.g_recv[me] = r.g_send[me]
    red.tick(12)
    for copy in kept:
        copy.wait()
    loads[0].wait()
    srows = clips * SP
    for clip in range(clips):
        r.rows_in[pl.ds(clip * SP, places)] = r.x[clip].astype(F32)
        r.rows_in[pl.ds(clip * SP + places, SP - places)] = jnp.zeros((SP - places, model), F32)
        r.total[pl.ds(clip * SP + places, SP - places)] = jnp.zeros((SP - places, model), F32)

    def come(d, carry):
        to_frame(d).wait()
        return carry

    lax.fori_loop(1, 16, come, 0)
    for cc in range(4):
        for zz in range(4):
            r.third[0:share] = r.g_recv[cc * 4 + zz].astype(F32)
            for start, count, clip, place in pair_segments(cc, share, clips, home_places):
                row = clip * SP + zz * home_places + place
                r.total[row : row + count] = r.third[start : start + count]

    att = Attention(clips, SP, None, r.w.at[0], None, r.q, r.k, r.v, r.o, spatial_probs(r.p))
    attention_back(
        att, r.rows_in, r.total, r.norm.at[0], r.normed, r.normed_t, r.branch, r.branch_t, r.dk, r.dv, r.gn,
        r.w.at[0], r.bias0, va, 0, each(12),
    )
    for zz in range(4):
        for clip in range(clips):
            row = clip * SP + zz * home_places
            r.third[0:home_places] = r.total[row : row + home_places]
            r.home_send[zz, clip] = r.third[0:home_places].astype(BF)
    for d in range(1, 4):
        peer = (z + d) % 4
        copy = pltpu.make_async_remote_copy(
            src_ref=r.home_send.at[peer], dst_ref=r.g_home.at[z],
            send_sem=r.hs.at[d], recv_sem=r.hq.at[d], device_id=(x, c, peer), device_id_type=MESH,
        )
        copy.start()
        outs.append(copy)
    g_own = pltpu.make_async_copy(r.home_send.at[z], r.g_home.at[z], r.hs.at[0])
    g_own.start()

    for j in range(r.ups.shape[0]):
        va[9 + j // halves : 10 + j // halves, (j % halves) * size : (j % halves + 1) * size] = r.ups[j]
    for i, ref in enumerate((r.bias0, r.bias1)):
        for t in range(4):
            va[16 + i * 8 + t * 2 : 18 + i * 8 + t * 2, 0:256] = ref[t]
    sides = ("core", "x", "y", "z1", "z2")

    def v_copy(j):
        return red.remote(r.va.at[j], r.vr.at[j], r.vs.at[j], r.vq.at[j], sides[j])

    v_copy(0).start()
    for n in range(16, STEPS + 8):
        red.tick(n)
        j = n - 16
        if j < 5:
            v_copy(j).wait()
            if j < 4:
                r.va[j + 1] = r.va[j] + r.vr[j]
                v_copy(j + 1).start()
            else:
                r.vectors[...] = r.va[j] + r.vr[j]
    red.finish()
    for copy in outs:
        copy.wait()
    y_own.wait()
    g_own.wait()


def backward(h, x, g, whole, kept, bias, norm, out_bias, up_bias, down_bias, own_rows, width):
    frames, share, model = h.shape
    clips, places = x.shape[:2]
    rows, srows = frames * share, clips * SP
    group = TG * frames
    row = jnp.arange(3 * group)[:, None] % group // frames
    column = jnp.arange(group)[None] // frames
    penalty = jnp.where(row == column, 0.0, -1e30).astype(F32)
    size = 384
    anywhere, vmem = pl.BlockSpec(memory_space=pl.ANY), pl.BlockSpec(memory_space=pltpu.VMEM)
    args = (h, x, g, whole, *kept, bias, norm, out_bias, up_bias.reshape(-1, 1, size), down_bias, penalty)
    in_specs = [anywhere, vmem] + [anywhere] * 7 + [vmem] * 6
    sub = (own_rows, width)
    big = max(rows, srows)

    def v(*dims, dtype=BF):
        return pltpu.VMEM(dims, dtype)

    def f(*dims):
        return pltpu.VMEM(dims, F32)

    dma = pltpu.SemaphoreType.DMA
    scratch = (
        [v(*whole.shape)]
        + [v(4, big, 256)] * 4
        + [v(4, clips, 3 * SP, SP)]
        + [f(big, model), f(big, model), f(rows, model), f(rows, model), f(big, model)]
        + [f(model // 128, rows, 128)]
        + [v(big, model), v(model, big), v(big, model), v(model, big), v(big, 256), v(big, 256)]
        + [v(frames, share, model), v(frames, share, model), v(frames, share, model)]
        + [v(4, clips, places // 4, model), f(4, 2, 256), f(4, 2, 256), f(up_bias.shape[0] // size, 1, size)]
        + [v(STEPS, 2, 2, *sub)]
        + [v(STEPS, *sub)] * 4
        + [v(PIECES, *sub)]
        + [f(5, 32, model)] * 2
        + [dma((4,))]
        + [dma((STEPS, 2, 2))] * 2
        + [dma((STEPS,))] * 9
        + [dma((5,))] * 2
        + [dma((4,))] * 2
        + [dma((16,))] * 2
        + [dma((4,))] * 2
        + [dma((5,))]
        + [dma((2,))]
    )
    return pl.pallas_call(
        back_kernel,
        out_shape=(
            shape(4, frames // 4, share, model),
            shape(4, clips, places // 4, model),
            shape(PIECES, *sub, dtype=F32),
            shape(32, model, dtype=F32),
        ),
        in_specs=in_specs,
        out_specs=[anywhere, anywhere, vmem, vmem],
        scratch_shapes=scratch,
        compiler_params=pltpu.CompilerParams(
            collective_id=2, has_side_effects=True, vmem_limit_bytes=67043328
        ),
        name="backward",
    )(*args)


def local(
    inputs,
    cotangent,
    norm_gain,
    norm_bias,
    attn_weight,
    attn_bias,
    out_weight,
    out_bias,
    up_weight,
    up_bias,
    down_weight,
    down_bias,
):
    ranks_c = lax.axis_size("ctx")
    tp_rank = lax.axis_index("tp")
    clips, frames, places, model = inputs.shape
    width = attn_weight.shape[3]

    shard = jnp.concatenate(
        [
            jnp.concatenate(
                [
                    attn_weight.transpose(0, 2, 1, 3).reshape(2, attn_weight.shape[2], 3 * width),
                    out_weight.transpose(0, 2, 1),
                ],
                axis=2,
            ),
            up_weight[None],
            down_weight.T[None],
        ]
    )
    bias = jnp.pad(attn_bias.reshape(4, width), ((0, 4), (0, 256 - width)))
    whole, bias = gather(shard, bias)
    bias = bias[:, :4].reshape(4, 2, 2, 256).transpose(1, 0, 2, 3)
    norm = jnp.stack([norm_gain, norm_bias], axis=1)

    pairs = clips * places
    share = -(-pairs // ranks_c)
    share += -share % TG

    def home_to_spatial(values):
        return lax.all_to_all(values, "tp", split_axis=1, concat_axis=2, tiled=True)

    def spatial_to_home(values):
        return lax.all_to_all(values, "tp", split_axis=2, concat_axis=1, tiled=True)

    def home_to_temporal(values):
        rows = values.transpose(1, 0, 2, 3).reshape(frames, pairs, model)
        rows = jnp.pad(rows, ((0, 0), (0, share * ranks_c - pairs), (0, 0)))
        return lax.all_to_all(rows, "ctx", split_axis=1, concat_axis=0, tiled=True)

    def temporal_to_home(values):
        rows = lax.all_to_all(values, "ctx", split_axis=0, concat_axis=1, tiled=True)[:, :pairs]
        return rows.reshape(frames, clips, places, model).transpose(1, 0, 2, 3)

    first = home_to_spatial(inputs)
    spatial_shape = first.shape
    first = first.reshape((-1,) + first.shape[2:])
    second, *kept = spatial_forward(first, whole, bias[0], norm[0], out_bias[0:1])
    second = home_to_temporal(spatial_to_home(second.reshape(spatial_shape)))
    grad_out = home_to_temporal(cotangent)
    ups = up_bias.shape[0] // model
    if lax.axis_size("fsdp") == 2 and (ranks_c, lax.axis_size("tp")) == (4, 4):
        home, grad_home, own, vectors = backward(
            second, first, grad_out, whole, kept, bias, norm, out_bias, up_bias, down_bias[None],
            attn_weight.shape[2] // 4, up_weight.shape[1],
        )
        outputs = home.transpose(1, 0, 2, 3).reshape(frames, -1, model)[:, :pairs]
        outputs = outputs.reshape(frames, clips, places, model).transpose(1, 0, 2, 3)
        input_grad = grad_home.transpose(1, 0, 2, 3)
        sums = vectors[16:, :256].reshape(2, 4, 2, 256)[..., :width].transpose(0, 2, 1, 3)
        attn_bias_sums = sums.reshape(2, 2, model)
    else:
        result, grad_second, grad_attn1, grad_up, grad_down, bias1, vec1, vec2, grad_up_bias = temporal(
            second, grad_out, whole, bias[1], norm[1], norm[2], out_bias[1:2], up_bias, down_bias[None]
        )
        outputs = temporal_to_home(result)
        grad_second = home_to_spatial(temporal_to_home(grad_second)).reshape(first.shape)
        grad_first, grad_attn0, bias0, vec0 = spatial_back(first, grad_second, whole, norm[0], kept)
        input_grad = spatial_to_home(grad_first.reshape(spatial_shape))
        bias_sums = jnp.stack([bias0, bias1])[..., :width].transpose(0, 2, 1, 3)
        lines = [vec0, vec1, vec2, grad_up_bias, bias_sums]
        flat = jnp.concatenate([line.reshape(-1, model) for line in lines])
        vectors = jnp.pad(flat, ((0, -flat.shape[0] % 8), (0, 0)))
        own, vectors = scatter([grad_attn0, grad_attn1, grad_up, grad_down], vectors)
        attn_bias_sums = vectors[9 + ups : 13 + ups].reshape(2, 2, model)
    triples = vectors[:9].reshape(3, 3, model)
    attn = own[:2].reshape(2, own.shape[1], 4, width)
    return (
        outputs,
        input_grad,
        triples[:, 0],
        triples[:, 1],
        attn[:, :, :3].transpose(0, 2, 1, 3),
        lax.dynamic_slice_in_dim(attn_bias_sums, tp_rank * width, width, 2),
        attn[:, :, 3].transpose(0, 2, 1),
        triples[:2, 2],
        own[2],
        vectors[9 : 9 + ups].reshape(-1),
        own[3].T,
        triples[2, 2],
    )


def solution(mesh):
    return jax.shard_map(
        local,
        mesh=mesh,
        in_specs=(
            P("fsdp", "ctx", "tp", None),
            P("fsdp", "ctx", "tp", None),
            P(),
            P(),
            P(None, None, "fsdp", "tp"),
            P(None, None, "tp"),
            P(None, "tp", "fsdp"),
            P(),
            P("fsdp", "tp"),
            P(),
            P("tp", "fsdp"),
            P(),
        ),
        out_specs=(
            P("fsdp", "ctx", "tp", None),
            P("fsdp", "ctx", "tp", None),
            P(),
            P(),
            P(None, None, ("fsdp", "ctx"), "tp"),
            P(None, None, "tp"),
            P(None, "tp", ("fsdp", "ctx")),
            P(),
            P(("fsdp", "ctx"), "tp"),
            P(),
            P("tp", ("fsdp", "ctx")),
            P(),
        ),
        check_vma=False,
    )
```

```python
import jax
import jax.numpy as jnp
from jax import lax
from jax.experimental import pallas as pl
from jax.experimental.pallas import tpu as pltpu
from jax.sharding import PartitionSpec as P

HEAD = 64
EPSILON = 1e-06
BF = jnp.bfloat16
F32 = jnp.float32
MESH = pl.DeviceIdType.MESH
PIECES = 4
ALL = ("fsdp", "ctx", "tp")


def places_of(x, y, k, z):
    return {
        "x": (1 - x, y * 2 + k, z),
        "y": (x, (1 - y) * 2 + k, z),
        "core": (x, y * 2 + 1 - k, z),
        "up": (x, y * 2 + k, z + 1),
        "down": (x, y * 2 + k, z - 1),
        "z1": (x, y * 2 + k, (z // 2) * 2 + 1 - z % 2),
        "z2": (x, y * 2 + k, (z + 2) % 4),
    }


def maybe(when, action):
    if when is None:
        action()
    else:
        pl.when(when)(action)


def gather(shard, bias):
    part = shard.shape[1] // lax.axis_size("ctx")
    mine = lax.dynamic_slice_in_dim(shard, lax.axis_index("ctx") * part, part, 1)
    tall = lax.all_gather(mine, ("fsdp", "ctx"), axis=1, tiled=True)
    return lax.all_gather(tall, "tp", axis=2, tiled=True), lax.all_gather(bias, "tp")


def scatter(grads, vectors):
    tall = lax.psum_scatter(jnp.concatenate(grads), ("fsdp", "ctx"), scatter_dimension=1, tiled=True)
    own = lax.psum_scatter(tall, "tp", scatter_dimension=2, tiled=True)
    return own.astype(F32), lax.psum(vectors, ALL)


def nn(a, b):
    return lax.dot_general(a, b, (((1,), (0,)), ((), ())), preferred_element_type=F32)


def nt(a, b):
    return lax.dot_general(a, b, (((1,), (1,)), ((), ())), preferred_element_type=F32)


def tn(a, b):
    return lax.dot_general(a, b, (((0,), (0,)), ((), ())), preferred_element_type=F32)


def normalise(rows):
    centre = rows - jnp.mean(rows, axis=-1, keepdims=True)
    scale = lax.rsqrt(jnp.mean(centre * centre, axis=-1, keepdims=True) + EPSILON)
    return centre * scale, scale


def chunks(count):
    size = 80 if count % 80 == 0 else 208
    return size, count // size


def norm_into(source, norm, target):
    size, number = chunks(source.shape[0])

    def body(i, carry):
        span = pl.ds(pl.multiple_of(i * size, 16), size)
        unit, _ = normalise(source[span])
        target[span] = (unit * norm[0:1] + norm[1:2]).astype(BF)
        return carry

    lax.fori_loop(0, number, body, 0)


def norm_back_into(source, norm, grad, total, vec, line):
    size, number = chunks(source.shape[0])
    vec[line : line + 2] = jnp.zeros((2, source.shape[1]), F32)

    def body(i, carry):
        span = pl.ds(pl.multiple_of(i * size, 16), size)
        back, gain, shift = norm_back(source[span], norm[0:1], grad[span])
        total[span] += back
        vec[line : line + 1] += gain
        vec[line + 1 : line + 2] += shift
        return carry

    lax.fori_loop(0, number, body, 0)


def round_into(source, target, vec, line):
    size, number = chunks(source.shape[0])
    vec[line : line + 1] = jnp.zeros((1, source.shape[1]), F32)

    def body(i, carry):
        span = pl.ds(pl.multiple_of(i * size, 16), size)
        rounded = source[span].astype(BF)
        target[span] = rounded
        vec[line : line + 1] += jnp.sum(rounded.astype(F32), axis=0, keepdims=True)
        return carry

    lax.fori_loop(0, number, body, 0)


def flip_into(source, target):
    rows = source.shape[0]
    for low in range(0, rows, 128):
        high = min(rows, low + 128)
        target[:, low:high] = source[low:high].T


def norm_back(rows, gain, grad):
    unit, scale = normalise(rows)
    inner = grad * gain
    mean = jnp.mean(inner, axis=-1, keepdims=True)
    along = jnp.mean(inner * unit, axis=-1, keepdims=True)
    return scale * (inner - mean - unit * along), jnp.sum(grad * unit, axis=0, keepdims=True), jnp.sum(
        grad, axis=0, keepdims=True
    )


def lanes_in(low, high):
    lane = lax.broadcasted_iota(jnp.int32, (1, 256), 1)
    return jnp.where((lane >= low) & (lane < high), 1.0, 0.0)


def stack_heads(values):
    return jnp.concatenate(
        [values * lanes_in(i * HEAD, i * HEAD + HEAD).astype(BF) for i in range(3)], axis=0
    )


def pick_heads(stacked):
    rows = stacked.shape[0] // 3
    return sum(
        stacked[i * rows : (i + 1) * rows] * lanes_in(i * HEAD, i * HEAD + HEAD) for i in range(3)
    )


def shifted(values):
    return pltpu.roll(values, 64, axis=1)


def unshifted(values):
    return pltpu.roll(values, 192, axis=1)


def block(w_ref, t, start, size):
    return w_ref[:, pl.ds(pl.multiple_of(t * (w_ref.shape[1] // 4) + start, 128), size)]


def spatial_probs(ref):
    return lambda t, g: ref.at[t, g]


def small_probs(ref, size):
    def find(t, g):
        row, lane = ((g % 2) * 3 * size, 0) if g < 4 else (0, 128)
        return ref.at[t, g // 2 % 2, pl.ds(row, 3 * size), pl.ds(lane, size)]

    return find


class Attention:
    def __init__(self, groups, rows, penalty, w, bias, q, k, v, o, p):
        self.groups, self.rows, self.penalty = groups, rows, penalty
        self.w, self.bias, self.q, self.k, self.v, self.o, self.p = w, bias, q, k, v, o, p

    def spans(self):
        return [(g, pl.ds(g * self.rows, self.rows)) for g in range(self.groups)]

    def forward(self, normed, total, after=lambda i: None):
        used = lanes_in(0, 192)

        def body(t, carry):
            mixed = nn(normed[...], block(self.w, t, 0, 640))
            self.q[t] = ((mixed[:, :256] + self.bias[t, 0:1]) * used).astype(BF)
            self.k[t] = (unshifted(mixed[:, 128:384]) * used).astype(BF)
            self.v[t] = ((mixed[:, 384:] + self.bias[t, 1:2]) * used).astype(BF)
            for g, span in self.spans():
                scores = nt(stack_heads(self.q[t, span]), self.k[t, span]) * 0.125 + self.penalty()
                weights = jnp.exp(scores - jnp.max(scores, axis=-1, keepdims=True))
                weights = weights * (1.0 / jnp.sum(weights, axis=-1, keepdims=True))
                weights = weights.astype(BF)
                self.p(t, g)[...] = weights
                out = pick_heads(nn(weights, self.v[t, span]))
                self.o[t, span] = shifted(out).astype(BF)
            total[...] += nt(self.o[t, pl.ds(0, self.groups * self.rows)], block(self.w, t, 512, 256))
            after(t)
            return carry

        lax.fori_loop(0, 4, body, 0)

    def backward(self, normed_t, branch, branch_t, dk, dv, grad_normed, grad_w, grad_bias, after):
        used = lanes_in(0, 192)

        def body(i, carry):
            t = (3 * i) % 4
            grad_o = (unshifted(nn(branch[...], block(self.w, t, 512, 256))) * used).astype(BF)
            dq = []
            for g, span in self.spans():
                stacked = stack_heads(grad_o[g * self.rows : (g + 1) * self.rows])
                weights = self.p(t, g)[...]
                probs = weights.astype(F32)
                grad_p = nt(stacked, self.v[t, span])
                inner = jnp.sum(probs * grad_p, axis=-1, keepdims=True)
                grad_s = (probs * (grad_p - inner)).astype(BF)
                dq.append((pick_heads(nn(grad_s, self.k[t, span])) * 0.125).astype(BF))
                dk[span] = shifted(tn(grad_s, stack_heads(self.q[t, span])) * 0.125).astype(BF)
                dv[span] = tn(weights, stacked).astype(BF)
            extra = normed_t.shape[1] - self.groups * self.rows
            if extra:
                dq.append(jnp.zeros((extra, 256), BF))
            dq = jnp.concatenate(dq, axis=0)
            grad_normed[...] += (
                nt(dq, block(self.w, t, 0, 256))
                + nt(dk[...], block(self.w, t, 128, 256))
                + nt(dv[...], block(self.w, t, 384, 256))
            )
            for start, low, high in (
                (0, nn(normed_t[...], dq), nn(normed_t[...], dk[...])),
                (384, nn(normed_t[...], dv[...]), nn(branch_t[...], self.o[t])),
            ):
                columns = pl.multiple_of(t * (self.w.shape[1] // 4) + start, 128)
                grad_w[:, pl.ds(columns, 128)] = low[:, :128].astype(BF)
                grad_w[:, pl.ds(columns + 128, 128)] = (low[:, 128:] + high[:, :128]).astype(BF)
                grad_w[:, pl.ds(columns + 256, 128)] = high[:, 128:].astype(BF)
            grad_bias[t, 0:1] = jnp.sum(dq.astype(F32), axis=0, keepdims=True)
            grad_bias[t, 1:2] = jnp.sum(dv[...].astype(F32), axis=0, keepdims=True)
            after(i)
            return carry

        lax.fori_loop(0, 4, body, 0)


SP = 208


def spatial_penalty(places):
    def penalty():
        lane = lax.broadcasted_iota(jnp.int32, (1, SP), 1)
        return jnp.where(lane < places, 0.0, -1e30)
    return penalty


def spatial_forward_kernel(x_ref, w_ref, bias_ref, norm_ref, ob_ref, h_out, q, k, v, o, p, total, normed):
    clips, places, model = x_ref.shape
    for g in range(clips):
        total[pl.ds(g * SP, places)] = x_ref[g].astype(F32)
        total[pl.ds(g * SP + places, SP - places)] = jnp.zeros((SP - places, model), F32)
        span = pl.ds(g * SP, SP)
        unit, _ = normalise(total[span])
        normed[span] = (unit * norm_ref[0:1] + norm_ref[1:2]).astype(BF)
        total[span] += ob_ref[...]
    att = Attention(clips, SP, spatial_penalty(places), w_ref.at[0], bias_ref, q, k, v, o, spatial_probs(p))
    att.forward(normed, total)
    for g in range(clips):
        h_out[g] = total[pl.ds(g * SP, places)].astype(BF)


def spatial_back_kernel(x_ref, g_ref, w_ref, norm_ref, q, k, v, o, p,
                        gx_out, gw, gbias, gvec, total, normed, normed_t, branch, branch_t, dk, dv, gn, rows_in):
    clips, places, model = x_ref.shape
    for g in range(clips):
        for ref, source in ((rows_in, x_ref), (total, g_ref)):
            ref[pl.ds(g * SP, places)] = source[g].astype(F32)
            ref[pl.ds(g * SP + places, SP - places)] = jnp.zeros((SP - places, model), F32)
    attention_back(Attention(clips, SP, None, w_ref.at[0], None, q, k, v, o, spatial_probs(p)),
                   rows_in, total, norm_ref, normed, normed_t, branch, branch_t, dk, dv, gn, gw.at[0], gbias, gvec, 0, lambda i: None)
    for g in range(clips):
        gx_out[g] = total[pl.ds(g * SP, places)].astype(BF)


def attention_back(
    att, rows_in, total, norm, normed, normed_t, branch, branch_t, dk, dv, gn, grad_w, gbias, vec, line, after
):
    round_into(total, branch, vec, line + 2)
    flip_into(branch, branch_t)
    norm_into(rows_in, norm, normed)
    flip_into(normed, normed_t)
    gn[...] = jnp.zeros(gn.shape, F32)
    att.backward(normed_t, branch, branch_t, dk, dv, gn, grad_w, gbias, after)
    norm_back_into(rows_in, norm, gn, total, vec, line)


def by_pair(source, target, mix):
    frames, pairs, model = source.shape
    for f in range(frames):
        values = source[f].astype(F32)
        for i in range(model // 128):
            mix[i, pl.ds(f, pairs, stride=frames)] = values[:, i * 128 : i * 128 + 128]
    for i in range(model // 128):
        target[:, i * 128 : i * 128 + 128] = mix[i]


def by_frame(source, target, mix):
    frames, pairs, model = target.shape
    for i in range(model // 128):
        mix[i] = source[:, i * 128 : i * 128 + 128]
    for f in range(frames):
        for i in range(model // 128):
            target[f, :, i * 128 : i * 128 + 128] = mix[i, pl.ds(f, pairs, stride=frames)].astype(BF)


TG = 5


def temporal_kernel(h_ref, g_ref, w_ref, u_ref, d_ref, bias_ref, norm_ref, norm2_ref, ob_ref, ub_ref, db_ref, pen_ref,
                    y_out, g_out, gw, gu, gd, gbias, gvec, gvec2, gub,
                    q, k, v, o, p, rows_in, total, third, grad, normed, normed_t, branch, branch_t, dk, dv, gn, mix):
    frames, pairs, model = h_ref.shape
    rows = frames * pairs
    by_pair(h_ref, rows_in, mix)
    by_pair(g_ref, grad, mix)
    unit, _ = normalise(rows_in[...])
    normed[...] = (unit * norm_ref[0:1] + norm_ref[1:2]).astype(BF)
    third[...] = rows_in[...] + ob_ref[...]
    group = TG * frames
    att = Attention(pairs // TG, group, lambda: pen_ref[...], w_ref.at[0], bias_ref, q, k, v, o, spatial_probs(p))
    att.forward(normed, third)
    unit, _ = normalise(third[...])
    n2 = unit * norm2_ref[0:1] + norm2_ref[1:2]
    normed[...] = n2.astype(BF)
    normed_t[...] = n2.T.astype(BF)
    branch[...] = grad[...].astype(BF)
    branch_t[...] = grad[...].T.astype(BF)
    gvec2[2:3] = jnp.sum(grad[...], axis=0, keepdims=True)
    total[...] = third[...] + db_ref[...]
    gn[...] = jnp.zeros_like(gn)
    size = 384
    def mlp(j, carry):
        columns = pl.ds(pl.multiple_of(j * size, 128), size)
        up = u_ref[0, :, columns]
        down = d_ref[0, :, columns]
        hidden = nn(normed[...], up) + ub_ref[j]
        half = 0.5 + 0.5 * lax.erf(hidden * (2.0 ** -0.5))
        active = (hidden * half).astype(BF)
        slope = half + hidden * (jnp.exp(-0.5 * hidden * hidden) * ((2.0 * jnp.pi) ** -0.5))
        grad_hidden = nn(branch[...], down) * slope
        rounded = grad_hidden.astype(BF)
        gub[j] = jnp.sum(rounded.astype(F32), axis=0, keepdims=True)
        total[...] += nt(active, down)
        gn[...] += nt(rounded, up)
        gd[0, :, columns] = nn(branch_t[...], active).astype(BF)
        gu[0, :, columns] = nn(normed_t[...], rounded).astype(BF)
        return carry
    lax.fori_loop(0, u_ref.shape[2] // size, mlp, 0)
    by_frame(total, y_out, mix)
    back, gain, shift = norm_back(third[...], norm2_ref[0:1], gn[...])
    grad[...] += back
    gvec2[0:1] = gain
    gvec2[1:2] = shift
    attention_back(att, rows_in, grad, norm_ref, normed, normed_t, branch, branch_t, dk, dv, gn, gw.at[0], gbias, gvec, 0, lambda i: None)
    by_frame(grad, g_out, mix)


def piece_spec(piece, whole):
    return pl.BlockSpec((1,) + whole.shape[1:], lambda i: (piece, 0, 0))


def full_spec(value):
    return pl.BlockSpec(value.shape, lambda i: (0,) * len(value.shape))


def run(kernel, args, specs, outs, scratch, name):
    return pl.pallas_call(
        kernel, grid=(1,),
        out_shape=outs, in_specs=specs, out_specs=[full_spec(out) for out in outs], scratch_shapes=scratch,
        compiler_params=pltpu.CompilerParams(vmem_limit_bytes=63 * 2**20),
        name=name,
    )(*args)


def shape(*size, dtype=BF):
    return jax.ShapeDtypeStruct(size, dtype)


def spatial_forward(x, whole, bias, norm, out_bias):
    clips, places, model = x.shape
    rows = clips * SP
    args = (x, whole, bias, norm, out_bias)
    specs = [full_spec(a) for a in args]
    specs[1] = piece_spec(0, whole)
    outs = [shape(clips, places, model)] + [shape(4, rows, 256)] * 4 + [shape(4, clips, 3 * SP, SP)]
    return run(spatial_forward_kernel, args, specs, outs,
               [pltpu.VMEM((rows, model), F32), pltpu.VMEM((rows, model), BF)], "spatial_forward")


def spatial_back(x, g, whole, norm, kept):
    clips, places, model = x.shape
    rows = clips * SP
    args = (x, g, whole, norm) + tuple(kept)
    specs = [full_spec(a) for a in args]
    specs[2] = piece_spec(0, whole)
    outs = [shape(clips, places, model), shape(1, *whole.shape[1:]), shape(4, 2, 256, dtype=F32), shape(3, model, dtype=F32)]
    scratch = [pltpu.VMEM((rows, model), F32), pltpu.VMEM((rows, model), BF), pltpu.VMEM((model, rows), BF), pltpu.VMEM((rows, model), BF),
               pltpu.VMEM((model, rows), BF), pltpu.VMEM((rows, 256), BF), pltpu.VMEM((rows, 256), BF),
               pltpu.VMEM((rows, model), F32), pltpu.VMEM((rows, model), F32)]
    return run(spatial_back_kernel, args, specs, outs, scratch, "spatial_back")


def temporal(h, g, whole, bias, norm, norm2, out_bias, up_bias, down_bias):
    frames, pairs, model = h.shape
    rows = frames * pairs
    group = TG * frames
    row = jnp.arange(3 * group)[:, None] % group // frames
    column = jnp.arange(group)[None] // frames
    penalty = jnp.where(row == column, 0.0, -1e30).astype(F32)
    args = (h, g, whole, whole, whole, bias, norm, norm2, out_bias, up_bias.reshape(-1, 1, 384), down_bias, penalty)
    specs = [full_spec(a) for a in args]
    for i, piece in ((2, 1), (3, 2), (4, 3)):
        specs[i] = piece_spec(piece, whole)
    hidden = whole.shape[2]
    outs = [shape(frames, pairs, model), shape(frames, pairs, model), shape(1, model, hidden), shape(1, model, hidden),
            shape(1, model, hidden), shape(4, 2, 256, dtype=F32), shape(3, model, dtype=F32), shape(3, model, dtype=F32),
            shape(hidden // 384, 1, 384, dtype=F32)]
    big = pltpu.VMEM((rows, model), F32)
    low = pltpu.VMEM((rows, model), BF)
    flip = pltpu.VMEM((model, rows), BF)
    part = pltpu.VMEM((rows, 256), BF)
    scratch = [pltpu.VMEM((4, rows, 256), BF)] * 4 + [pltpu.VMEM((4, pairs // TG, 3 * group, group), BF)] + [
        big, big, big, big, low, flip, low, flip, part, part, big, pltpu.VMEM((model // 128, rows, 128), F32)]
    return run(temporal_kernel, args, specs, outs, scratch, "temporal_and_mlp")


STEPS = 16


class Refs:
    def __init__(self, names, refs):
        for name, ref in zip(names, refs, strict=True):
            setattr(self, name, ref)


def pair_segments(index, share, clips, places):
    found = []
    for clip in range(clips):
        low = max(index * share, clip * places)
        high = min(index * share + share, clip * places + places)
        if low < high:
            found.append((low - index * share, high - low, clip, low - clip * places))
    return found


class Reduction:
    def __init__(self, r, places, x, y, k, z, rows, width):
        self.r, self.places, self.rows, self.width = r, places, rows, width
        self.x, self.y, self.k, self.z = x, y, k, z
        self.quads = [(f, yy) for f in range(2) for yy in range(2)]
        self.last = 3

    def piece_of(self, s):
        if isinstance(s, int):
            return 2 + s % 2 if s < 8 else 1 if s < 12 else 0
        early, middle = (s < 8).astype(jnp.int32), ((s >= 8) & (s < 12)).astype(jnp.int32)
        return early * (2 + s % 2) + middle

    def tp_of(self, s):
        if isinstance(s, int):
            return 3 * (s // 2 if s < 8 else s) % 4
        early = (s < 8).astype(jnp.int32)
        return (3 * (early * (s // 2) + (1 - early) * s)) % 4

    def spot(self, f, yy, kk, s):
        row = pl.multiple_of((f * 4 + yy * 2 + kk) * self.rows, 16)
        column = pl.multiple_of(self.tp_of(s) * self.width, 128)
        return self.r.w.at[self.piece_of(s), pl.ds(row, self.rows), pl.ds(column, self.width)]

    def remote(self, src, dst, send, recv, side):
        return pltpu.make_async_remote_copy(
            src_ref=src, dst_ref=dst, send_sem=send, recv_sem=recv,
            device_id=self.places[side], device_id_type=MESH,
        )

    def core_copy(self, s, f, yy):
        r = self.r
        return self.remote(
            self.spot(f, yy, 1 - self.k, s), r.r1.at[s, f, yy], r.s1.at[s, f, yy], r.q1s.at[s, f, yy], "core"
        )

    def diag_copy(self, s, side):
        r = self.r
        return self.remote(r.r1.at[s, 1 - self.x, 1 - self.y], r.r2.at[s], r.s2.at[s], r.q2.at[s], side)

    def x_copy(self, s):
        r = self.r
        return self.remote(r.r1.at[s, 1 - self.x, self.y], r.r3x.at[s], r.s3x.at[s], r.q3x.at[s], "x")

    def y_copy(self, s):
        r = self.r
        return self.remote(r.r1.at[s, self.x, 1 - self.y], r.r3y.at[s], r.s3y.at[s], r.q3y.at[s], "y")

    def up_copy(self, s):
        r = self.r
        return self.remote(r.r1.at[s, self.x, self.y], r.rz.at[s], r.sz.at[s], r.qup.at[s], "up")

    def down_copy(self, s, owner=False):
        r = self.r
        target = r.re.at[self.piece_of(s)] if owner else r.rz.at[s]
        return self.remote(r.r1.at[s, self.x, self.y], target, r.sz.at[s], r.qdn.at[s], "down")

    def start(self, s):
        for f, yy in self.quads:
            self.core_copy(s, f, yy).start()

    def even_odd(self, s, even, odd):
        if isinstance(s, int):
            (odd if s % 2 else even)()
        else:
            pl.when(s % 2 == 0)(even)
            pl.when(s % 2 == 1)(odd)

    def chip_sum(self, s):
        r1 = self.r.r1
        for f, yy in self.quads:
            self.core_copy(s, f, yy).wait_recv()
            r1[s, f, yy] = r1[s, f, yy] + self.spot(f, yy, self.k, s)[...]

        def even():
            self.diag_copy(s, "x").start()
            self.x_copy(s).start()

        def odd():
            self.diag_copy(s, "y").start()
            self.y_copy(s).start()

        self.even_odd(s, even, odd)

    def turn(self, s):
        r1, r2, x, y = self.r.r1, self.r.r2, self.x, self.y
        self.diag_copy(s, "x").wait_recv()

        def even():
            r1[s, x, 1 - y] = r1[s, x, 1 - y] + r2[s]
            self.y_copy(s).start()

        def odd():
            r1[s, 1 - x, y] = r1[s, 1 - x, y] + r2[s]
            self.x_copy(s).start()

        self.even_odd(s, even, odd)

    def plane_sum(self, s):
        r = self.r
        self.x_copy(s).wait_recv()
        self.y_copy(s).wait_recv()
        total = r.r1[s, self.x, self.y].astype(F32) + r.r3x[s].astype(F32) + r.r3y[s].astype(F32)
        r.r1[s, self.x, self.y] = total.astype(BF)

    def line(self, s, hop):
        r, x, y, z, last = self.r, self.x, self.y, self.z, self.last
        t = self.tp_of(s)

        @pl.when((z < t) & (z == hop))
        def _():
            if hop > 0:
                self.up_copy(s).wait_recv()
                r.r1[s, x, y] = r.r1[s, x, y] + r.rz[s]
            self.up_copy(s).start()

        @pl.when((z > t) & (last - z == hop))
        def _():
            if hop > 0:
                self.down_copy(s).wait_recv()
                r.r1[s, x, y] = r.r1[s, x, y] + r.rz[s]

            @pl.when(z - 1 == t)
            def _():
                self.down_copy(s, True).start()

            @pl.when(z - 1 != t)
            def _():
                self.down_copy(s).start()

        far = z + (last - 2 * z) * ((last - 2 * z) > 0).astype(jnp.int32)

        @pl.when((z == t) & (far == hop))
        def _():
            piece = self.piece_of(s)
            r.own[piece] = r.r1[s, x, y].astype(F32)

            @pl.when(z > 0)
            def _():
                self.up_copy(s).wait_recv()
                r.own[piece] = r.own[piece] + r.rz[s].astype(F32)

            @pl.when(z < last)
            def _():
                self.down_copy(s, True).wait_recv()
                r.own[piece] = r.own[piece] + r.re[piece].astype(F32)

    def guard(self, action, s, *rest):
        if isinstance(s, int):
            if 0 <= s < STEPS:
                action(s, *rest)
        else:

            @pl.when((s >= 0) & (s < STEPS))
            def _():
                action(s, *rest)

    def tick(self, n):
        self.guard(self.chip_sum, n - 1)
        self.guard(self.turn, n - 2)
        self.guard(self.plane_sum, n - 4)
        for hop in range(4):
            self.guard(self.line, n - 5 - hop, hop)

    def finish(self):
        def body(s, carry):
            for f, yy in self.quads:
                self.core_copy(s, f, yy).wait_send()
            self.diag_copy(s, "x").wait_send()
            self.x_copy(s).wait_send()
            self.y_copy(s).wait_send()

            @pl.when(self.z != self.tp_of(s))
            def _():
                self.up_copy(s).wait_send()

            return carry

        lax.fori_loop(0, STEPS, body, 0)


STAGES = 7
SKEW = 2
X_LAST = (0, 1)


class Gather:
    def __init__(self, r, places, x, y, k, z):
        self.r, self.places, self.x, self.k, self.z = r, places, x, k, z
        self.c = y * 2 + k
        self.rows, self.width = r.shard.shape[1] // 4, r.shard.shape[2]
        self.sends = []
        c, other_y, last = self.c, (1 - y) * 2 + k, 3
        self.stages = [[] for _ in range(STAGES)]

        def wait(stage, unit, when=None):
            self.stages[stage].append(("wait", unit, when))

        def send(stage, side, unit, when=None, mine=False, x_last=None):
            entry = (side, unit, when, mine, x_last, len(self.sends))
            self.sends.append(entry)
            self.stages[stage].append(("send",) + entry)

        me = (x, c, z)
        send(0, "up", me, z < last, True)
        send(0, "down", me, z > 0, True)
        send(0, "x", me, None, True)
        send(0, "x", (x, other_y, z), None, True)
        for d in (1, 2, 3):
            for sign in (-1, 1):
                t = z + sign * d
                have = (t >= 0) if sign < 0 else (t <= last)
                unit = (x, c, t)
                wait(d, unit, have)
                if d < last:
                    if sign < 0:
                        send(d, "up", unit, have & (z < last))
                    else:
                        send(d, "down", unit, have & (z > 0))
                for side in ("x", "y", "core"):
                    send(d, side, unit, have)
            if d == 1:
                wait(1, (1 - x, c, z))
                send(1, "core", (1 - x, c, z))
            if d == 2:
                wait(2, (1 - x, other_y, z))
                send(2, "core", (1 - x, other_y, z))
        for d in (1, 2, 3):
            for sign in (-1, 1):
                t = z + sign * d
                have = (t >= 0) if sign < 0 else (t <= last)
                wait(d + 1, (1 - x, c, t), have)
                send(d + 1, "y", (1 - x, c, t), have, x_last=False)
                send(d + 1, "core", (1 - x, c, t), have)
                wait(d + 1, (x, other_y, t), have)
                send(d + 1, "x", (x, other_y, t), have, x_last=True)
                send(d + 1, "core", (x, other_y, t), have)
                wait(d + 2, (1 - x, other_y, t), have)
                send(d + 2, "core", (1 - x, other_y, t), have)
                for f in (x, 1 - x):
                    for yy in (y, 1 - y):
                        wait(6, (f, yy * 2 + 1 - k, t), have)
        for yy in (y, 1 - y):
            wait(6, (1 - x, yy * 2 + 1 - k, z))

    def spot(self, piece, unit):
        f, cc, t = unit
        row = pl.multiple_of((f * 4 + cc) * self.rows, 16)
        return self.r.w.at[piece, pl.ds(row, self.rows), pl.ds(pl.multiple_of(t * self.width, 128), self.width)]

    def condition(self, piece, when, x_last):
        if x_last is None:
            return when
        by_x = sum((piece == p) * 1 for p in X_LAST) > 0
        return when & (by_x if x_last else jnp.logical_not(by_x))

    def copy(self, piece, entry):
        side, unit, _, mine, _, number = entry
        f, cc, t = unit
        target = self.spot(piece, unit)
        source = self.r.shard.at[piece, pl.ds(pl.multiple_of(cc * self.rows, 16), self.rows)] if mine else target
        return pltpu.make_async_remote_copy(
            src_ref=source, dst_ref=target,
            send_sem=self.r.ws.at[number, piece], recv_sem=self.r.wq.at[(f * 4 + cc) * 4 + t, piece],
            device_id=self.places[side], device_id_type=MESH,
        )

    def own(self, piece):
        row = pl.multiple_of(self.x * self.rows * 4, 16)
        column = pl.multiple_of(self.z * self.width, 128)
        target = self.r.w.at[piece, pl.ds(row, self.rows * 4), pl.ds(column, self.width)]
        return pltpu.make_async_copy(self.r.shard.at[piece], target, self.r.wl.at[piece])

    def put(self, piece):
        return pltpu.make_async_copy(self.r.w.at[piece], self.r.whole.at[piece], self.r.wo.at[piece])

    def arrived(self, piece, unit):
        f, cc, t = unit
        ref = self.spot(piece, unit)
        pltpu.make_async_copy(ref, ref, self.r.wq.at[(f * 4 + cc) * 4 + t, piece]).wait()

    def stage(self, piece, number):
        if number == 0:
            self.own(piece).start()
        for kind, *rest in self.stages[number]:
            if kind == "wait":
                unit, when = rest
                maybe(when, lambda: self.arrived(piece, unit))
            else:
                when = self.condition(piece, rest[2], rest[4])
                maybe(when, lambda: self.copy(piece, rest).start())
        if number == STAGES - 1:
            self.own(piece).wait()
            self.put(piece).start()

    def tick(self, n):
        for number in range(STAGES):
            steps = n - number
            if isinstance(n, int):
                if steps % SKEW == 0 and 0 <= steps // SKEW < PIECES:
                    self.stage(steps // SKEW, number)
            else:
                now = (steps >= 0) & (steps < PIECES * SKEW) & (steps % SKEW == 0)
                maybe(now, lambda: self.stage(steps // SKEW, number))

    def finish(self):
        def body(piece, carry):
            for entry in self.sends:
                when = self.condition(piece, entry[2], entry[4])
                maybe(when, lambda: self.copy(piece, entry).wait_send())
            self.put(piece).wait()
            return carry

        lax.fori_loop(0, PIECES, body, 0)


TICKS = STAGES + SKEW * (PIECES - 1)

FORWARD_NAMES = [
    "shard", "bias", "x_in", "g_in", "norm", "ob", "penalty",
    "whole", "x_out", "q0", "k0", "v0", "o0", "p0", "q1", "k1", "v1", "o1", "p1", "rows_out", "third_out", "grad_out",
    "w", "bias_all", "q", "k", "v", "o", "p", "total", "normed", "rows_in", "third", "grad", "mix",
    "x_recv", "g_send", "g_recv", "h_send", "h_recv",
    "ws", "wq", "wl", "wo", "bs", "bq", "xs", "xq", "cs", "cq", "hs", "hq", "keep",
]


def forward_kernel(*refs):
    r = Refs(FORWARD_NAMES, refs)
    x, c, z = lax.axis_index("fsdp"), lax.axis_index("ctx"), lax.axis_index("tp")
    y, k = c // 2, c % 2
    clips, home_places = r.x_in.shape[0], r.x_in.shape[2]
    model = r.x_in.shape[3]
    places = home_places * 4
    frames, share = r.h_recv.shape[:2]
    rows = frames * share
    me = c * 4 + z
    where = places_of(x, y, k, z)

    barrier = pltpu.get_barrier_semaphore()
    pl.semaphore_signal(barrier, inc=1, device_id=where["x"], device_id_type=MESH)

    def greet(d, carry):
        peer = (me + d) % 16
        pl.semaphore_signal(barrier, inc=1, device_id=(x, peer // 4, peer % 4), device_id_type=MESH)
        return carry

    lax.fori_loop(1, 16, greet, 0)
    pl.semaphore_wait(barrier, 16)

    def remote(src, dst, send, recv, place):
        return pltpu.make_async_remote_copy(
            src_ref=src, dst_ref=dst, send_sem=send, recv_sem=recv, device_id=place, device_id_type=MESH
        )

    gather = Gather(r, where, x, y, k, z)
    early = []
    for d in range(1, 4):
        to = (z + d) % 4
        place = (x, c, to)
        early.append(remote(r.x_in.at[:, to], r.x_recv.at[z], r.xs.at[d], r.xq.at[d], place))
        early.append(remote(r.bias, r.bias_all.at[z], r.bs.at[d], r.bq.at[d], place))
    early.append(pltpu.make_async_copy(r.x_in.at[:, z], r.x_recv.at[z], r.xs.at[0]))
    early.append(pltpu.make_async_copy(r.bias, r.bias_all.at[z], r.bs.at[0]))
    for copy in early:
        copy.start()
    gather.tick(0)

    def share_out(f, carry):
        for clip in range(clips):
            r.third[64 * clip + 64 : 64 * clip + 64 + home_places] = r.g_in[clip, f].astype(F32)
        for to in range(4):
            used = 0
            for start, count, clip, place in pair_segments(to, share, clips, home_places):
                low = 64 * clip + 64 + place
                r.third[start : start + count] = r.third[low : low + count]
                used = start + count
            if used < share:
                r.third[used:share] = jnp.zeros((share - used, model), F32)
            r.g_send[to * 4 + f] = r.third[0:share].astype(BF)
        return carry

    lax.fori_loop(0, 4, share_out, 0)
    gather.tick(1)
    shares = []
    for d in range(1, 4):
        to = (c + d) % 4
        shares.append(
            remote(r.g_send.at[pl.ds(to * 4, 4)], r.g_recv.at[pl.ds(c * 4, 4)], r.cs.at[d], r.cq.at[d], (x, to, z))
        )
    shares.append(
        pltpu.make_async_copy(r.g_send.at[pl.ds(c * 4, 4)], r.g_recv.at[pl.ds(c * 4, 4)], r.cs.at[0])
    )
    for copy in shares:
        copy.start()
    gather.tick(2)

    for copy in early:
        copy.wait()
    keep_x = pltpu.make_async_copy(r.x_recv, r.x_out, r.keep.at[0])
    keep_x.start()
    for clip in range(clips):
        for zz in range(4):
            row = clip * SP + zz * home_places
            r.total[row : row + home_places] = r.x_recv[zz, clip].astype(F32)
        r.total[clip * SP + places : clip * SP + SP] = jnp.zeros((SP - places, model), F32)
    norm_into(r.total, r.norm.at[0], r.normed)
    r.total[...] += r.ob[0:1]
    for n in range(3, STAGES):
        gather.tick(n)
    att = Attention(clips, SP, spatial_penalty(places), r.w.at[0], r.bias_all.at[:, 0], r.q, r.k, r.v, r.o, spatial_probs(r.p))
    att.forward(r.normed, r.total, lambda i: gather.tick(STAGES + i))
    values = (r.q, r.k, r.v, r.o, r.p)
    kept = [
        pltpu.make_async_copy(source, target, r.keep.at[1 + i])
        for i, (source, target) in enumerate(zip(values, (r.q0, r.k0, r.v0, r.o0, r.p0)))
    ]
    for copy in kept:
        copy.start()
    for cc in range(4):
        for zz in range(4):
            used = 0
            for start, count, clip, place in pair_segments(cc, share, clips, home_places):
                row = clip * SP + zz * home_places + place
                r.third[start : start + count] = r.total[row : row + count]
                used = start + count
            if used < share:
                r.third[used:share] = jnp.zeros((share - used, model), F32)
            r.h_send[cc * 4 + zz] = r.third[0:share].astype(BF)

    def to_column(d):
        peer = (me + d) % 16
        return remote(
            r.h_send.at[peer], r.h_recv.at[me], r.hs.at[d], r.hq.at[d], (x, peer // 4, peer % 4)
        )

    def go(d, carry):
        to_column(d).start()
        return carry

    lax.fori_loop(1, 16, go, 0)
    r.h_recv[me] = r.h_send[me]
    for copy in shares:
        copy.wait()
    by_pair(r.g_recv, r.grad, r.mix)
    gather.tick(STAGES + 4)

    def come(d, carry):
        to_column(d).wait()
        return carry

    lax.fori_loop(1, 16, come, 0)

    by_pair(r.h_recv, r.rows_in, r.mix)
    normed = r.normed.at[pl.ds(0, rows)]
    norm_into(r.rows_in, r.norm.at[1], normed)
    r.third[...] = r.rows_in[...] + r.ob[1:2]
    for copy in kept:
        copy.wait()
    group = TG * frames
    att = Attention(
        share // TG, group, lambda: r.penalty[...], r.w.at[1], r.bias_all.at[:, 1],
        *(ref.at[:, pl.ds(0, rows)] for ref in (r.q, r.k, r.v)), r.o, small_probs(r.p, group),
    )
    att.forward(normed, r.third, lambda i: gather.tick(STAGES + 5 + i))
    for n in range(STAGES + 9, TICKS):
        gather.tick(n)
    kept = [
        pltpu.make_async_copy(source, target, r.keep.at[1 + i])
        for i, (source, target) in enumerate(
            zip(
                values + (r.rows_in, r.third, r.grad),
                (r.q1, r.k1, r.v1, r.o1, r.p1, r.rows_out, r.third_out, r.grad_out),
            )
        )
    ]
    for copy in kept:
        copy.start()
    gather.finish()
    for copy in kept:
        copy.wait()
    keep_x.wait()


def whole_penalty(group, frames):
    row = jnp.arange(3 * group)[:, None] % group // frames
    column = jnp.arange(group)[None] // frames
    return jnp.where(row == column, 0.0, -1e30).astype(F32)


def forward(shard, bias, inputs, cotangent, norm, out_bias, frames, share):
    clips, _, home_places, model = inputs.shape
    rows, srows = frames * share, clips * SP
    args = (shard, bias, inputs, cotangent, norm, out_bias, whole_penalty(TG * frames, frames))
    anywhere, vmem = pl.BlockSpec(memory_space=pl.ANY), pl.BlockSpec(memory_space=pltpu.VMEM)
    whole = (PIECES, shard.shape[1] * 2, shard.shape[2] * 4)
    blocks = (4, clips, home_places, model)
    part, probs = (4, srows, 256), (4, clips, 3 * SP, SP)
    attention = [part] * 4 + [probs]
    outs = [shape(*whole), shape(*blocks)] + [shape(*size) for size in attention * 2]
    outs += [shape(rows, model, dtype=F32)] * 3
    dma = pltpu.SemaphoreType.DMA
    sends = 58
    scratch = (
        [pltpu.VMEM(whole, BF), pltpu.VMEM((4,) + bias.shape, F32)]
        + [pltpu.VMEM(size, BF) for size in attention]
        + [pltpu.VMEM((srows, model), F32), pltpu.VMEM((srows, model), BF)]
        + [pltpu.VMEM((rows, model), F32)] * 3
        + [pltpu.VMEM((model // 128, rows, 128), F32), pltpu.VMEM(blocks, BF)]
        + [pltpu.VMEM((frames, share, model), BF)] * 4
        + [dma((sends, PIECES)), dma((32, PIECES)), dma((PIECES,)), dma((PIECES,))]
        + [dma((4,))] * 6
        + [dma((16,))] * 2
        + [dma((9,))]
    )
    return pl.pallas_call(
        forward_kernel,
        out_shape=outs,
        in_specs=[vmem, vmem, anywhere, vmem, vmem, vmem, vmem],
        out_specs=[anywhere] * len(outs),
        scratch_shapes=scratch,
        compiler_params=pltpu.CompilerParams(
            collective_id=0, has_side_effects=True, vmem_limit_bytes=67043328
        ),
        name="forward",
    )(*args)


BACK_NAMES = [
    "x", "rows_from", "third_from", "grad_from", "whole", "q1", "k1", "v1", "o1", "p1", "q0", "k0", "v0", "o0", "p0",
    "norm", "ub", "db", "y_home", "g_home", "own", "vectors", "w", "q", "k", "v", "o", "p", "rows_in", "total",
    "third", "grad", "gn", "mix", "normed", "normed_t", "branch", "branch_t", "dk", "dv", "y_send",
    "g_send", "g_recv", "home_send", "bias1", "bias0", "ups", "r1", "r2", "r3x", "r3y", "rz", "re", "va",
    "vr", "load", "s1", "q1s", "s2", "q2", "s3x", "s3y", "q3x", "q3y", "sz", "qup", "qdn", "vs", "vq", "ys",
    "yq", "gs", "gq", "hs", "hq", "keep", "early",
]


def back_kernel(*refs):
    r = Refs(BACK_NAMES, refs)
    x, c, z = lax.axis_index("fsdp"), lax.axis_index("ctx"), lax.axis_index("tp")
    y, k = c // 2, c % 2
    _, clips, home_places, model = r.x.shape
    frames, share = r.y_send.shape[:2]
    rows = frames * share
    places = home_places * 4
    me = c * 4 + z
    where = places_of(x, y, k, z)

    barrier = pltpu.get_barrier_semaphore()
    pl.semaphore_signal(barrier, inc=1, device_id=where["x"], device_id_type=MESH)

    def greet(d, carry):
        peer = (me + d) % 16
        pl.semaphore_signal(barrier, inc=1, device_id=(x, peer // 4, peer % 4), device_id_type=MESH)
        return carry

    lax.fori_loop(1, 16, greet, 0)

    loads = [pltpu.make_async_copy(r.whole.at[i], r.w.at[i], r.load.at[i]) for i in range(4)]
    frames_in = r.rows_in.at[pl.ds(0, rows)]
    values = (r.q, r.k, r.v, r.o, r.p)
    early = [
        pltpu.make_async_copy(source, target, r.early.at[i])
        for i, (source, target) in enumerate(
            zip(
                (r.third_from, r.grad_from, r.rows_from, r.q1, r.k1, r.v1, r.o1, r.p1),
                (r.third, r.grad, frames_in) + values,
            )
        )
    ]
    kept = [
        pltpu.make_async_copy(source, target, r.keep.at[i])
        for i, (source, target) in enumerate(zip((r.q0, r.k0, r.v0, r.o0, r.p0), values))
    ]
    for copy in early[:2] + loads[2:] + early[2:] + loads[:2]:
        copy.start()
    spare = r.normed.shape[0] - rows
    for ref in (r.normed, r.branch, r.dk, r.dv):
        ref[rows:] = jnp.zeros((spare, ref.shape[1]), BF)
    r.total[rows:] = jnp.zeros((spare, model), F32)
    early[0].wait()
    early[1].wait()

    norm_into(r.third, r.norm.at[2], r.normed)
    flip_into(r.normed, r.normed_t)
    va = r.va.at[0]
    round_into(r.grad, r.branch, va, 8)
    flip_into(r.branch, r.branch_t)
    r.total[0:rows] = r.third[...] + r.db[...]
    r.gn[...] = jnp.zeros(r.gn.shape, F32)
    loads[2].wait()
    loads[3].wait()
    pl.semaphore_wait(barrier, 16)
    red = Reduction(r, where, x, y, k, z, r.own.shape[1], r.own.shape[2])
    size = r.ub.shape[2]
    halves = r.own.shape[2] // size

    def mlp(i, carry):
        t = (3 * i) % 4
        for half in range(halves):
            j = t * halves + half
            columns = pl.ds(pl.multiple_of(j * size, 128), size)
            up = r.w[2, :, columns]
            down = r.w[3, :, columns]
            hidden = nn(r.normed[...], up) + r.ub[j]
            cdf = 0.5 + 0.5 * lax.erf(hidden * (2.0**-0.5))
            active = (hidden * cdf).astype(BF)
            slope = cdf + hidden * (jnp.exp(-0.5 * hidden * hidden) * ((2.0 * jnp.pi) ** -0.5))
            rounded = (nn(r.branch[...], down) * slope).astype(BF)
            r.ups[j] = jnp.sum(rounded.astype(F32), axis=0, keepdims=True)
            r.total[...] += nt(active, down)
            r.gn[...] += nt(rounded, up)
            r.w[3, :, columns] = nn(r.branch_t[...], active).astype(BF)
            r.w[2, :, columns] = nn(r.normed_t[...], rounded).astype(BF)
        for s in (2 * i, 2 * i + 1):
            red.start(s)
        for s in (2 * i, 2 * i + 1):
            red.tick(s)
        return carry

    lax.fori_loop(0, 4, mlp, 0)

    by_frame(r.total.at[pl.ds(0, rows)], r.y_send, r.mix)
    outs = []
    for d in range(1, 4):
        peer = (c + d) % 4
        copy = pltpu.make_async_remote_copy(
            src_ref=r.y_send.at[pl.ds(peer * 4, 4)], dst_ref=r.y_home.at[c],
            send_sem=r.ys.at[d], recv_sem=r.yq.at[d], device_id=(x, peer, z), device_id_type=MESH,
        )
        copy.start()
        outs.append(copy)
    y_own = pltpu.make_async_copy(r.y_send.at[pl.ds(c * 4, 4)], r.y_home.at[c], r.ys.at[0])
    y_own.start()

    norm_back_into(r.third, r.norm.at[2], r.gn, r.grad, va, 6)
    for copy in early[2:]:
        copy.wait()
    loads[1].wait()
    for t in range(4):
        r.o[t, rows:] = jnp.zeros((spare, r.o.shape[2]), BF)
    group = TG * frames
    att = Attention(
        share // TG, group, None, r.w.at[1], None,
        *(ref.at[:, pl.ds(0, rows)] for ref in (r.q, r.k, r.v)), r.o, small_probs(r.p, group),
    )

    def each(first):
        def after(i):
            red.start(first + i)
            maybe(i > 0 if first == 12 else None, lambda: red.tick(first + i))

        return after

    attention_back(
        att, frames_in, r.grad, r.norm.at[1], r.normed, r.normed_t, r.branch, r.branch_t,
        r.dk, r.dv, r.gn, r.w.at[1], r.bias1, va, 3, each(8),
    )
    for copy in kept:
        copy.start()
    by_frame(r.grad, r.g_send, r.mix)

    def to_frame(d):
        peer = (me + d) % 16
        return pltpu.make_async_remote_copy(
            src_ref=r.g_send.at[peer], dst_ref=r.g_recv.at[me],
            send_sem=r.gs.at[d], recv_sem=r.gq.at[d], device_id=(x, peer // 4, peer % 4), device_id_type=MESH,
        )

    def go(d, carry):
        to_frame(d).start()
        return carry

    lax.fori_loop(1, 16, go, 0)
    r.g_recv[me] = r.g_send[me]
    red.tick(12)
    for copy in kept:
        copy.wait()
    loads[0].wait()
    srows = clips * SP
    for clip in range(clips):
        for zz in range(4):
            row = clip * SP + zz * home_places
            r.rows_in[row : row + home_places] = r.x[zz, clip].astype(F32)
        r.rows_in[pl.ds(clip * SP + places, SP - places)] = jnp.zeros((SP - places, model), F32)
        r.total[pl.ds(clip * SP + places, SP - places)] = jnp.zeros((SP - places, model), F32)

    def come(d, carry):
        to_frame(d).wait()
        return carry

    lax.fori_loop(1, 16, come, 0)
    for cc in range(4):
        for zz in range(4):
            r.third[0:share] = r.g_recv[cc * 4 + zz].astype(F32)
            for start, count, clip, place in pair_segments(cc, share, clips, home_places):
                row = clip * SP + zz * home_places + place
                r.total[row : row + count] = r.third[start : start + count]

    att = Attention(clips, SP, None, r.w.at[0], None, r.q, r.k, r.v, r.o, spatial_probs(r.p))
    attention_back(
        att, r.rows_in, r.total, r.norm.at[0], r.normed, r.normed_t, r.branch, r.branch_t, r.dk, r.dv, r.gn,
        r.w.at[0], r.bias0, va, 0, each(12),
    )
    for zz in range(4):
        for clip in range(clips):
            row = clip * SP + zz * home_places
            r.third[0:home_places] = r.total[row : row + home_places]
            r.home_send[zz, clip] = r.third[0:home_places].astype(BF)
    for d in range(1, 4):
        peer = (z + d) % 4
        copy = pltpu.make_async_remote_copy(
            src_ref=r.home_send.at[peer], dst_ref=r.g_home.at[z],
            send_sem=r.hs.at[d], recv_sem=r.hq.at[d], device_id=(x, c, peer), device_id_type=MESH,
        )
        copy.start()
        outs.append(copy)
    g_own = pltpu.make_async_copy(r.home_send.at[z], r.g_home.at[z], r.hs.at[0])
    g_own.start()

    for j in range(r.ups.shape[0]):
        va[9 + j // halves : 10 + j // halves, (j % halves) * size : (j % halves + 1) * size] = r.ups[j]
    for i, ref in enumerate((r.bias0, r.bias1)):
        for t in range(4):
            va[16 + i * 8 + t * 2 : 18 + i * 8 + t * 2, 0:256] = ref[t]
    sides = ("core", "x", "y", "z1", "z2")

    def v_copy(j):
        return red.remote(r.va.at[j], r.vr.at[j], r.vs.at[j], r.vq.at[j], sides[j])

    v_copy(0).start()
    for n in range(16, STEPS + 8):
        red.tick(n)
        j = n - 16
        if j < 5:
            v_copy(j).wait()
            if j < 4:
                r.va[j + 1] = r.va[j] + r.vr[j]
                v_copy(j + 1).start()
            else:
                r.vectors[...] = r.va[j] + r.vr[j]
    red.finish()
    for copy in outs:
        copy.wait()
    y_own.wait()
    g_own.wait()


def backward(x, rows_in, third, grad, whole, kept, norm, up_bias, down_bias, own_rows, width, frames):
    _, clips, home_places, model = x.shape
    rows, srows = third.shape[0], clips * SP
    places, share = home_places * 4, rows // frames
    size = 384
    anywhere, vmem = pl.BlockSpec(memory_space=pl.ANY), pl.BlockSpec(memory_space=pltpu.VMEM)
    args = (x, rows_in, third, grad, whole, *kept, norm, up_bias.reshape(-1, 1, size), down_bias)
    in_specs = [vmem] + [anywhere] * 14 + [vmem] * 3
    sub = (own_rows, width)
    big = max(rows, srows)

    def v(*dims, dtype=BF):
        return pltpu.VMEM(dims, dtype)

    def f(*dims):
        return pltpu.VMEM(dims, F32)

    dma = pltpu.SemaphoreType.DMA
    scratch = (
        [v(*whole.shape)]
        + [v(4, big, 256)] * 4
        + [v(4, clips, 3 * SP, SP)]
        + [f(big, model), f(big, model), f(rows, model), f(rows, model), f(big, model)]
        + [f(model // 128, rows, 128)]
        + [v(big, model), v(model, big), v(big, model), v(model, big), v(big, 256), v(big, 256)]
        + [v(frames, share, model), v(frames, share, model), v(frames, share, model)]
        + [v(4, clips, places // 4, model), f(4, 2, 256), f(4, 2, 256), f(up_bias.shape[0] // size, 1, size)]
        + [v(STEPS, 2, 2, *sub)]
        + [v(STEPS, *sub)] * 4
        + [v(PIECES, *sub)]
        + [f(5, 32, model)] * 2
        + [dma((4,))]
        + [dma((STEPS, 2, 2))] * 2
        + [dma((STEPS,))] * 9
        + [dma((5,))] * 2
        + [dma((4,))] * 2
        + [dma((16,))] * 2
        + [dma((4,))] * 2
        + [dma((5,))]
        + [dma((8,))]
    )
    return pl.pallas_call(
        back_kernel,
        out_shape=(
            shape(4, frames // 4, share, model),
            shape(4, clips, places // 4, model),
            shape(PIECES, *sub, dtype=F32),
            shape(32, model, dtype=F32),
        ),
        in_specs=in_specs,
        out_specs=[anywhere, anywhere, vmem, vmem],
        scratch_shapes=scratch,
        compiler_params=pltpu.CompilerParams(
            collective_id=2, has_side_effects=True, vmem_limit_bytes=67043328
        ),
        name="backward",
    )(*args)


def local(
    inputs,
    cotangent,
    norm_gain,
    norm_bias,
    attn_weight,
    attn_bias,
    out_weight,
    out_bias,
    up_weight,
    up_bias,
    down_weight,
    down_bias,
):
    ranks_c = lax.axis_size("ctx")
    tp_rank = lax.axis_index("tp")
    clips, frames, places, model = inputs.shape
    width = attn_weight.shape[3]

    shard = jnp.concatenate(
        [
            jnp.concatenate(
                [
                    attn_weight.transpose(0, 2, 1, 3).reshape(2, attn_weight.shape[2], 3 * width),
                    out_weight.transpose(0, 2, 1),
                ],
                axis=2,
            ),
            up_weight[None],
            down_weight.T[None],
        ]
    )
    norm = jnp.stack([norm_gain, norm_bias], axis=1)

    pairs = clips * places
    share = -(-pairs // ranks_c)
    share += -share % TG

    def home_to_spatial(values):
        return lax.all_to_all(values, "tp", split_axis=1, concat_axis=2, tiled=True)

    def spatial_to_home(values):
        return lax.all_to_all(values, "tp", split_axis=2, concat_axis=1, tiled=True)

    def home_to_temporal(values):
        rows = values.transpose(1, 0, 2, 3).reshape(frames, pairs, model)
        rows = jnp.pad(rows, ((0, 0), (0, share * ranks_c - pairs), (0, 0)))
        return lax.all_to_all(rows, "ctx", split_axis=1, concat_axis=0, tiled=True)

    def temporal_to_home(values):
        rows = lax.all_to_all(values, "ctx", split_axis=0, concat_axis=1, tiled=True)[:, :pairs]
        return rows.reshape(frames, clips, places, model).transpose(1, 0, 2, 3)

    ups = up_bias.shape[0] // model
    bias = jnp.pad(attn_bias, ((0, 0), (0, 6), (0, 256 - width)))
    if lax.axis_size("fsdp") == 2 and (ranks_c, lax.axis_size("tp")) == (4, 4):
        frames *= ranks_c
        whole, first, *kept = forward(shard, bias, inputs, cotangent, norm, out_bias, frames, share)
        kept, rows = kept[5:10] + kept[:5], kept[10:]
        home, grad_home, own, vectors = backward(
            first, *rows, whole, kept, norm, up_bias, down_bias[None], attn_weight.shape[2] // 4, up_weight.shape[1], frames
        )
        frames //= ranks_c
        outputs = home.transpose(1, 0, 2, 3).reshape(frames, -1, model)[:, :pairs]
        outputs = outputs.reshape(frames, clips, places, model).transpose(1, 0, 2, 3)
        input_grad = grad_home.transpose(1, 0, 2, 3)
        sums = vectors[16:, :256].reshape(2, 4, 2, 256)[..., :width].transpose(0, 2, 1, 3)
        attn_bias_sums = sums.reshape(2, 2, model)
    else:
        whole, bias = gather(shard, bias)
        bias = bias[:, :, :2].transpose(1, 0, 2, 3)
        first = home_to_spatial(inputs)
        spatial_shape = first.shape
        first = first.reshape((-1,) + first.shape[2:])
        second, *kept = spatial_forward(first, whole, bias[0], norm[0], out_bias[0:1])
        second = home_to_temporal(spatial_to_home(second.reshape(spatial_shape)))
        grad_out = home_to_temporal(cotangent)
        result, grad_second, grad_attn1, grad_up, grad_down, bias1, vec1, vec2, grad_up_bias = temporal(
            second, grad_out, whole, bias[1], norm[1], norm[2], out_bias[1:2], up_bias, down_bias[None]
        )
        outputs = temporal_to_home(result)
        grad_second = home_to_spatial(temporal_to_home(grad_second)).reshape(first.shape)
        grad_first, grad_attn0, bias0, vec0 = spatial_back(first, grad_second, whole, norm[0], kept)
        input_grad = spatial_to_home(grad_first.reshape(spatial_shape))
        bias_sums = jnp.stack([bias0, bias1])[..., :width].transpose(0, 2, 1, 3)
        lines = [vec0, vec1, vec2, grad_up_bias, bias_sums]
        flat = jnp.concatenate([line.reshape(-1, model) for line in lines])
        vectors = jnp.pad(flat, ((0, -flat.shape[0] % 8), (0, 0)))
        own, vectors = scatter([grad_attn0, grad_attn1, grad_up, grad_down], vectors)
        attn_bias_sums = vectors[9 + ups : 13 + ups].reshape(2, 2, model)
    triples = vectors[:9].reshape(3, 3, model)
    attn = own[:2].reshape(2, own.shape[1], 4, width)
    return (
        outputs,
        input_grad,
        triples[:, 0],
        triples[:, 1],
        attn[:, :, :3].transpose(0, 2, 1, 3),
        lax.dynamic_slice_in_dim(attn_bias_sums, tp_rank * width, width, 2),
        attn[:, :, 3].transpose(0, 2, 1),
        triples[:2, 2],
        own[2],
        vectors[9 : 9 + ups].reshape(-1),
        own[3].T,
        triples[2, 2],
    )


def solution(mesh):
    return jax.shard_map(
        local,
        mesh=mesh,
        in_specs=(
            P("fsdp", "ctx", "tp", None),
            P("fsdp", "ctx", "tp", None),
            P(),
            P(),
            P(None, None, "fsdp", "tp"),
            P(None, None, "tp"),
            P(None, "tp", "fsdp"),
            P(),
            P("fsdp", "tp"),
            P(),
            P("tp", "fsdp"),
            P(),
        ),
        out_specs=(
            P("fsdp", "ctx", "tp", None),
            P("fsdp", "ctx", "tp", None),
            P(),
            P(),
            P(None, None, ("fsdp", "ctx"), "tp"),
            P(None, None, "tp"),
            P(None, "tp", ("fsdp", "ctx")),
            P(),
            P(("fsdp", "ctx"), "tp"),
            P(),
            P("tp", ("fsdp", "ctx")),
            P(),
        ),
        check_vma=False,
    )
```

```python
import jax
import jax.numpy as jnp
from jax import lax
from jax.experimental import pallas as pl
from jax.experimental.pallas import tpu as pltpu
from jax.sharding import PartitionSpec as P

HEAD = 64
EPSILON = 1e-06
BF = jnp.bfloat16
F32 = jnp.float32
MESH = pl.DeviceIdType.MESH
PIECES = 4
ALL = ("fsdp", "ctx", "tp")


def places_of(x, y, k, z):
    return {
        "x": (1 - x, y * 2 + k, z),
        "y": (x, (1 - y) * 2 + k, z),
        "core": (x, y * 2 + 1 - k, z),
        "up": (x, y * 2 + k, z + 1),
        "down": (x, y * 2 + k, z - 1),
        "z1": (x, y * 2 + k, (z // 2) * 2 + 1 - z % 2),
        "z2": (x, y * 2 + k, (z + 2) % 4),
    }


def maybe(when, action):
    if when is None:
        action()
    else:
        pl.when(when)(action)


def gather(shard, bias):
    part = shard.shape[1] // lax.axis_size("ctx")
    mine = lax.dynamic_slice_in_dim(shard, lax.axis_index("ctx") * part, part, 1)
    tall = lax.all_gather(mine, ("fsdp", "ctx"), axis=1, tiled=True)
    return lax.all_gather(tall, "tp", axis=2, tiled=True), lax.all_gather(bias, "tp")


def scatter(grads, vectors):
    tall = lax.psum_scatter(jnp.concatenate(grads), ("fsdp", "ctx"), scatter_dimension=1, tiled=True)
    own = lax.psum_scatter(tall, "tp", scatter_dimension=2, tiled=True)
    return own.astype(F32), lax.psum(vectors, ALL)


def nn(a, b):
    return lax.dot_general(a, b, (((1,), (0,)), ((), ())), preferred_element_type=F32)


def nt(a, b):
    return lax.dot_general(a, b, (((1,), (1,)), ((), ())), preferred_element_type=F32)


def tn(a, b):
    return lax.dot_general(a, b, (((0,), (0,)), ((), ())), preferred_element_type=F32)


def normalise(rows):
    centre = rows - jnp.mean(rows, axis=-1, keepdims=True)
    scale = lax.rsqrt(jnp.mean(centre * centre, axis=-1, keepdims=True) + EPSILON)
    return centre * scale, scale


def chunks(count):
    size = 80 if count % 80 == 0 else 208
    return size, count // size


def norm_into(source, norm, target):
    size, number = chunks(source.shape[0])

    def body(i, carry):
        span = pl.ds(pl.multiple_of(i * size, 16), size)
        unit, _ = normalise(source[span])
        target[span] = (unit * norm[0:1] + norm[1:2]).astype(BF)
        return carry

    lax.fori_loop(0, number, body, 0)


def norm_back_into(source, norm, grad, total, vec, line):
    size, number = chunks(source.shape[0])
    vec[line : line + 2] = jnp.zeros((2, source.shape[1]), F32)

    def body(i, carry):
        span = pl.ds(pl.multiple_of(i * size, 16), size)
        back, gain, shift = norm_back(source[span], norm[0:1], grad[span])
        total[span] += back
        vec[line : line + 1] += gain
        vec[line + 1 : line + 2] += shift
        return carry

    lax.fori_loop(0, number, body, 0)


def round_into(source, target, vec, line):
    size, number = chunks(source.shape[0])
    vec[line : line + 1] = jnp.zeros((1, source.shape[1]), F32)

    def body(i, carry):
        span = pl.ds(pl.multiple_of(i * size, 16), size)
        rounded = source[span].astype(BF)
        target[span] = rounded
        vec[line : line + 1] += jnp.sum(rounded.astype(F32), axis=0, keepdims=True)
        return carry

    lax.fori_loop(0, number, body, 0)


def flip_into(source, target):
    rows = source.shape[0]
    for low in range(0, rows, 128):
        high = min(rows, low + 128)
        target[:, low:high] = source[low:high].T


def norm_back(rows, gain, grad):
    unit, scale = normalise(rows)
    inner = grad * gain
    mean = jnp.mean(inner, axis=-1, keepdims=True)
    along = jnp.mean(inner * unit, axis=-1, keepdims=True)
    return scale * (inner - mean - unit * along), jnp.sum(grad * unit, axis=0, keepdims=True), jnp.sum(
        grad, axis=0, keepdims=True
    )


def lanes_in(low, high):
    lane = lax.broadcasted_iota(jnp.int32, (1, 256), 1)
    return jnp.where((lane >= low) & (lane < high), 1.0, 0.0)


def stack_heads(values):
    return jnp.concatenate(
        [values * lanes_in(i * HEAD, i * HEAD + HEAD).astype(BF) for i in range(3)], axis=0
    )


def pick_heads(stacked):
    rows = stacked.shape[0] // 3
    return sum(
        stacked[i * rows : (i + 1) * rows] * lanes_in(i * HEAD, i * HEAD + HEAD) for i in range(3)
    )


def shifted(values):
    return pltpu.roll(values, 64, axis=1)


def unshifted(values):
    return pltpu.roll(values, 192, axis=1)


def block(w_ref, t, start, size):
    return w_ref[:, pl.ds(pl.multiple_of(t * (w_ref.shape[1] // 4) + start, 128), size)]


def spatial_probs(ref):
    return lambda t, g: ref.at[t, g]


def small_probs(ref, size):
    def find(t, g):
        row, lane = ((g % 2) * 3 * size, 0) if g < 4 else (0, 128)
        return ref.at[t, g // 2 % 2, pl.ds(row, 3 * size), pl.ds(lane, size)]

    return find


class Attention:
    def __init__(self, groups, rows, penalty, w, bias, q, k, v, o, p):
        self.groups, self.rows, self.penalty = groups, rows, penalty
        self.w, self.bias, self.q, self.k, self.v, self.o, self.p = w, bias, q, k, v, o, p

    def spans(self):
        return [(g, pl.ds(g * self.rows, self.rows)) for g in range(self.groups)]

    def forward(self, normed, total, after=lambda i: None):
        used = lanes_in(0, 192)

        def body(t, carry):
            mixed = nn(normed[...], block(self.w, t, 0, 640))
            self.q[t] = ((mixed[:, :256] + self.bias[t, 0:1]) * used).astype(BF)
            self.k[t] = (unshifted(mixed[:, 128:384]) * used).astype(BF)
            self.v[t] = ((mixed[:, 384:] + self.bias[t, 1:2]) * used).astype(BF)
            for g, span in self.spans():
                scores = nt(stack_heads(self.q[t, span]), self.k[t, span]) * 0.125 + self.penalty()
                weights = jnp.exp(scores - jnp.max(scores, axis=-1, keepdims=True))
                weights = weights * (1.0 / jnp.sum(weights, axis=-1, keepdims=True))
                weights = weights.astype(BF)
                self.p(t, g)[...] = weights
                out = pick_heads(nn(weights, self.v[t, span]))
                self.o[t, span] = shifted(out).astype(BF)
            total[...] += nt(self.o[t, pl.ds(0, self.groups * self.rows)], block(self.w, t, 512, 256))
            after(t)
            return carry

        lax.fori_loop(0, 4, body, 0)

    def backward(self, normed_t, branch, branch_t, dk, dv, grad_normed, grad_w, grad_bias, after):
        used = lanes_in(0, 192)

        def body(i, carry):
            t = (3 * i) % 4
            grad_o = (unshifted(nn(branch[...], block(self.w, t, 512, 256))) * used).astype(BF)
            dq = []
            for g, span in self.spans():
                stacked = stack_heads(grad_o[g * self.rows : (g + 1) * self.rows])
                weights = self.p(t, g)[...]
                probs = weights.astype(F32)
                grad_p = nt(stacked, self.v[t, span])
                inner = jnp.sum(probs * grad_p, axis=-1, keepdims=True)
                grad_s = (probs * (grad_p - inner)).astype(BF)
                dq.append((pick_heads(nn(grad_s, self.k[t, span])) * 0.125).astype(BF))
                dk[span] = shifted(tn(grad_s, stack_heads(self.q[t, span])) * 0.125).astype(BF)
                dv[span] = tn(weights, stacked).astype(BF)
            extra = normed_t.shape[1] - self.groups * self.rows
            if extra:
                dq.append(jnp.zeros((extra, 256), BF))
            dq = jnp.concatenate(dq, axis=0)
            grad_normed[...] += (
                nt(dq, block(self.w, t, 0, 256))
                + nt(dk[...], block(self.w, t, 128, 256))
                + nt(dv[...], block(self.w, t, 384, 256))
            )
            for start, low, high in (
                (0, nn(normed_t[...], dq), nn(normed_t[...], dk[...])),
                (384, nn(normed_t[...], dv[...]), nn(branch_t[...], self.o[t])),
            ):
                columns = pl.multiple_of(t * (self.w.shape[1] // 4) + start, 128)
                grad_w[:, pl.ds(columns, 128)] = low[:, :128].astype(BF)
                grad_w[:, pl.ds(columns + 128, 128)] = (low[:, 128:] + high[:, :128]).astype(BF)
                grad_w[:, pl.ds(columns + 256, 128)] = high[:, 128:].astype(BF)
            grad_bias[t, 0:1] = jnp.sum(dq.astype(F32), axis=0, keepdims=True)
            grad_bias[t, 1:2] = jnp.sum(dv[...].astype(F32), axis=0, keepdims=True)
            after(i)
            return carry

        lax.fori_loop(0, 4, body, 0)


SP = 208


def spatial_penalty(places):
    def penalty():
        lane = lax.broadcasted_iota(jnp.int32, (1, SP), 1)
        return jnp.where(lane < places, 0.0, -1e30)
    return penalty


def spatial_forward_kernel(x_ref, w_ref, bias_ref, norm_ref, ob_ref, h_out, q, k, v, o, p, total, normed):
    clips, places, model = x_ref.shape
    for g in range(clips):
        total[pl.ds(g * SP, places)] = x_ref[g].astype(F32)
        total[pl.ds(g * SP + places, SP - places)] = jnp.zeros((SP - places, model), F32)
        span = pl.ds(g * SP, SP)
        unit, _ = normalise(total[span])
        normed[span] = (unit * norm_ref[0:1] + norm_ref[1:2]).astype(BF)
        total[span] += ob_ref[...]
    att = Attention(clips, SP, spatial_penalty(places), w_ref.at[0], bias_ref, q, k, v, o, spatial_probs(p))
    att.forward(normed, total)
    for g in range(clips):
        h_out[g] = total[pl.ds(g * SP, places)].astype(BF)


def spatial_back_kernel(x_ref, g_ref, w_ref, norm_ref, q, k, v, o, p,
                        gx_out, gw, gbias, gvec, total, normed, normed_t, branch, branch_t, dk, dv, gn, rows_in):
    clips, places, model = x_ref.shape
    for g in range(clips):
        for ref, source in ((rows_in, x_ref), (total, g_ref)):
            ref[pl.ds(g * SP, places)] = source[g].astype(F32)
            ref[pl.ds(g * SP + places, SP - places)] = jnp.zeros((SP - places, model), F32)
    attention_back(Attention(clips, SP, None, w_ref.at[0], None, q, k, v, o, spatial_probs(p)),
                   rows_in, total, norm_ref, normed, normed_t, branch, branch_t, dk, dv, gn, gw.at[0], gbias, gvec, 0, lambda i: None)
    for g in range(clips):
        gx_out[g] = total[pl.ds(g * SP, places)].astype(BF)


def attention_back(
    att, rows_in, total, norm, normed, normed_t, branch, branch_t, dk, dv, gn, grad_w, gbias, vec, line, after
):
    round_into(total, branch, vec, line + 2)
    flip_into(branch, branch_t)
    norm_into(rows_in, norm, normed)
    flip_into(normed, normed_t)
    gn[...] = jnp.zeros(gn.shape, F32)
    att.backward(normed_t, branch, branch_t, dk, dv, gn, grad_w, gbias, after)
    norm_back_into(rows_in, norm, gn, total, vec, line)


def by_pair(source, target, mix):
    frames, pairs, model = source.shape
    for f in range(frames):
        values = source[f].astype(F32)
        for i in range(model // 128):
            mix[i, pl.ds(f, pairs, stride=frames)] = values[:, i * 128 : i * 128 + 128]
    for i in range(model // 128):
        target[:, i * 128 : i * 128 + 128] = mix[i]


def by_frame(source, target, mix):
    frames, pairs, model = target.shape
    for i in range(model // 128):
        mix[i] = source[:, i * 128 : i * 128 + 128]
    for f in range(frames):
        for i in range(model // 128):
            target[f, :, i * 128 : i * 128 + 128] = mix[i, pl.ds(f, pairs, stride=frames)].astype(BF)


TG = 5


def temporal_kernel(h_ref, g_ref, w_ref, u_ref, d_ref, bias_ref, norm_ref, norm2_ref, ob_ref, ub_ref, db_ref, pen_ref,
                    y_out, g_out, gw, gu, gd, gbias, gvec, gvec2, gub,
                    q, k, v, o, p, rows_in, total, third, grad, normed, normed_t, branch, branch_t, dk, dv, gn, mix):
    frames, pairs, model = h_ref.shape
    rows = frames * pairs
    by_pair(h_ref, rows_in, mix)
    by_pair(g_ref, grad, mix)
    unit, _ = normalise(rows_in[...])
    normed[...] = (unit * norm_ref[0:1] + norm_ref[1:2]).astype(BF)
    third[...] = rows_in[...] + ob_ref[...]
    group = TG * frames
    att = Attention(pairs // TG, group, lambda: pen_ref[...], w_ref.at[0], bias_ref, q, k, v, o, spatial_probs(p))
    att.forward(normed, third)
    unit, _ = normalise(third[...])
    n2 = unit * norm2_ref[0:1] + norm2_ref[1:2]
    normed[...] = n2.astype(BF)
    normed_t[...] = n2.T.astype(BF)
    branch[...] = grad[...].astype(BF)
    branch_t[...] = grad[...].T.astype(BF)
    gvec2[2:3] = jnp.sum(grad[...], axis=0, keepdims=True)
    total[...] = third[...] + db_ref[...]
    gn[...] = jnp.zeros_like(gn)
    size = 384
    def mlp(j, carry):
        columns = pl.ds(pl.multiple_of(j * size, 128), size)
        up = u_ref[0, :, columns]
        down = d_ref[0, :, columns]
        hidden = nn(normed[...], up) + ub_ref[j]
        half = 0.5 + 0.5 * lax.erf(hidden * (2.0 ** -0.5))
        active = (hidden * half).astype(BF)
        slope = half + hidden * (jnp.exp(-0.5 * hidden * hidden) * ((2.0 * jnp.pi) ** -0.5))
        grad_hidden = nn(branch[...], down) * slope
        rounded = grad_hidden.astype(BF)
        gub[j] = jnp.sum(rounded.astype(F32), axis=0, keepdims=True)
        total[...] += nt(active, down)
        gn[...] += nt(rounded, up)
        gd[0, :, columns] = nn(branch_t[...], active).astype(BF)
        gu[0, :, columns] = nn(normed_t[...], rounded).astype(BF)
        return carry
    lax.fori_loop(0, u_ref.shape[2] // size, mlp, 0)
    by_frame(total, y_out, mix)
    back, gain, shift = norm_back(third[...], norm2_ref[0:1], gn[...])
    grad[...] += back
    gvec2[0:1] = gain
    gvec2[1:2] = shift
    attention_back(att, rows_in, grad, norm_ref, normed, normed_t, branch, branch_t, dk, dv, gn, gw.at[0], gbias, gvec, 0, lambda i: None)
    by_frame(grad, g_out, mix)


def piece_spec(piece, whole):
    return pl.BlockSpec((1,) + whole.shape[1:], lambda i: (piece, 0, 0))


def full_spec(value):
    return pl.BlockSpec(value.shape, lambda i: (0,) * len(value.shape))


def run(kernel, args, specs, outs, scratch, name):
    return pl.pallas_call(
        kernel, grid=(1,),
        out_shape=outs, in_specs=specs, out_specs=[full_spec(out) for out in outs], scratch_shapes=scratch,
        compiler_params=pltpu.CompilerParams(vmem_limit_bytes=63 * 2**20),
        name=name,
    )(*args)


def shape(*size, dtype=BF):
    return jax.ShapeDtypeStruct(size, dtype)


def spatial_forward(x, whole, bias, norm, out_bias):
    clips, places, model = x.shape
    rows = clips * SP
    args = (x, whole, bias, norm, out_bias)
    specs = [full_spec(a) for a in args]
    specs[1] = piece_spec(0, whole)
    outs = [shape(clips, places, model)] + [shape(4, rows, 256)] * 4 + [shape(4, clips, 3 * SP, SP)]
    return run(spatial_forward_kernel, args, specs, outs,
               [pltpu.VMEM((rows, model), F32), pltpu.VMEM((rows, model), BF)], "spatial_forward")


def spatial_back(x, g, whole, norm, kept):
    clips, places, model = x.shape
    rows = clips * SP
    args = (x, g, whole, norm) + tuple(kept)
    specs = [full_spec(a) for a in args]
    specs[2] = piece_spec(0, whole)
    outs = [shape(clips, places, model), shape(1, *whole.shape[1:]), shape(4, 2, 256, dtype=F32), shape(3, model, dtype=F32)]
    scratch = [pltpu.VMEM((rows, model), F32), pltpu.VMEM((rows, model), BF), pltpu.VMEM((model, rows), BF), pltpu.VMEM((rows, model), BF),
               pltpu.VMEM((model, rows), BF), pltpu.VMEM((rows, 256), BF), pltpu.VMEM((rows, 256), BF),
               pltpu.VMEM((rows, model), F32), pltpu.VMEM((rows, model), F32)]
    return run(spatial_back_kernel, args, specs, outs, scratch, "spatial_back")


def temporal(h, g, whole, bias, norm, norm2, out_bias, up_bias, down_bias):
    frames, pairs, model = h.shape
    rows = frames * pairs
    group = TG * frames
    row = jnp.arange(3 * group)[:, None] % group // frames
    column = jnp.arange(group)[None] // frames
    penalty = jnp.where(row == column, 0.0, -1e30).astype(F32)
    args = (h, g, whole, whole, whole, bias, norm, norm2, out_bias, up_bias.reshape(-1, 1, 384), down_bias, penalty)
    specs = [full_spec(a) for a in args]
    for i, piece in ((2, 1), (3, 2), (4, 3)):
        specs[i] = piece_spec(piece, whole)
    hidden = whole.shape[2]
    outs = [shape(frames, pairs, model), shape(frames, pairs, model), shape(1, model, hidden), shape(1, model, hidden),
            shape(1, model, hidden), shape(4, 2, 256, dtype=F32), shape(3, model, dtype=F32), shape(3, model, dtype=F32),
            shape(hidden // 384, 1, 384, dtype=F32)]
    big = pltpu.VMEM((rows, model), F32)
    low = pltpu.VMEM((rows, model), BF)
    flip = pltpu.VMEM((model, rows), BF)
    part = pltpu.VMEM((rows, 256), BF)
    scratch = [pltpu.VMEM((4, rows, 256), BF)] * 4 + [pltpu.VMEM((4, pairs // TG, 3 * group, group), BF)] + [
        big, big, big, big, low, flip, low, flip, part, part, big, pltpu.VMEM((model // 128, rows, 128), F32)]
    return run(temporal_kernel, args, specs, outs, scratch, "temporal_and_mlp")


STEPS = 16


class Refs:
    def __init__(self, names, refs):
        for name, ref in zip(names, refs, strict=True):
            setattr(self, name, ref)


def pair_segments(index, share, clips, places):
    found = []
    for clip in range(clips):
        low = max(index * share, clip * places)
        high = min(index * share + share, clip * places + places)
        if low < high:
            found.append((low - index * share, high - low, clip, low - clip * places))
    return found


class Reduction:
    def __init__(self, r, places, x, y, k, z, rows, width):
        self.r, self.places, self.rows, self.width = r, places, rows, width
        self.x, self.y, self.k, self.z = x, y, k, z
        self.quads = [(f, yy) for f in range(2) for yy in range(2)]
        self.last = 3

    def piece_of(self, s):
        if isinstance(s, int):
            return 2 + s % 2 if s < 8 else 1 if s < 12 else 0
        early, middle = (s < 8).astype(jnp.int32), ((s >= 8) & (s < 12)).astype(jnp.int32)
        return early * (2 + s % 2) + middle

    def tp_of(self, s):
        if isinstance(s, int):
            return 3 * (s // 2 if s < 8 else s) % 4
        early = (s < 8).astype(jnp.int32)
        return (3 * (early * (s // 2) + (1 - early) * s)) % 4

    def spot(self, f, yy, kk, s):
        row = pl.multiple_of((f * 4 + yy * 2 + kk) * self.rows, 16)
        column = pl.multiple_of(self.tp_of(s) * self.width, 128)
        return self.r.w.at[self.piece_of(s), pl.ds(row, self.rows), pl.ds(column, self.width)]

    def remote(self, src, dst, send, recv, side):
        return pltpu.make_async_remote_copy(
            src_ref=src, dst_ref=dst, send_sem=send, recv_sem=recv,
            device_id=self.places[side], device_id_type=MESH,
        )

    def core_copy(self, s, f, yy):
        r = self.r
        return self.remote(
            self.spot(f, yy, 1 - self.k, s), r.r1.at[s, f, yy], r.s1.at[s, f, yy], r.q1s.at[s, f, yy], "core"
        )

    def diag_copy(self, s, side):
        r = self.r
        return self.remote(r.r1.at[s, 1 - self.x, 1 - self.y], r.r2.at[s], r.s2.at[s], r.q2.at[s], side)

    def x_copy(self, s):
        r = self.r
        return self.remote(r.r1.at[s, 1 - self.x, self.y], r.r3x.at[s], r.s3x.at[s], r.q3x.at[s], "x")

    def y_copy(self, s):
        r = self.r
        return self.remote(r.r1.at[s, self.x, 1 - self.y], r.r3y.at[s], r.s3y.at[s], r.q3y.at[s], "y")

    def up_copy(self, s):
        r = self.r
        return self.remote(r.r1.at[s, self.x, self.y], r.rz.at[s], r.sz.at[s], r.qup.at[s], "up")

    def down_copy(self, s, owner=False):
        r = self.r
        target = r.re.at[self.piece_of(s)] if owner else r.rz.at[s]
        return self.remote(r.r1.at[s, self.x, self.y], target, r.sz.at[s], r.qdn.at[s], "down")

    def start(self, s):
        for f, yy in self.quads:
            self.core_copy(s, f, yy).start()

    def even_odd(self, s, even, odd):
        if isinstance(s, int):
            (odd if s % 2 else even)()
        else:
            pl.when(s % 2 == 0)(even)
            pl.when(s % 2 == 1)(odd)

    def chip_sum(self, s):
        r1 = self.r.r1
        for f, yy in self.quads:
            self.core_copy(s, f, yy).wait_recv()
            r1[s, f, yy] = r1[s, f, yy] + self.spot(f, yy, self.k, s)[...]

        def even():
            self.diag_copy(s, "x").start()
            self.x_copy(s).start()

        def odd():
            self.diag_copy(s, "y").start()
            self.y_copy(s).start()

        self.even_odd(s, even, odd)

    def turn(self, s):
        r1, r2, x, y = self.r.r1, self.r.r2, self.x, self.y
        self.diag_copy(s, "x").wait_recv()

        def even():
            r1[s, x, 1 - y] = r1[s, x, 1 - y] + r2[s]
            self.y_copy(s).start()

        def odd():
            r1[s, 1 - x, y] = r1[s, 1 - x, y] + r2[s]
            self.x_copy(s).start()

        self.even_odd(s, even, odd)

    def plane_sum(self, s):
        r = self.r
        self.x_copy(s).wait_recv()
        self.y_copy(s).wait_recv()
        total = r.r1[s, self.x, self.y].astype(F32) + r.r3x[s].astype(F32) + r.r3y[s].astype(F32)
        r.r1[s, self.x, self.y] = total.astype(BF)

    def line(self, s, hop):
        r, x, y, z, last = self.r, self.x, self.y, self.z, self.last
        t = self.tp_of(s)

        @pl.when((z < t) & (z == hop))
        def _():
            if hop > 0:
                self.up_copy(s).wait_recv()
                r.r1[s, x, y] = r.r1[s, x, y] + r.rz[s]
            self.up_copy(s).start()

        @pl.when((z > t) & (last - z == hop))
        def _():
            if hop > 0:
                self.down_copy(s).wait_recv()
                r.r1[s, x, y] = r.r1[s, x, y] + r.rz[s]

            @pl.when(z - 1 == t)
            def _():
                self.down_copy(s, True).start()

            @pl.when(z - 1 != t)
            def _():
                self.down_copy(s).start()

        far = z + (last - 2 * z) * ((last - 2 * z) > 0).astype(jnp.int32)

        @pl.when((z == t) & (far == hop))
        def _():
            piece = self.piece_of(s)
            r.own[piece] = r.r1[s, x, y].astype(F32)

            @pl.when(z > 0)
            def _():
                self.up_copy(s).wait_recv()
                r.own[piece] = r.own[piece] + r.rz[s].astype(F32)

            @pl.when(z < last)
            def _():
                self.down_copy(s, True).wait_recv()
                r.own[piece] = r.own[piece] + r.re[piece].astype(F32)

    def guard(self, action, s, *rest):
        if isinstance(s, int):
            if 0 <= s < STEPS:
                action(s, *rest)
        else:

            @pl.when((s >= 0) & (s < STEPS))
            def _():
                action(s, *rest)

    def tick(self, n):
        self.guard(self.chip_sum, n - 1)
        self.guard(self.turn, n - 3)
        self.guard(self.plane_sum, n - 5)
        for hop in range(4):
            self.guard(self.line, n - 7 - 2 * hop, hop)

    def finish(self):
        def body(s, carry):
            for f, yy in self.quads:
                self.core_copy(s, f, yy).wait_send()
            self.diag_copy(s, "x").wait_send()
            self.x_copy(s).wait_send()
            self.y_copy(s).wait_send()

            @pl.when(self.z != self.tp_of(s))
            def _():
                self.up_copy(s).wait_send()

            return carry

        lax.fori_loop(0, STEPS, body, 0)


STAGES = 7
X_LAST = (3,)
FIRST = [[(0, 0), (1, 0)], [(0, 1)], [(0, 2), (1, 1)], [(0, 3), (1, 2), (2, 0), (0, 4), (1, 3), (3, 0), (0, 5), (1, 4), (2, 1), (0, 6)]]
WITH_SPATIAL = [[(1, 5)], [(3, 1)], [(1, 6)], [(2, 2)]]
WITH_EXCHANGE = [[(3, 2)], [(2, 3)], [(3, 3)]]
WITH_TEMPORAL = [[(2, 4)], [(3, 4)], [(2, 5)], [(3, 5)]]
AT_END = [(2, 6), (3, 6)]


class Gather:
    def __init__(self, r, places, x, y, k, z):
        self.r, self.places, self.x, self.k, self.z = r, places, x, k, z
        self.c = y * 2 + k
        self.rows, self.width = r.shard.shape[1] // 4, r.shard.shape[2]
        self.sends = []
        c, other_y, last = self.c, (1 - y) * 2 + k, 3
        self.stages = [[] for _ in range(STAGES)]

        def wait(stage, unit, when=None):
            self.stages[stage].append(("wait", unit, when))

        def send(stage, side, unit, when=None, mine=False, x_last=None):
            entry = (side, unit, when, mine, x_last, len(self.sends))
            self.sends.append(entry)
            self.stages[stage].append(("send",) + entry)

        me = (x, c, z)
        send(0, "up", me, z < last, True)
        send(0, "down", me, z > 0, True)
        send(0, "x", me, None, True)
        send(0, "x", (x, other_y, z), None, True)
        for d in (1, 2, 3):
            for sign in (-1, 1):
                t = z + sign * d
                have = (t >= 0) if sign < 0 else (t <= last)
                unit = (x, c, t)
                wait(d, unit, have)
                if d < last:
                    if sign < 0:
                        send(d, "up", unit, have & (z < last))
                    else:
                        send(d, "down", unit, have & (z > 0))
                for side in ("x", "y", "core"):
                    send(d, side, unit, have)
            if d == 1:
                wait(1, (1 - x, c, z))
                send(1, "core", (1 - x, c, z))
            if d == 2:
                wait(2, (1 - x, other_y, z))
                send(2, "core", (1 - x, other_y, z))
        for d in (1, 2, 3):
            for sign in (-1, 1):
                t = z + sign * d
                have = (t >= 0) if sign < 0 else (t <= last)
                wait(d + 1, (1 - x, c, t), have)
                send(d + 1, "y", (1 - x, c, t), have, x_last=False)
                send(d + 1, "core", (1 - x, c, t), have)
                wait(d + 1, (x, other_y, t), have)
                send(d + 1, "x", (x, other_y, t), have, x_last=True)
                send(d + 1, "core", (x, other_y, t), have)
                wait(d + 2, (1 - x, other_y, t), have)
                send(d + 2, "core", (1 - x, other_y, t), have)
                for f in (x, 1 - x):
                    for yy in (y, 1 - y):
                        wait(6, (f, yy * 2 + 1 - k, t), have)
        for yy in (y, 1 - y):
            wait(6, (1 - x, yy * 2 + 1 - k, z))

    def spot(self, piece, unit):
        f, cc, t = unit
        row = pl.multiple_of((f * 4 + cc) * self.rows, 16)
        return self.r.w.at[piece, pl.ds(row, self.rows), pl.ds(pl.multiple_of(t * self.width, 128), self.width)]

    def active(self, piece):
        return lambda entry: entry[4] is None or entry[4] == (piece in X_LAST)

    def copy(self, piece, entry):
        side, unit, _, mine, _, number = entry
        f, cc, t = unit
        target = self.spot(piece, unit)
        source = self.r.shard.at[piece, pl.ds(pl.multiple_of(cc * self.rows, 16), self.rows)] if mine else target
        return pltpu.make_async_remote_copy(
            src_ref=source, dst_ref=target,
            send_sem=self.r.ws.at[number, piece], recv_sem=self.r.wq.at[(f * 4 + cc) * 4 + t, piece],
            device_id=self.places[side], device_id_type=MESH,
        )

    def own(self, piece):
        row = pl.multiple_of(self.x * self.rows * 4, 16)
        column = pl.multiple_of(self.z * self.width, 128)
        target = self.r.w.at[piece, pl.ds(row, self.rows * 4), pl.ds(column, self.width)]
        return pltpu.make_async_copy(self.r.shard.at[piece], target, self.r.wl.at[piece])

    def put(self, piece):
        return pltpu.make_async_copy(self.r.w.at[piece], self.r.whole.at[piece], self.r.wo.at[piece])

    def arrived(self, piece, unit):
        f, cc, t = unit
        ref = self.spot(piece, unit)
        pltpu.make_async_copy(ref, ref, self.r.wq.at[(f * 4 + cc) * 4 + t, piece]).wait()

    def stage(self, piece, number):
        if number == 0:
            self.own(piece).start()
        for kind, *rest in self.stages[number]:
            if kind == "wait":
                unit, when = rest
                maybe(when, lambda: self.arrived(piece, unit))
            elif self.active(piece)(rest):
                maybe(rest[2], lambda: self.copy(piece, rest).start())
        if number == STAGES - 1:
            self.own(piece).wait()
            self.put(piece).start()

    def run(self, items):
        for piece, number in items:
            self.stage(piece, number)

    def beside(self, plan):
        def after(i):
            for step, items in enumerate(plan):
                pl.when(i == step)(lambda: self.run(items))

        return after

    def finish(self):
        always = [entry for entry in self.sends if entry[4] is None]

        def body(piece, carry):
            for entry in always:
                maybe(entry[2], lambda: self.copy(piece, entry).wait_send())
            self.put(piece).wait()
            return carry

        lax.fori_loop(0, PIECES, body, 0)
        for piece in range(PIECES):
            for entry in self.sends:
                if entry[4] is not None and self.active(piece)(entry):
                    maybe(entry[2], lambda: self.copy(piece, entry).wait_send())


FORWARD_NAMES = [
    "shard", "bias", "x_in", "g_in", "norm", "ob", "penalty",
    "whole", "x_out", "q0", "k0", "v0", "o0", "p0", "q1", "k1", "v1", "o1", "p1", "rows_out", "third_out", "grad_out",
    "w", "bias_all", "q", "k", "v", "o", "p", "total", "normed", "rows_in", "third", "grad", "mix",
    "x_recv", "g_send", "g_recv", "h_send", "h_recv",
    "ws", "wq", "wl", "wo", "bs", "bq", "xs", "xq", "cs", "cq", "hs", "hq", "keep",
]


def forward_kernel(*refs):
    r = Refs(FORWARD_NAMES, refs)
    x, c, z = lax.axis_index("fsdp"), lax.axis_index("ctx"), lax.axis_index("tp")
    y, k = c // 2, c % 2
    clips, home_places = r.x_in.shape[0], r.x_in.shape[2]
    model = r.x_in.shape[3]
    places = home_places * 4
    frames, share = r.h_recv.shape[:2]
    rows = frames * share
    me = c * 4 + z
    where = places_of(x, y, k, z)

    barrier = pltpu.get_barrier_semaphore()
    pl.semaphore_signal(barrier, inc=1, device_id=where["x"], device_id_type=MESH)

    def greet(d, carry):
        peer = (me + d) % 16
        pl.semaphore_signal(barrier, inc=1, device_id=(x, peer // 4, peer % 4), device_id_type=MESH)
        return carry

    lax.fori_loop(1, 16, greet, 0)
    pl.semaphore_wait(barrier, 16)

    def remote(src, dst, send, recv, place):
        return pltpu.make_async_remote_copy(
            src_ref=src, dst_ref=dst, send_sem=send, recv_sem=recv, device_id=place, device_id_type=MESH
        )

    gather = Gather(r, where, x, y, k, z)
    early = []
    for d in range(1, 4):
        to = (z + d) % 4
        place = (x, c, to)
        early.append(remote(r.x_in.at[:, to], r.x_recv.at[z], r.xs.at[d], r.xq.at[d], place))
        early.append(remote(r.bias, r.bias_all.at[z], r.bs.at[d], r.bq.at[d], place))
    early.append(pltpu.make_async_copy(r.x_in.at[:, z], r.x_recv.at[z], r.xs.at[0]))
    early.append(pltpu.make_async_copy(r.bias, r.bias_all.at[z], r.bs.at[0]))
    for copy in early:
        copy.start()
    gather.run(FIRST[0])

    def share_out(f, carry):
        for clip in range(clips):
            r.third[64 * clip + 64 : 64 * clip + 64 + home_places] = r.g_in[clip, f].astype(F32)
        for to in range(4):
            used = 0
            for start, count, clip, place in pair_segments(to, share, clips, home_places):
                low = 64 * clip + 64 + place
                r.third[start : start + count] = r.third[low : low + count]
                used = start + count
            if used < share:
                r.third[used:share] = jnp.zeros((share - used, model), F32)
            r.g_send[to * 4 + f] = r.third[0:share].astype(BF)
        return carry

    lax.fori_loop(0, 4, share_out, 0)
    gather.run(FIRST[1])
    shares = []
    for d in range(1, 4):
        to = (c + d) % 4
        shares.append(
            remote(r.g_send.at[pl.ds(to * 4, 4)], r.g_recv.at[pl.ds(c * 4, 4)], r.cs.at[d], r.cq.at[d], (x, to, z))
        )
    shares.append(
        pltpu.make_async_copy(r.g_send.at[pl.ds(c * 4, 4)], r.g_recv.at[pl.ds(c * 4, 4)], r.cs.at[0])
    )
    for copy in shares:
        copy.start()
    gather.run(FIRST[2])

    for copy in early:
        copy.wait()
    keep_x = pltpu.make_async_copy(r.x_recv, r.x_out, r.keep.at[0])
    keep_x.start()
    for clip in range(clips):
        for zz in range(4):
            row = clip * SP + zz * home_places
            r.total[row : row + home_places] = r.x_recv[zz, clip].astype(F32)
        r.total[clip * SP + places : clip * SP + SP] = jnp.zeros((SP - places, model), F32)
    norm_into(r.total, r.norm.at[0], r.normed)
    r.total[...] += r.ob[0:1]
    gather.run(FIRST[3])
    att = Attention(clips, SP, spatial_penalty(places), r.w.at[0], r.bias_all.at[:, 0], r.q, r.k, r.v, r.o, spatial_probs(r.p))
    att.forward(r.normed, r.total, gather.beside(WITH_SPATIAL))
    values = (r.q, r.k, r.v, r.o, r.p)
    kept = [
        pltpu.make_async_copy(source, target, r.keep.at[1 + i])
        for i, (source, target) in enumerate(zip(values, (r.q0, r.k0, r.v0, r.o0, r.p0)))
    ]
    for copy in kept:
        copy.start()
    for cc in range(4):
        for zz in range(4):
            used = 0
            for start, count, clip, place in pair_segments(cc, share, clips, home_places):
                row = clip * SP + zz * home_places + place
                r.third[start : start + count] = r.total[row : row + count]
                used = start + count
            if used < share:
                r.third[used:share] = jnp.zeros((share - used, model), F32)
            r.h_send[cc * 4 + zz] = r.third[0:share].astype(BF)

    def to_column(d):
        peer = (me + d) % 16
        return remote(
            r.h_send.at[peer], r.h_recv.at[me], r.hs.at[d], r.hq.at[d], (x, peer // 4, peer % 4)
        )

    def go(d, carry):
        to_column(d).start()
        return carry

    lax.fori_loop(1, 16, go, 0)
    r.h_recv[me] = r.h_send[me]
    for copy in shares:
        copy.wait()
    gather.run(WITH_EXCHANGE[0])
    by_pair(r.g_recv, r.grad, r.mix)
    gather.run(WITH_EXCHANGE[1])

    def come(d, carry):
        to_column(d).wait()
        return carry

    lax.fori_loop(1, 16, come, 0)

    by_pair(r.h_recv, r.rows_in, r.mix)
    normed = r.normed.at[pl.ds(0, rows)]
    norm_into(r.rows_in, r.norm.at[1], normed)
    r.third[...] = r.rows_in[...] + r.ob[1:2]
    for copy in kept:
        copy.wait()
    group = TG * frames
    att = Attention(
        share // TG, group, lambda: r.penalty[...], r.w.at[1], r.bias_all.at[:, 1],
        *(ref.at[:, pl.ds(0, rows)] for ref in (r.q, r.k, r.v)), r.o, small_probs(r.p, group),
    )
    gather.run(WITH_EXCHANGE[2])
    att.forward(normed, r.third, gather.beside(WITH_TEMPORAL))
    gather.run(AT_END)
    kept = [
        pltpu.make_async_copy(source, target, r.keep.at[1 + i])
        for i, (source, target) in enumerate(
            zip(
                values + (r.rows_in, r.third, r.grad),
                (r.q1, r.k1, r.v1, r.o1, r.p1, r.rows_out, r.third_out, r.grad_out),
            )
        )
    ]
    for copy in kept:
        copy.start()
    gather.finish()
    for copy in kept:
        copy.wait()
    keep_x.wait()


def whole_penalty(group, frames):
    row = jnp.arange(3 * group)[:, None] % group // frames
    column = jnp.arange(group)[None] // frames
    return jnp.where(row == column, 0.0, -1e30).astype(F32)


def forward(shard, bias, inputs, cotangent, norm, out_bias, frames, share):
    clips, _, home_places, model = inputs.shape
    rows, srows = frames * share, clips * SP
    args = (shard, bias, inputs, cotangent, norm, out_bias, whole_penalty(TG * frames, frames))
    anywhere, vmem = pl.BlockSpec(memory_space=pl.ANY), pl.BlockSpec(memory_space=pltpu.VMEM)
    whole = (PIECES, shard.shape[1] * 2, shard.shape[2] * 4)
    blocks = (4, clips, home_places, model)
    part, probs = (4, srows, 256), (4, clips, 3 * SP, SP)
    attention = [part] * 4 + [probs]
    outs = [shape(*whole), shape(*blocks)] + [shape(*size) for size in attention * 2]
    outs += [shape(rows, model, dtype=F32)] * 3
    dma = pltpu.SemaphoreType.DMA
    sends = 58
    scratch = (
        [pltpu.VMEM(whole, BF), pltpu.VMEM((4,) + bias.shape, F32)]
        + [pltpu.VMEM(size, BF) for size in attention]
        + [pltpu.VMEM((srows, model), F32), pltpu.VMEM((srows, model), BF)]
        + [pltpu.VMEM((rows, model), F32)] * 3
        + [pltpu.VMEM((model // 128, rows, 128), F32), pltpu.VMEM(blocks, BF)]
        + [pltpu.VMEM((frames, share, model), BF)] * 4
        + [dma((sends, PIECES)), dma((32, PIECES)), dma((PIECES,)), dma((PIECES,))]
        + [dma((4,))] * 6
        + [dma((16,))] * 2
        + [dma((9,))]
    )
    return pl.pallas_call(
        forward_kernel,
        out_shape=outs,
        in_specs=[vmem, vmem, anywhere, vmem, vmem, vmem, vmem],
        out_specs=[anywhere] * len(outs),
        scratch_shapes=scratch,
        compiler_params=pltpu.CompilerParams(
            collective_id=0, has_side_effects=True, vmem_limit_bytes=67043328
        ),
        name="forward",
    )(*args)


BACK_NAMES = [
    "x", "rows_from", "third_from", "grad_from", "whole", "q1", "k1", "v1", "o1", "p1", "q0", "k0", "v0", "o0", "p0",
    "norm", "ub", "db", "y_home", "g_home", "own", "vectors", "w", "q", "k", "v", "o", "p", "rows_in", "total",
    "third", "grad", "gn", "mix", "normed", "normed_t", "branch", "branch_t", "dk", "dv", "y_send",
    "g_send", "g_recv", "home_send", "bias1", "bias0", "ups", "r1", "r2", "r3x", "r3y", "rz", "re", "va",
    "vr", "load", "s1", "q1s", "s2", "q2", "s3x", "s3y", "q3x", "q3y", "sz", "qup", "qdn", "vs", "vq", "ys",
    "yq", "gs", "gq", "hs", "hq", "keep", "early",
]


def back_kernel(*refs):
    r = Refs(BACK_NAMES, refs)
    x, c, z = lax.axis_index("fsdp"), lax.axis_index("ctx"), lax.axis_index("tp")
    y, k = c // 2, c % 2
    _, clips, home_places, model = r.x.shape
    frames, share = r.y_send.shape[:2]
    rows = frames * share
    places = home_places * 4
    me = c * 4 + z
    where = places_of(x, y, k, z)

    barrier = pltpu.get_barrier_semaphore()
    pl.semaphore_signal(barrier, inc=1, device_id=where["x"], device_id_type=MESH)

    def greet(d, carry):
        peer = (me + d) % 16
        pl.semaphore_signal(barrier, inc=1, device_id=(x, peer // 4, peer % 4), device_id_type=MESH)
        return carry

    lax.fori_loop(1, 16, greet, 0)

    loads = [pltpu.make_async_copy(r.whole.at[i], r.w.at[i], r.load.at[i]) for i in range(4)]
    frames_in = r.rows_in.at[pl.ds(0, rows)]
    values = (r.q, r.k, r.v, r.o, r.p)
    early = [
        pltpu.make_async_copy(source, target, r.early.at[i])
        for i, (source, target) in enumerate(
            zip(
                (r.third_from, r.grad_from, r.rows_from, r.q1, r.k1, r.v1, r.o1, r.p1),
                (r.third, r.grad, frames_in) + values,
            )
        )
    ]
    kept = [
        pltpu.make_async_copy(source, target, r.keep.at[i])
        for i, (source, target) in enumerate(zip((r.q0, r.k0, r.v0, r.o0, r.p0), values))
    ]
    for copy in early[:2] + loads[2:] + early[2:] + loads[:2]:
        copy.start()
    spare = r.normed.shape[0] - rows
    for ref in (r.normed, r.branch, r.dk, r.dv):
        ref[rows:] = jnp.zeros((spare, ref.shape[1]), BF)
    r.total[rows:] = jnp.zeros((spare, model), F32)
    early[0].wait()
    early[1].wait()

    norm_into(r.third, r.norm.at[2], r.normed)
    flip_into(r.normed, r.normed_t)
    va = r.va.at[0]
    round_into(r.grad, r.branch, va, 8)
    flip_into(r.branch, r.branch_t)
    r.total[0:rows] = r.third[...] + r.db[...]
    r.gn[...] = jnp.zeros(r.gn.shape, F32)
    loads[2].wait()
    loads[3].wait()
    pl.semaphore_wait(barrier, 16)
    red = Reduction(r, where, x, y, k, z, r.own.shape[1], r.own.shape[2])
    size = r.ub.shape[2]
    halves = r.own.shape[2] // size

    def mlp(i, carry):
        t = (3 * i) % 4
        for half in range(halves):
            j = t * halves + half
            columns = pl.ds(pl.multiple_of(j * size, 128), size)
            up = r.w[2, :, columns]
            down = r.w[3, :, columns]
            hidden = nn(r.normed[...], up) + r.ub[j]
            cdf = 0.5 + 0.5 * lax.erf(hidden * (2.0**-0.5))
            active = (hidden * cdf).astype(BF)
            slope = cdf + hidden * (jnp.exp(-0.5 * hidden * hidden) * ((2.0 * jnp.pi) ** -0.5))
            rounded = (nn(r.branch[...], down) * slope).astype(BF)
            r.ups[j] = jnp.sum(rounded.astype(F32), axis=0, keepdims=True)
            r.total[...] += nt(active, down)
            r.gn[...] += nt(rounded, up)
            r.w[3, :, columns] = nn(r.branch_t[...], active).astype(BF)
            r.w[2, :, columns] = nn(r.normed_t[...], rounded).astype(BF)
        for s in (2 * i, 2 * i + 1):
            red.start(s)
        for s in (2 * i, 2 * i + 1):
            red.tick(s)
        return carry

    lax.fori_loop(0, 4, mlp, 0)

    by_frame(r.total.at[pl.ds(0, rows)], r.y_send, r.mix)
    outs = []
    for d in range(1, 4):
        peer = (c + d) % 4
        copy = pltpu.make_async_remote_copy(
            src_ref=r.y_send.at[pl.ds(peer * 4, 4)], dst_ref=r.y_home.at[c],
            send_sem=r.ys.at[d], recv_sem=r.yq.at[d], device_id=(x, peer, z), device_id_type=MESH,
        )
        copy.start()
        outs.append(copy)
    y_own = pltpu.make_async_copy(r.y_send.at[pl.ds(c * 4, 4)], r.y_home.at[c], r.ys.at[0])
    y_own.start()

    norm_back_into(r.third, r.norm.at[2], r.gn, r.grad, va, 6)
    for copy in early[2:]:
        copy.wait()
    loads[1].wait()
    for t in range(4):
        r.o[t, rows:] = jnp.zeros((spare, r.o.shape[2]), BF)
    group = TG * frames
    att = Attention(
        share // TG, group, None, r.w.at[1], None,
        *(ref.at[:, pl.ds(0, rows)] for ref in (r.q, r.k, r.v)), r.o, small_probs(r.p, group),
    )

    def each(first):
        def after(i):
            red.start(first + i)
            maybe(i > 0 if first == 12 else None, lambda: red.tick(first + i))

        return after

    attention_back(
        att, frames_in, r.grad, r.norm.at[1], r.normed, r.normed_t, r.branch, r.branch_t,
        r.dk, r.dv, r.gn, r.w.at[1], r.bias1, va, 3, each(8),
    )
    for copy in kept:
        copy.start()
    by_frame(r.grad, r.g_send, r.mix)

    def to_frame(d):
        peer = (me + d) % 16
        return pltpu.make_async_remote_copy(
            src_ref=r.g_send.at[peer], dst_ref=r.g_recv.at[me],
            send_sem=r.gs.at[d], recv_sem=r.gq.at[d], device_id=(x, peer // 4, peer % 4), device_id_type=MESH,
        )

    def go(d, carry):
        to_frame(d).start()
        return carry

    lax.fori_loop(1, 16, go, 0)
    r.g_recv[me] = r.g_send[me]
    red.tick(12)
    for copy in kept:
        copy.wait()
    loads[0].wait()
    srows = clips * SP
    for clip in range(clips):
        for zz in range(4):
            row = clip * SP + zz * home_places
            r.rows_in[row : row + home_places] = r.x[zz, clip].astype(F32)
        r.rows_in[pl.ds(clip * SP + places, SP - places)] = jnp.zeros((SP - places, model), F32)
        r.total[pl.ds(clip * SP + places, SP - places)] = jnp.zeros((SP - places, model), F32)

    def come(d, carry):
        to_frame(d).wait()
        return carry

    lax.fori_loop(1, 16, come, 0)
    for cc in range(4):
        for zz in range(4):
            r.third[0:share] = r.g_recv[cc * 4 + zz].astype(F32)
            for start, count, clip, place in pair_segments(cc, share, clips, home_places):
                row = clip * SP + zz * home_places + place
                r.total[row : row + count] = r.third[start : start + count]

    att = Attention(clips, SP, None, r.w.at[0], None, r.q, r.k, r.v, r.o, spatial_probs(r.p))
    attention_back(
        att, r.rows_in, r.total, r.norm.at[0], r.normed, r.normed_t, r.branch, r.branch_t, r.dk, r.dv, r.gn,
        r.w.at[0], r.bias0, va, 0, each(12),
    )
    for zz in range(4):
        for clip in range(clips):
            row = clip * SP + zz * home_places
            r.third[0:home_places] = r.total[row : row + home_places]
            r.home_send[zz, clip] = r.third[0:home_places].astype(BF)
    for d in range(1, 4):
        peer = (z + d) % 4
        copy = pltpu.make_async_remote_copy(
            src_ref=r.home_send.at[peer], dst_ref=r.g_home.at[z],
            send_sem=r.hs.at[d], recv_sem=r.hq.at[d], device_id=(x, c, peer), device_id_type=MESH,
        )
        copy.start()
        outs.append(copy)
    g_own = pltpu.make_async_copy(r.home_send.at[z], r.g_home.at[z], r.hs.at[0])
    g_own.start()

    for j in range(r.ups.shape[0]):
        va[9 + j // halves : 10 + j // halves, (j % halves) * size : (j % halves + 1) * size] = r.ups[j]
    for i, ref in enumerate((r.bias0, r.bias1)):
        for t in range(4):
            va[16 + i * 8 + t * 2 : 18 + i * 8 + t * 2, 0:256] = ref[t]
    sides = ("core", "x", "y", "z1", "z2")

    def v_copy(j):
        return red.remote(r.va.at[j], r.vr.at[j], r.vs.at[j], r.vq.at[j], sides[j])

    v_copy(0).start()
    for n in range(16, STEPS + 13):
        red.tick(n)
        j = n - 16
        if j < 5:
            v_copy(j).wait()
            if j < 4:
                r.va[j + 1] = r.va[j] + r.vr[j]
                v_copy(j + 1).start()
            else:
                r.vectors[...] = r.va[j] + r.vr[j]
    red.finish()
    for copy in outs:
        copy.wait()
    y_own.wait()
    g_own.wait()


def backward(x, rows_in, third, grad, whole, kept, norm, up_bias, down_bias, own_rows, width, frames):
    _, clips, home_places, model = x.shape
    rows, srows = third.shape[0], clips * SP
    places, share = home_places * 4, rows // frames
    size = 384
    anywhere, vmem = pl.BlockSpec(memory_space=pl.ANY), pl.BlockSpec(memory_space=pltpu.VMEM)
    args = (x, rows_in, third, grad, whole, *kept, norm, up_bias.reshape(-1, 1, size), down_bias)
    in_specs = [vmem] + [anywhere] * 14 + [vmem] * 3
    sub = (own_rows, width)
    big = max(rows, srows)

    def v(*dims, dtype=BF):
        return pltpu.VMEM(dims, dtype)

    def f(*dims):
        return pltpu.VMEM(dims, F32)

    dma = pltpu.SemaphoreType.DMA
    scratch = (
        [v(*whole.shape)]
        + [v(4, big, 256)] * 4
        + [v(4, clips, 3 * SP, SP)]
        + [f(big, model), f(big, model), f(rows, model), f(rows, model), f(big, model)]
        + [f(model // 128, rows, 128)]
        + [v(big, model), v(model, big), v(big, model), v(model, big), v(big, 256), v(big, 256)]
        + [v(frames, share, model), v(frames, share, model), v(frames, share, model)]
        + [v(4, clips, places // 4, model), f(4, 2, 256), f(4, 2, 256), f(up_bias.shape[0] // size, 1, size)]
        + [v(STEPS, 2, 2, *sub)]
        + [v(STEPS, *sub)] * 4
        + [v(PIECES, *sub)]
        + [f(5, 32, model)] * 2
        + [dma((4,))]
        + [dma((STEPS, 2, 2))] * 2
        + [dma((STEPS,))] * 9
        + [dma((5,))] * 2
        + [dma((4,))] * 2
        + [dma((16,))] * 2
        + [dma((4,))] * 2
        + [dma((5,))]
        + [dma((8,))]
    )
    return pl.pallas_call(
        back_kernel,
        out_shape=(
            shape(4, frames // 4, share, model),
            shape(4, clips, places // 4, model),
            shape(PIECES, *sub, dtype=F32),
            shape(32, model, dtype=F32),
        ),
        in_specs=in_specs,
        out_specs=[anywhere, anywhere, vmem, vmem],
        scratch_shapes=scratch,
        compiler_params=pltpu.CompilerParams(
            collective_id=2, has_side_effects=True, vmem_limit_bytes=67043328
        ),
        name="backward",
    )(*args)


def local(
    inputs,
    cotangent,
    norm_gain,
    norm_bias,
    attn_weight,
    attn_bias,
    out_weight,
    out_bias,
    up_weight,
    up_bias,
    down_weight,
    down_bias,
):
    ranks_c = lax.axis_size("ctx")
    tp_rank = lax.axis_index("tp")
    clips, frames, places, model = inputs.shape
    width = attn_weight.shape[3]

    shard = jnp.concatenate(
        [
            jnp.concatenate(
                [
                    attn_weight.transpose(0, 2, 1, 3).reshape(2, attn_weight.shape[2], 3 * width),
                    out_weight.transpose(0, 2, 1),
                ],
                axis=2,
            ),
            up_weight[None],
            down_weight.T[None],
        ]
    )
    norm = jnp.stack([norm_gain, norm_bias], axis=1)

    pairs = clips * places
    share = -(-pairs // ranks_c)
    share += -share % TG

    def home_to_spatial(values):
        return lax.all_to_all(values, "tp", split_axis=1, concat_axis=2, tiled=True)

    def spatial_to_home(values):
        return lax.all_to_all(values, "tp", split_axis=2, concat_axis=1, tiled=True)

    def home_to_temporal(values):
        rows = values.transpose(1, 0, 2, 3).reshape(frames, pairs, model)
        rows = jnp.pad(rows, ((0, 0), (0, share * ranks_c - pairs), (0, 0)))
        return lax.all_to_all(rows, "ctx", split_axis=1, concat_axis=0, tiled=True)

    def temporal_to_home(values):
        rows = lax.all_to_all(values, "ctx", split_axis=0, concat_axis=1, tiled=True)[:, :pairs]
        return rows.reshape(frames, clips, places, model).transpose(1, 0, 2, 3)

    ups = up_bias.shape[0] // model
    bias = jnp.pad(attn_bias, ((0, 0), (0, 6), (0, 256 - width)))
    if lax.axis_size("fsdp") == 2 and (ranks_c, lax.axis_size("tp")) == (4, 4):
        frames *= ranks_c
        whole, first, *kept = forward(shard, bias, inputs, cotangent, norm, out_bias, frames, share)
        kept, rows = kept[5:10] + kept[:5], kept[10:]
        home, grad_home, own, vectors = backward(
            first, *rows, whole, kept, norm, up_bias, down_bias[None], attn_weight.shape[2] // 4, up_weight.shape[1], frames
        )
        frames //= ranks_c
        outputs = home.transpose(1, 0, 2, 3).reshape(frames, -1, model)[:, :pairs]
        outputs = outputs.reshape(frames, clips, places, model).transpose(1, 0, 2, 3)
        input_grad = grad_home.transpose(1, 0, 2, 3)
        sums = vectors[16:, :256].reshape(2, 4, 2, 256)[..., :width].transpose(0, 2, 1, 3)
        attn_bias_sums = sums.reshape(2, 2, model)
    else:
        whole, bias = gather(shard, bias)
        bias = bias[:, :, :2].transpose(1, 0, 2, 3)
        first = home_to_spatial(inputs)
        spatial_shape = first.shape
        first = first.reshape((-1,) + first.shape[2:])
        second, *kept = spatial_forward(first, whole, bias[0], norm[0], out_bias[0:1])
        second = home_to_temporal(spatial_to_home(second.reshape(spatial_shape)))
        grad_out = home_to_temporal(cotangent)
        result, grad_second, grad_attn1, grad_up, grad_down, bias1, vec1, vec2, grad_up_bias = temporal(
            second, grad_out, whole, bias[1], norm[1], norm[2], out_bias[1:2], up_bias, down_bias[None]
        )
        outputs = temporal_to_home(result)
        grad_second = home_to_spatial(temporal_to_home(grad_second)).reshape(first.shape)
        grad_first, grad_attn0, bias0, vec0 = spatial_back(first, grad_second, whole, norm[0], kept)
        input_grad = spatial_to_home(grad_first.reshape(spatial_shape))
        bias_sums = jnp.stack([bias0, bias1])[..., :width].transpose(0, 2, 1, 3)
        lines = [vec0, vec1, vec2, grad_up_bias, bias_sums]
        flat = jnp.concatenate([line.reshape(-1, model) for line in lines])
        vectors = jnp.pad(flat, ((0, -flat.shape[0] % 8), (0, 0)))
        own, vectors = scatter([grad_attn0, grad_attn1, grad_up, grad_down], vectors)
        attn_bias_sums = vectors[9 + ups : 13 + ups].reshape(2, 2, model)
    triples = vectors[:9].reshape(3, 3, model)
    attn = own[:2].reshape(2, own.shape[1], 4, width)
    return (
        outputs,
        input_grad,
        triples[:, 0],
        triples[:, 1],
        attn[:, :, :3].transpose(0, 2, 1, 3),
        lax.dynamic_slice_in_dim(attn_bias_sums, tp_rank * width, width, 2),
        attn[:, :, 3].transpose(0, 2, 1),
        triples[:2, 2],
        own[2],
        vectors[9 : 9 + ups].reshape(-1),
        own[3].T,
        triples[2, 2],
    )


def solution(mesh):
    return jax.shard_map(
        local,
        mesh=mesh,
        in_specs=(
            P("fsdp", "ctx", "tp", None),
            P("fsdp", "ctx", "tp", None),
            P(),
            P(),
            P(None, None, "fsdp", "tp"),
            P(None, None, "tp"),
            P(None, "tp", "fsdp"),
            P(),
            P("fsdp", "tp"),
            P(),
            P("tp", "fsdp"),
            P(),
        ),
        out_specs=(
            P("fsdp", "ctx", "tp", None),
            P("fsdp", "ctx", "tp", None),
            P(),
            P(),
            P(None, None, ("fsdp", "ctx"), "tp"),
            P(None, None, "tp"),
            P(None, "tp", ("fsdp", "ctx")),
            P(),
            P(("fsdp", "ctx"), "tp"),
            P(),
            P("tp", ("fsdp", "ctx")),
            P(),
        ),
        check_vma=False,
    )
```

```python
import jax
import jax.numpy as jnp
from jax import lax
from jax.experimental import pallas as pl
from jax.experimental.pallas import tpu as pltpu
from jax.sharding import PartitionSpec as P

HEAD = 64
EPSILON = 1e-06
BF = jnp.bfloat16
F32 = jnp.float32
MESH = pl.DeviceIdType.MESH
PIECES = 4
ALL = ("fsdp", "ctx", "tp")


def places_of(x, y, k, z):
    return {
        "x": (1 - x, y * 2 + k, z),
        "y": (x, (1 - y) * 2 + k, z),
        "core": (x, y * 2 + 1 - k, z),
        "up": (x, y * 2 + k, z + 1),
        "down": (x, y * 2 + k, z - 1),
        "z1": (x, y * 2 + k, (z // 2) * 2 + 1 - z % 2),
        "z2": (x, y * 2 + k, (z + 2) % 4),
    }


def maybe(when, action):
    if when is None:
        action()
    else:
        pl.when(when)(action)


def gather(shard, bias):
    part = shard.shape[1] // lax.axis_size("ctx")
    mine = lax.dynamic_slice_in_dim(shard, lax.axis_index("ctx") * part, part, 1)
    tall = lax.all_gather(mine, ("fsdp", "ctx"), axis=1, tiled=True)
    return lax.all_gather(tall, "tp", axis=2, tiled=True), lax.all_gather(bias, "tp")


def scatter(grads, vectors):
    tall = lax.psum_scatter(jnp.concatenate(grads), ("fsdp", "ctx"), scatter_dimension=1, tiled=True)
    own = lax.psum_scatter(tall, "tp", scatter_dimension=2, tiled=True)
    return own.astype(F32), lax.psum(vectors, ALL)


def nn(a, b):
    return lax.dot_general(a, b, (((1,), (0,)), ((), ())), preferred_element_type=F32)


def nt(a, b):
    return lax.dot_general(a, b, (((1,), (1,)), ((), ())), preferred_element_type=F32)


def tn(a, b):
    return lax.dot_general(a, b, (((0,), (0,)), ((), ())), preferred_element_type=F32)


def normalise(rows):
    centre = rows - jnp.mean(rows, axis=-1, keepdims=True)
    scale = lax.rsqrt(jnp.mean(centre * centre, axis=-1, keepdims=True) + EPSILON)
    return centre * scale, scale


def chunks(count):
    size = 80 if count % 80 == 0 else 208
    return size, count // size


def norm_into(source, norm, target):
    size, number = chunks(source.shape[0])

    def body(i, carry):
        span = pl.ds(pl.multiple_of(i * size, 16), size)
        unit, _ = normalise(source[span])
        target[span] = (unit * norm[0:1] + norm[1:2]).astype(BF)
        return carry

    lax.fori_loop(0, number, body, 0)


def norm_back_into(source, norm, grad, total, vec, line):
    size, number = chunks(source.shape[0])
    vec[line : line + 2] = jnp.zeros((2, source.shape[1]), F32)

    def body(i, carry):
        span = pl.ds(pl.multiple_of(i * size, 16), size)
        back, gain, shift = norm_back(source[span], norm[0:1], grad[span])
        total[span] += back
        vec[line : line + 1] += gain
        vec[line + 1 : line + 2] += shift
        return carry

    lax.fori_loop(0, number, body, 0)


def round_into(source, target, vec, line):
    size, number = chunks(source.shape[0])
    vec[line : line + 1] = jnp.zeros((1, source.shape[1]), F32)

    def body(i, carry):
        span = pl.ds(pl.multiple_of(i * size, 16), size)
        rounded = source[span].astype(BF)
        target[span] = rounded
        vec[line : line + 1] += jnp.sum(rounded.astype(F32), axis=0, keepdims=True)
        return carry

    lax.fori_loop(0, number, body, 0)


def flip_into(source, target):
    rows = source.shape[0]
    for low in range(0, rows, 128):
        high = min(rows, low + 128)
        target[:, low:high] = source[low:high].T


def norm_back(rows, gain, grad):
    unit, scale = normalise(rows)
    inner = grad * gain
    mean = jnp.mean(inner, axis=-1, keepdims=True)
    along = jnp.mean(inner * unit, axis=-1, keepdims=True)
    return scale * (inner - mean - unit * along), jnp.sum(grad * unit, axis=0, keepdims=True), jnp.sum(
        grad, axis=0, keepdims=True
    )


def lanes_in(low, high):
    lane = lax.broadcasted_iota(jnp.int32, (1, 256), 1)
    return jnp.where((lane >= low) & (lane < high), 1.0, 0.0)


def stack_heads(values):
    return jnp.concatenate(
        [values * lanes_in(i * HEAD, i * HEAD + HEAD).astype(BF) for i in range(3)], axis=0
    )


def pick_heads(stacked):
    rows = stacked.shape[0] // 3
    return sum(
        stacked[i * rows : (i + 1) * rows] * lanes_in(i * HEAD, i * HEAD + HEAD) for i in range(3)
    )


def shifted(values):
    return pltpu.roll(values, 64, axis=1)


def unshifted(values):
    return pltpu.roll(values, 192, axis=1)


def block(w_ref, t, start, size):
    return w_ref[:, pl.ds(pl.multiple_of(t * (w_ref.shape[1] // 4) + start, 128), size)]


def spatial_probs(ref):
    return lambda t, g: ref.at[t, g]


def small_probs(ref, size):
    def find(t, g):
        row, lane = ((g % 2) * 3 * size, 0) if g < 4 else (0, 128)
        return ref.at[t, g // 2 % 2, pl.ds(row, 3 * size), pl.ds(lane, size)]

    return find


class Attention:
    def __init__(self, groups, rows, penalty, w, bias, q, k, v, o, p):
        self.groups, self.rows, self.penalty = groups, rows, penalty
        self.w, self.bias, self.q, self.k, self.v, self.o, self.p = w, bias, q, k, v, o, p

    def spans(self):
        return [(g, pl.ds(g * self.rows, self.rows)) for g in range(self.groups)]

    def forward(self, normed, total, after=lambda i: None):
        used = lanes_in(0, 192)

        def body(t, carry):
            mixed = nn(normed[...], block(self.w, t, 0, 640))
            self.q[t] = ((mixed[:, :256] + self.bias[t, 0:1]) * used).astype(BF)
            self.k[t] = (unshifted(mixed[:, 128:384]) * used).astype(BF)
            self.v[t] = ((mixed[:, 384:] + self.bias[t, 1:2]) * used).astype(BF)
            for g, span in self.spans():
                scores = nt(stack_heads(self.q[t, span]), self.k[t, span]) * 0.125 + self.penalty()
                weights = jnp.exp(scores - jnp.max(scores, axis=-1, keepdims=True))
                weights = weights * (1.0 / jnp.sum(weights, axis=-1, keepdims=True))
                weights = weights.astype(BF)
                self.p(t, g)[...] = weights
                out = pick_heads(nn(weights, self.v[t, span]))
                self.o[t, span] = shifted(out).astype(BF)
            total[...] += nt(self.o[t, pl.ds(0, self.groups * self.rows)], block(self.w, t, 512, 256))
            after(t)
            return carry

        lax.fori_loop(0, 4, body, 0)

    def backward(self, normed_t, branch, branch_t, dk, dv, grad_normed, grad_w, grad_bias, after):
        used = lanes_in(0, 192)

        def body(i, carry):
            t = (3 * i) % 4
            grad_o = (unshifted(nn(branch[...], block(self.w, t, 512, 256))) * used).astype(BF)
            dq = []
            for g, span in self.spans():
                stacked = stack_heads(grad_o[g * self.rows : (g + 1) * self.rows])
                weights = self.p(t, g)[...]
                probs = weights.astype(F32)
                grad_p = nt(stacked, self.v[t, span])
                inner = jnp.sum(probs * grad_p, axis=-1, keepdims=True)
                grad_s = (probs * (grad_p - inner)).astype(BF)
                dq.append((pick_heads(nn(grad_s, self.k[t, span])) * 0.125).astype(BF))
                dk[span] = shifted(tn(grad_s, stack_heads(self.q[t, span])) * 0.125).astype(BF)
                dv[span] = tn(weights, stacked).astype(BF)
            extra = normed_t.shape[1] - self.groups * self.rows
            if extra:
                dq.append(jnp.zeros((extra, 256), BF))
            dq = jnp.concatenate(dq, axis=0)
            grad_normed[...] += (
                nt(dq, block(self.w, t, 0, 256))
                + nt(dk[...], block(self.w, t, 128, 256))
                + nt(dv[...], block(self.w, t, 384, 256))
            )
            for start, low, high in (
                (0, nn(normed_t[...], dq), nn(normed_t[...], dk[...])),
                (384, nn(normed_t[...], dv[...]), nn(branch_t[...], self.o[t])),
            ):
                columns = pl.multiple_of(t * (self.w.shape[1] // 4) + start, 128)
                grad_w[:, pl.ds(columns, 128)] = low[:, :128].astype(BF)
                grad_w[:, pl.ds(columns + 128, 128)] = (low[:, 128:] + high[:, :128]).astype(BF)
                grad_w[:, pl.ds(columns + 256, 128)] = high[:, 128:].astype(BF)
            grad_bias[t, 0:1] = jnp.sum(dq.astype(F32), axis=0, keepdims=True)
            grad_bias[t, 1:2] = jnp.sum(dv[...].astype(F32), axis=0, keepdims=True)
            after(i)
            return carry

        lax.fori_loop(0, 4, body, 0)


SP = 208


def spatial_penalty(places):
    def penalty():
        lane = lax.broadcasted_iota(jnp.int32, (1, SP), 1)
        return jnp.where(lane < places, 0.0, -1e30)
    return penalty


def spatial_forward_kernel(x_ref, w_ref, bias_ref, norm_ref, ob_ref, h_out, q, k, v, o, p, total, normed):
    clips, places, model = x_ref.shape
    for g in range(clips):
        total[pl.ds(g * SP, places)] = x_ref[g].astype(F32)
        total[pl.ds(g * SP + places, SP - places)] = jnp.zeros((SP - places, model), F32)
        span = pl.ds(g * SP, SP)
        unit, _ = normalise(total[span])
        normed[span] = (unit * norm_ref[0:1] + norm_ref[1:2]).astype(BF)
        total[span] += ob_ref[...]
    att = Attention(clips, SP, spatial_penalty(places), w_ref.at[0], bias_ref, q, k, v, o, spatial_probs(p))
    att.forward(normed, total)
    for g in range(clips):
        h_out[g] = total[pl.ds(g * SP, places)].astype(BF)


def spatial_back_kernel(x_ref, g_ref, w_ref, norm_ref, q, k, v, o, p,
                        gx_out, gw, gbias, gvec, total, normed, normed_t, branch, branch_t, dk, dv, gn, rows_in):
    clips, places, model = x_ref.shape
    for g in range(clips):
        for ref, source in ((rows_in, x_ref), (total, g_ref)):
            ref[pl.ds(g * SP, places)] = source[g].astype(F32)
            ref[pl.ds(g * SP + places, SP - places)] = jnp.zeros((SP - places, model), F32)
    attention_back(Attention(clips, SP, None, w_ref.at[0], None, q, k, v, o, spatial_probs(p)),
                   rows_in, total, norm_ref, normed, normed_t, branch, branch_t, dk, dv, gn, gw.at[0], gbias, gvec, 0, lambda i: None)
    for g in range(clips):
        gx_out[g] = total[pl.ds(g * SP, places)].astype(BF)


def attention_back(
    att, rows_in, total, norm, normed, normed_t, branch, branch_t, dk, dv, gn, grad_w, gbias, vec, line, after
):
    round_into(total, branch, vec, line + 2)
    flip_into(branch, branch_t)
    norm_into(rows_in, norm, normed)
    flip_into(normed, normed_t)
    gn[...] = jnp.zeros(gn.shape, F32)
    att.backward(normed_t, branch, branch_t, dk, dv, gn, grad_w, gbias, after)
    norm_back_into(rows_in, norm, gn, total, vec, line)


def by_pair(source, target, mix):
    frames, pairs, model = source.shape
    for f in range(frames):
        values = source[f].astype(F32)
        for i in range(model // 128):
            mix[i, pl.ds(f, pairs, stride=frames)] = values[:, i * 128 : i * 128 + 128]
    for i in range(model // 128):
        target[:, i * 128 : i * 128 + 128] = mix[i]


def by_frame(source, target, mix):
    frames, pairs, model = target.shape
    for i in range(model // 128):
        mix[i] = source[:, i * 128 : i * 128 + 128]
    for f in range(frames):
        for i in range(model // 128):
            target[f, :, i * 128 : i * 128 + 128] = mix[i, pl.ds(f, pairs, stride=frames)].astype(BF)


TG = 5


def temporal_kernel(h_ref, g_ref, w_ref, u_ref, d_ref, bias_ref, norm_ref, norm2_ref, ob_ref, ub_ref, db_ref, pen_ref,
                    y_out, g_out, gw, gu, gd, gbias, gvec, gvec2, gub,
                    q, k, v, o, p, rows_in, total, third, grad, normed, normed_t, branch, branch_t, dk, dv, gn, mix):
    frames, pairs, model = h_ref.shape
    rows = frames * pairs
    by_pair(h_ref, rows_in, mix)
    by_pair(g_ref, grad, mix)
    unit, _ = normalise(rows_in[...])
    normed[...] = (unit * norm_ref[0:1] + norm_ref[1:2]).astype(BF)
    third[...] = rows_in[...] + ob_ref[...]
    group = TG * frames
    att = Attention(pairs // TG, group, lambda: pen_ref[...], w_ref.at[0], bias_ref, q, k, v, o, spatial_probs(p))
    att.forward(normed, third)
    unit, _ = normalise(third[...])
    n2 = unit * norm2_ref[0:1] + norm2_ref[1:2]
    normed[...] = n2.astype(BF)
    normed_t[...] = n2.T.astype(BF)
    branch[...] = grad[...].astype(BF)
    branch_t[...] = grad[...].T.astype(BF)
    gvec2[2:3] = jnp.sum(grad[...], axis=0, keepdims=True)
    total[...] = third[...] + db_ref[...]
    gn[...] = jnp.zeros_like(gn)
    size = 384
    def mlp(j, carry):
        columns = pl.ds(pl.multiple_of(j * size, 128), size)
        up = u_ref[0, :, columns]
        down = d_ref[0, :, columns]
        hidden = nn(normed[...], up) + ub_ref[j]
        half = 0.5 + 0.5 * lax.erf(hidden * (2.0 ** -0.5))
        active = (hidden * half).astype(BF)
        slope = half + hidden * (jnp.exp(-0.5 * hidden * hidden) * ((2.0 * jnp.pi) ** -0.5))
        grad_hidden = nn(branch[...], down) * slope
        rounded = grad_hidden.astype(BF)
        gub[j] = jnp.sum(rounded.astype(F32), axis=0, keepdims=True)
        total[...] += nt(active, down)
        gn[...] += nt(rounded, up)
        gd[0, :, columns] = nn(branch_t[...], active).astype(BF)
        gu[0, :, columns] = nn(normed_t[...], rounded).astype(BF)
        return carry
    lax.fori_loop(0, u_ref.shape[2] // size, mlp, 0)
    by_frame(total, y_out, mix)
    back, gain, shift = norm_back(third[...], norm2_ref[0:1], gn[...])
    grad[...] += back
    gvec2[0:1] = gain
    gvec2[1:2] = shift
    attention_back(att, rows_in, grad, norm_ref, normed, normed_t, branch, branch_t, dk, dv, gn, gw.at[0], gbias, gvec, 0, lambda i: None)
    by_frame(grad, g_out, mix)


def piece_spec(piece, whole):
    return pl.BlockSpec((1,) + whole.shape[1:], lambda i: (piece, 0, 0))


def full_spec(value):
    return pl.BlockSpec(value.shape, lambda i: (0,) * len(value.shape))


def run(kernel, args, specs, outs, scratch, name):
    return pl.pallas_call(
        kernel, grid=(1,),
        out_shape=outs, in_specs=specs, out_specs=[full_spec(out) for out in outs], scratch_shapes=scratch,
        compiler_params=pltpu.CompilerParams(vmem_limit_bytes=63 * 2**20),
        name=name,
    )(*args)


def shape(*size, dtype=BF):
    return jax.ShapeDtypeStruct(size, dtype)


def spatial_forward(x, whole, bias, norm, out_bias):
    clips, places, model = x.shape
    rows = clips * SP
    args = (x, whole, bias, norm, out_bias)
    specs = [full_spec(a) for a in args]
    specs[1] = piece_spec(0, whole)
    outs = [shape(clips, places, model)] + [shape(4, rows, 256)] * 4 + [shape(4, clips, 3 * SP, SP)]
    return run(spatial_forward_kernel, args, specs, outs,
               [pltpu.VMEM((rows, model), F32), pltpu.VMEM((rows, model), BF)], "spatial_forward")


def spatial_back(x, g, whole, norm, kept):
    clips, places, model = x.shape
    rows = clips * SP
    args = (x, g, whole, norm) + tuple(kept)
    specs = [full_spec(a) for a in args]
    specs[2] = piece_spec(0, whole)
    outs = [shape(clips, places, model), shape(1, *whole.shape[1:]), shape(4, 2, 256, dtype=F32), shape(3, model, dtype=F32)]
    scratch = [pltpu.VMEM((rows, model), F32), pltpu.VMEM((rows, model), BF), pltpu.VMEM((model, rows), BF), pltpu.VMEM((rows, model), BF),
               pltpu.VMEM((model, rows), BF), pltpu.VMEM((rows, 256), BF), pltpu.VMEM((rows, 256), BF),
               pltpu.VMEM((rows, model), F32), pltpu.VMEM((rows, model), F32)]
    return run(spatial_back_kernel, args, specs, outs, scratch, "spatial_back")


def temporal(h, g, whole, bias, norm, norm2, out_bias, up_bias, down_bias):
    frames, pairs, model = h.shape
    rows = frames * pairs
    group = TG * frames
    row = jnp.arange(3 * group)[:, None] % group // frames
    column = jnp.arange(group)[None] // frames
    penalty = jnp.where(row == column, 0.0, -1e30).astype(F32)
    args = (h, g, whole, whole, whole, bias, norm, norm2, out_bias, up_bias.reshape(-1, 1, 384), down_bias, penalty)
    specs = [full_spec(a) for a in args]
    for i, piece in ((2, 1), (3, 2), (4, 3)):
        specs[i] = piece_spec(piece, whole)
    hidden = whole.shape[2]
    outs = [shape(frames, pairs, model), shape(frames, pairs, model), shape(1, model, hidden), shape(1, model, hidden),
            shape(1, model, hidden), shape(4, 2, 256, dtype=F32), shape(3, model, dtype=F32), shape(3, model, dtype=F32),
            shape(hidden // 384, 1, 384, dtype=F32)]
    big = pltpu.VMEM((rows, model), F32)
    low = pltpu.VMEM((rows, model), BF)
    flip = pltpu.VMEM((model, rows), BF)
    part = pltpu.VMEM((rows, 256), BF)
    scratch = [pltpu.VMEM((4, rows, 256), BF)] * 4 + [pltpu.VMEM((4, pairs // TG, 3 * group, group), BF)] + [
        big, big, big, big, low, flip, low, flip, part, part, big, pltpu.VMEM((model // 128, rows, 128), F32)]
    return run(temporal_kernel, args, specs, outs, scratch, "temporal_and_mlp")


STEPS = 16


class Refs:
    def __init__(self, names, refs):
        for name, ref in zip(names, refs, strict=True):
            setattr(self, name, ref)


def pair_segments(index, share, clips, places):
    found = []
    for clip in range(clips):
        low = max(index * share, clip * places)
        high = min(index * share + share, clip * places + places)
        if low < high:
            found.append((low - index * share, high - low, clip, low - clip * places))
    return found


class Reduction:
    def __init__(self, r, places, x, y, k, z, rows, width):
        self.r, self.places, self.rows, self.width = r, places, rows, width
        self.x, self.y, self.k, self.z = x, y, k, z
        self.quads = [(f, yy) for f in range(2) for yy in range(2)]
        self.last = 3

    def piece_of(self, s):
        if isinstance(s, int):
            return 2 + s % 2 if s < 8 else 1 if s < 12 else 0
        early, middle = (s < 8).astype(jnp.int32), ((s >= 8) & (s < 12)).astype(jnp.int32)
        return early * (2 + s % 2) + middle

    def tp_of(self, s):
        if isinstance(s, int):
            return 3 * (s // 2 if s < 8 else s) % 4
        early = (s < 8).astype(jnp.int32)
        return (3 * (early * (s // 2) + (1 - early) * s)) % 4

    def spot(self, f, yy, kk, s):
        row = pl.multiple_of((f * 4 + yy * 2 + kk) * self.rows, 16)
        column = pl.multiple_of(self.tp_of(s) * self.width, 128)
        return self.r.w.at[self.piece_of(s), pl.ds(row, self.rows), pl.ds(column, self.width)]

    def remote(self, src, dst, send, recv, side):
        return pltpu.make_async_remote_copy(
            src_ref=src, dst_ref=dst, send_sem=send, recv_sem=recv,
            device_id=self.places[side], device_id_type=MESH,
        )

    def core_copy(self, s, f, yy):
        r = self.r
        return self.remote(
            self.spot(f, yy, 1 - self.k, s), r.r1.at[s, f, yy], r.s1.at[s, f, yy], r.q1s.at[s, f, yy], "core"
        )

    def diag_copy(self, s, side):
        r = self.r
        return self.remote(r.r1.at[s, 1 - self.x, 1 - self.y], r.r2.at[s], r.s2.at[s], r.q2.at[s], side)

    def x_copy(self, s):
        r = self.r
        return self.remote(r.r1.at[s, 1 - self.x, self.y], r.r3x.at[s], r.s3x.at[s], r.q3x.at[s], "x")

    def y_copy(self, s):
        r = self.r
        return self.remote(r.r1.at[s, self.x, 1 - self.y], r.r3y.at[s], r.s3y.at[s], r.q3y.at[s], "y")

    def up_copy(self, s):
        r = self.r
        return self.remote(r.r1.at[s, self.x, self.y], r.rz.at[s], r.sz.at[s], r.qup.at[s], "up")

    def down_copy(self, s, owner=False):
        r = self.r
        target = r.re.at[self.piece_of(s)] if owner else r.rz.at[s]
        return self.remote(r.r1.at[s, self.x, self.y], target, r.sz.at[s], r.qdn.at[s], "down")

    def start(self, s):
        for f, yy in self.quads:
            self.core_copy(s, f, yy).start()

    def even_odd(self, s, even, odd):
        if isinstance(s, int):
            (odd if s % 2 else even)()
        else:
            pl.when(s % 2 == 0)(even)
            pl.when(s % 2 == 1)(odd)

    def chip_sum(self, s):
        r1 = self.r.r1
        for f, yy in self.quads:
            self.core_copy(s, f, yy).wait_recv()
            r1[s, f, yy] = r1[s, f, yy] + self.spot(f, yy, self.k, s)[...]

        def even():
            self.diag_copy(s, "x").start()
            self.x_copy(s).start()

        def odd():
            self.diag_copy(s, "y").start()
            self.y_copy(s).start()

        self.even_odd(s, even, odd)

    def turn(self, s):
        r1, r2, x, y = self.r.r1, self.r.r2, self.x, self.y
        self.diag_copy(s, "x").wait_recv()

        def even():
            r1[s, x, 1 - y] = r1[s, x, 1 - y] + r2[s]
            self.y_copy(s).start()

        def odd():
            r1[s, 1 - x, y] = r1[s, 1 - x, y] + r2[s]
            self.x_copy(s).start()

        self.even_odd(s, even, odd)

    def plane_sum(self, s):
        r = self.r
        self.x_copy(s).wait_recv()
        self.y_copy(s).wait_recv()
        total = r.r1[s, self.x, self.y].astype(F32) + r.r3x[s].astype(F32) + r.r3y[s].astype(F32)
        r.r1[s, self.x, self.y] = total.astype(BF)

    def line(self, s, hop):
        r, x, y, z, last = self.r, self.x, self.y, self.z, self.last
        t = self.tp_of(s)

        @pl.when((z < t) & (z == hop))
        def _():
            if hop > 0:
                self.up_copy(s).wait_recv()
                r.r1[s, x, y] = r.r1[s, x, y] + r.rz[s]
            self.up_copy(s).start()

        @pl.when((z > t) & (last - z == hop))
        def _():
            if hop > 0:
                self.down_copy(s).wait_recv()
                r.r1[s, x, y] = r.r1[s, x, y] + r.rz[s]

            @pl.when(z - 1 == t)
            def _():
                self.down_copy(s, True).start()

            @pl.when(z - 1 != t)
            def _():
                self.down_copy(s).start()

        far = z + (last - 2 * z) * ((last - 2 * z) > 0).astype(jnp.int32)

        @pl.when((z == t) & (far == hop))
        def _():
            piece = self.piece_of(s)
            r.own[piece] = r.r1[s, x, y].astype(F32)

            @pl.when(z > 0)
            def _():
                self.up_copy(s).wait_recv()
                r.own[piece] = r.own[piece] + r.rz[s].astype(F32)

            @pl.when(z < last)
            def _():
                self.down_copy(s, True).wait_recv()
                r.own[piece] = r.own[piece] + r.re[piece].astype(F32)

    def guard(self, action, s, *rest):
        if isinstance(s, int):
            if 0 <= s < STEPS:
                action(s, *rest)
        else:

            @pl.when((s >= 0) & (s < STEPS))
            def _():
                action(s, *rest)

    def tick(self, n):
        self.guard(self.chip_sum, n - 1)
        self.guard(self.turn, n - 3)
        self.guard(self.plane_sum, n - 5)
        for hop in range(4):
            self.guard(self.line, n - 7 - 2 * hop, hop)

    def finish(self):
        def body(s, carry):
            for f, yy in self.quads:
                self.core_copy(s, f, yy).wait_send()
            self.diag_copy(s, "x").wait_send()
            self.x_copy(s).wait_send()
            self.y_copy(s).wait_send()

            @pl.when(self.z != self.tp_of(s))
            def _():
                self.up_copy(s).wait_send()

            return carry

        lax.fori_loop(0, STEPS, body, 0)


STAGES = 7
X_LAST = (3,)
FIRST = [[(0, 0), (1, 0)], [(0, 1)], [(0, 2), (1, 1)], [(0, 3), (1, 2), (2, 0), (0, 4), (1, 3), (3, 0), (0, 5), (1, 4), (2, 1), (0, 6)]]
WITH_SPATIAL = [[(1, 5)], [(3, 1)], [(1, 6)], [(2, 2)]]
WITH_EXCHANGE = [[(3, 2)], [(2, 3)], [(3, 3)]]
WITH_TEMPORAL = [[(2, 4)], [(3, 4)], [(2, 5)], [(3, 5)]]
AT_END = [(2, 6), (3, 6)]


class Gather:
    def __init__(self, r, places, x, y, k, z):
        self.r, self.places, self.x, self.k, self.z = r, places, x, k, z
        self.c = y * 2 + k
        self.rows, self.width = r.shard.shape[1] // 4, r.shard.shape[2]
        self.sends = []
        c, other_y, last = self.c, (1 - y) * 2 + k, 3
        self.stages = [[] for _ in range(STAGES)]

        def wait(stage, unit, when=None):
            self.stages[stage].append(("wait", unit, when))

        def send(stage, side, unit, when=None, mine=False, x_last=None):
            entry = (side, unit, when, mine, x_last, len(self.sends))
            self.sends.append(entry)
            self.stages[stage].append(("send",) + entry)

        me = (x, c, z)
        send(0, "up", me, z < last, True)
        send(0, "down", me, z > 0, True)
        send(0, "x", me, None, True)
        send(0, "x", (x, other_y, z), None, True)
        for d in (1, 2, 3):
            for sign in (-1, 1):
                t = z + sign * d
                have = (t >= 0) if sign < 0 else (t <= last)
                unit = (x, c, t)
                wait(d, unit, have)
                if d < last:
                    if sign < 0:
                        send(d, "up", unit, have & (z < last))
                    else:
                        send(d, "down", unit, have & (z > 0))
                for side in ("x", "y", "core"):
                    send(d, side, unit, have)
            if d == 1:
                wait(1, (1 - x, c, z))
                send(1, "core", (1 - x, c, z))
            if d == 2:
                wait(2, (1 - x, other_y, z))
                send(2, "core", (1 - x, other_y, z))
        for d in (1, 2, 3):
            for sign in (-1, 1):
                t = z + sign * d
                have = (t >= 0) if sign < 0 else (t <= last)
                wait(d + 1, (1 - x, c, t), have)
                send(d + 1, "y", (1 - x, c, t), have, x_last=False)
                send(d + 1, "core", (1 - x, c, t), have)
                wait(d + 1, (x, other_y, t), have)
                send(d + 1, "x", (x, other_y, t), have, x_last=True)
                send(d + 1, "core", (x, other_y, t), have)
                wait(d + 2, (1 - x, other_y, t), have)
                send(d + 2, "core", (1 - x, other_y, t), have)
                for f in (x, 1 - x):
                    for yy in (y, 1 - y):
                        wait(6, (f, yy * 2 + 1 - k, t), have)
        for yy in (y, 1 - y):
            wait(6, (1 - x, yy * 2 + 1 - k, z))

    def spot(self, piece, unit):
        f, cc, t = unit
        row = pl.multiple_of((f * 4 + cc) * self.rows, 16)
        return self.r.w.at[piece, pl.ds(row, self.rows), pl.ds(pl.multiple_of(t * self.width, 128), self.width)]

    def active(self, piece):
        return lambda entry: entry[4] is None or entry[4] == (piece in X_LAST)

    def copy(self, piece, entry):
        side, unit, _, mine, _, number = entry
        f, cc, t = unit
        target = self.spot(piece, unit)
        source = self.r.shard.at[piece, pl.ds(pl.multiple_of(cc * self.rows, 16), self.rows)] if mine else target
        return pltpu.make_async_remote_copy(
            src_ref=source, dst_ref=target,
            send_sem=self.r.ws.at[number, piece], recv_sem=self.r.wq.at[(f * 4 + cc) * 4 + t, piece],
            device_id=self.places[side], device_id_type=MESH,
        )

    def own(self, piece):
        row = pl.multiple_of(self.x * self.rows * 4, 16)
        column = pl.multiple_of(self.z * self.width, 128)
        target = self.r.w.at[piece, pl.ds(row, self.rows * 4), pl.ds(column, self.width)]
        return pltpu.make_async_copy(self.r.shard.at[piece], target, self.r.wl.at[piece])

    def put(self, piece):
        return pltpu.make_async_copy(self.r.w.at[piece], self.r.whole.at[piece], self.r.wo.at[piece])

    def arrived(self, piece, unit):
        f, cc, t = unit
        ref = self.spot(piece, unit)
        pltpu.make_async_copy(ref, ref, self.r.wq.at[(f * 4 + cc) * 4 + t, piece]).wait()

    def stage(self, piece, number):
        if number == 0:
            self.own(piece).start()
        for kind, *rest in self.stages[number]:
            if kind == "wait":
                unit, when = rest
                maybe(when, lambda: self.arrived(piece, unit))
            elif self.active(piece)(rest):
                maybe(rest[2], lambda: self.copy(piece, rest).start())
        if number == STAGES - 1:
            self.own(piece).wait()
            self.put(piece).start()

    def run(self, items):
        for piece, number in items:
            self.stage(piece, number)

    def beside(self, plan):
        def after(i):
            for step, items in enumerate(plan):
                pl.when(i == step)(lambda: self.run(items))

        return after

    def finish(self):
        always = [entry for entry in self.sends if entry[4] is None]

        def body(piece, carry):
            for entry in always:
                maybe(entry[2], lambda: self.copy(piece, entry).wait_send())
            self.put(piece).wait()
            return carry

        lax.fori_loop(0, PIECES, body, 0)
        for piece in range(PIECES):
            for entry in self.sends:
                if entry[4] is not None and self.active(piece)(entry):
                    maybe(entry[2], lambda: self.copy(piece, entry).wait_send())


FORWARD_NAMES = [
    "shard", "bias", "x_in", "g_in", "norm", "ob", "penalty",
    "whole", "x_out", "q0", "k0", "v0", "o0", "p0", "q1", "k1", "v1", "o1", "p1", "rows_out", "third_out", "grad_out",
    "w", "bias_all", "q", "k", "v", "o", "p", "total", "normed", "rows_in", "third", "grad", "mix",
    "x_recv", "g_send", "g_recv", "h_send", "h_recv",
    "ws", "wq", "wl", "wo", "bs", "bq", "xs", "xq", "cs", "cq", "hs", "hq", "keep",
]


def forward_kernel(*refs):
    r = Refs(FORWARD_NAMES, refs)
    x, c, z = lax.axis_index("fsdp"), lax.axis_index("ctx"), lax.axis_index("tp")
    y, k = c // 2, c % 2
    clips, home_places = r.x_in.shape[0], r.x_in.shape[2]
    model = r.x_in.shape[3]
    places = home_places * 4
    frames, share = r.h_recv.shape[:2]
    rows = frames * share
    me = c * 4 + z
    where = places_of(x, y, k, z)

    barrier = pltpu.get_barrier_semaphore()
    pl.semaphore_signal(barrier, inc=1, device_id=where["x"], device_id_type=MESH)

    def greet(d, carry):
        peer = (me + d) % 16
        pl.semaphore_signal(barrier, inc=1, device_id=(x, peer // 4, peer % 4), device_id_type=MESH)
        return carry

    lax.fori_loop(1, 16, greet, 0)
    pl.semaphore_wait(barrier, 16)

    def remote(src, dst, send, recv, place):
        return pltpu.make_async_remote_copy(
            src_ref=src, dst_ref=dst, send_sem=send, recv_sem=recv, device_id=place, device_id_type=MESH
        )

    gather = Gather(r, where, x, y, k, z)
    early = []
    for d in range(1, 4):
        to = (z + d) % 4
        place = (x, c, to)
        early.append(remote(r.x_in.at[:, to], r.x_recv.at[z], r.xs.at[d], r.xq.at[d], place))
        early.append(remote(r.bias, r.bias_all.at[z], r.bs.at[d], r.bq.at[d], place))
    early.append(pltpu.make_async_copy(r.x_in.at[:, z], r.x_recv.at[z], r.xs.at[0]))
    early.append(pltpu.make_async_copy(r.bias, r.bias_all.at[z], r.bs.at[0]))
    for copy in early:
        copy.start()
    gather.run(FIRST[0])

    def share_out(f, carry):
        for clip in range(clips):
            r.third[64 * clip + 64 : 64 * clip + 64 + home_places] = r.g_in[clip, f].astype(F32)
        for to in range(4):
            used = 0
            for start, count, clip, place in pair_segments(to, share, clips, home_places):
                low = 64 * clip + 64 + place
                r.third[start : start + count] = r.third[low : low + count]
                used = start + count
            if used < share:
                r.third[used:share] = jnp.zeros((share - used, model), F32)
            r.g_send[to * 4 + f] = r.third[0:share].astype(BF)
        return carry

    lax.fori_loop(0, 4, share_out, 0)
    gather.run(FIRST[1])
    shares = []
    for d in range(1, 4):
        to = (c + d) % 4
        shares.append(
            remote(r.g_send.at[pl.ds(to * 4, 4)], r.g_recv.at[pl.ds(c * 4, 4)], r.cs.at[d], r.cq.at[d], (x, to, z))
        )
    shares.append(
        pltpu.make_async_copy(r.g_send.at[pl.ds(c * 4, 4)], r.g_recv.at[pl.ds(c * 4, 4)], r.cs.at[0])
    )
    for copy in shares:
        copy.start()
    gather.run(FIRST[2])

    for copy in early:
        copy.wait()
    keep_x = pltpu.make_async_copy(r.x_recv, r.x_out, r.keep.at[0])
    keep_x.start()
    for clip in range(clips):
        for zz in range(4):
            row = clip * SP + zz * home_places
            r.total[row : row + home_places] = r.x_recv[zz, clip].astype(F32)
        r.total[clip * SP + places : clip * SP + SP] = jnp.zeros((SP - places, model), F32)
    norm_into(r.total, r.norm.at[0], r.normed)
    r.total[...] += r.ob[0:1]
    gather.run(FIRST[3])
    att = Attention(clips, SP, spatial_penalty(places), r.w.at[0], r.bias_all.at[:, 0], r.q, r.k, r.v, r.o, spatial_probs(r.p))
    att.forward(r.normed, r.total, gather.beside(WITH_SPATIAL))
    values = (r.q, r.k, r.v, r.o, r.p)
    kept = [
        pltpu.make_async_copy(source, target, r.keep.at[1 + i])
        for i, (source, target) in enumerate(zip(values, (r.q0, r.k0, r.v0, r.o0, r.p0)))
    ]
    for copy in kept:
        copy.start()
    for cc in range(4):
        for zz in range(4):
            used = 0
            for start, count, clip, place in pair_segments(cc, share, clips, home_places):
                row = clip * SP + zz * home_places + place
                r.third[start : start + count] = r.total[row : row + count]
                used = start + count
            if used < share:
                r.third[used:share] = jnp.zeros((share - used, model), F32)
            r.h_send[cc * 4 + zz] = r.third[0:share].astype(BF)

    def to_column(d):
        peer = (me + d) % 16
        return remote(
            r.h_send.at[peer], r.h_recv.at[me], r.hs.at[d], r.hq.at[d], (x, peer // 4, peer % 4)
        )

    def go(d, carry):
        to_column(d).start()
        return carry

    lax.fori_loop(1, 16, go, 0)
    r.h_recv[me] = r.h_send[me]
    for copy in shares:
        copy.wait()
    gather.run(WITH_EXCHANGE[0])
    by_pair(r.g_recv, r.grad, r.mix)
    gather.run(WITH_EXCHANGE[1])

    def come(d, carry):
        to_column(d).wait()
        return carry

    lax.fori_loop(1, 16, come, 0)

    by_pair(r.h_recv, r.rows_in, r.mix)
    normed = r.normed.at[pl.ds(0, rows)]
    norm_into(r.rows_in, r.norm.at[1], normed)
    r.third[...] = r.rows_in[...] + r.ob[1:2]
    for copy in kept:
        copy.wait()
    group = TG * frames
    att = Attention(
        share // TG, group, lambda: r.penalty[...], r.w.at[1], r.bias_all.at[:, 1],
        *(ref.at[:, pl.ds(0, rows)] for ref in (r.q, r.k, r.v)), r.o, small_probs(r.p, group),
    )
    gather.run(WITH_EXCHANGE[2])
    att.forward(normed, r.third, gather.beside(WITH_TEMPORAL))
    gather.run(AT_END)
    kept = [
        pltpu.make_async_copy(source, target, r.keep.at[1 + i])
        for i, (source, target) in enumerate(
            zip(
                values + (r.rows_in, r.third, r.grad),
                (r.q1, r.k1, r.v1, r.o1, r.p1, r.rows_out, r.third_out, r.grad_out),
            )
        )
    ]
    for copy in kept:
        copy.start()
    gather.finish()
    for copy in kept:
        copy.wait()
    keep_x.wait()


def whole_penalty(group, frames):
    row = jnp.arange(3 * group)[:, None] % group // frames
    column = jnp.arange(group)[None] // frames
    return jnp.where(row == column, 0.0, -1e30).astype(F32)


def forward(shard, bias, inputs, cotangent, norm, out_bias, frames, share):
    clips, _, home_places, model = inputs.shape
    rows, srows = frames * share, clips * SP
    args = (shard, bias, inputs, cotangent, norm, out_bias, whole_penalty(TG * frames, frames))
    anywhere, vmem = pl.BlockSpec(memory_space=pl.ANY), pl.BlockSpec(memory_space=pltpu.VMEM)
    whole = (PIECES, shard.shape[1] * 2, shard.shape[2] * 4)
    blocks = (4, clips, home_places, model)
    part, probs = (4, srows, 256), (4, clips, 3 * SP, SP)
    attention = [part] * 4 + [probs]
    outs = [shape(*whole), shape(*blocks)] + [shape(*size) for size in attention * 2]
    outs += [shape(rows, model, dtype=F32)] * 3
    dma = pltpu.SemaphoreType.DMA
    sends = 58
    scratch = (
        [pltpu.VMEM(whole, BF), pltpu.VMEM((4,) + bias.shape, F32)]
        + [pltpu.VMEM(size, BF) for size in attention]
        + [pltpu.VMEM((srows, model), F32), pltpu.VMEM((srows, model), BF)]
        + [pltpu.VMEM((rows, model), F32)] * 3
        + [pltpu.VMEM((model // 128, rows, 128), F32), pltpu.VMEM(blocks, BF)]
        + [pltpu.VMEM((frames, share, model), BF)] * 4
        + [dma((sends, PIECES)), dma((32, PIECES)), dma((PIECES,)), dma((PIECES,))]
        + [dma((4,))] * 6
        + [dma((16,))] * 2
        + [dma((9,))]
    )
    return pl.pallas_call(
        forward_kernel,
        out_shape=outs,
        in_specs=[vmem, vmem, anywhere, vmem, vmem, vmem, vmem],
        out_specs=[anywhere] * len(outs),
        scratch_shapes=scratch,
        compiler_params=pltpu.CompilerParams(
            collective_id=0, has_side_effects=True, vmem_limit_bytes=67043328
        ),
        name="forward",
    )(*args)


BACK_NAMES = [
    "x", "rows_from", "third_from", "grad_from", "whole", "q1", "k1", "v1", "o1", "p1", "q0", "k0", "v0", "o0", "p0",
    "norm", "ub", "db", "y_home", "g_home", "own", "vectors", "w", "q", "k", "v", "o", "p", "rows_in", "total",
    "third", "grad", "gn", "mix", "normed", "normed_t", "branch", "branch_t", "dk", "dv", "y_send",
    "g_send", "g_recv", "home_send", "bias1", "bias0", "ups", "r1", "r2", "r3x", "r3y", "rz", "re", "va",
    "vr", "load", "s1", "q1s", "s2", "q2", "s3x", "s3y", "q3x", "q3y", "sz", "qup", "qdn", "vs", "vq", "ys",
    "yq", "gs", "gq", "hs", "hq", "keep", "early",
]


def back_kernel(*refs):
    r = Refs(BACK_NAMES, refs)
    x, c, z = lax.axis_index("fsdp"), lax.axis_index("ctx"), lax.axis_index("tp")
    y, k = c // 2, c % 2
    _, clips, home_places, model = r.x.shape
    frames, share = r.y_send.shape[:2]
    rows = frames * share
    places = home_places * 4
    me = c * 4 + z
    where = places_of(x, y, k, z)

    barrier = pltpu.get_barrier_semaphore()
    pl.semaphore_signal(barrier, inc=1, device_id=where["x"], device_id_type=MESH)

    def greet(d, carry):
        peer = (me + d) % 16
        pl.semaphore_signal(barrier, inc=1, device_id=(x, peer // 4, peer % 4), device_id_type=MESH)
        return carry

    lax.fori_loop(1, 16, greet, 0)

    loads = [pltpu.make_async_copy(r.whole.at[i], r.w.at[i], r.load.at[i]) for i in range(4)]
    frames_in = r.rows_in.at[pl.ds(0, rows)]
    values = (r.q, r.k, r.v, r.o, r.p)
    early = [
        pltpu.make_async_copy(source, target, r.early.at[i])
        for i, (source, target) in enumerate(
            zip(
                (r.third_from, r.grad_from, r.rows_from, r.q1, r.k1, r.v1, r.o1, r.p1),
                (r.third, r.grad, frames_in) + values,
            )
        )
    ]
    kept = [
        pltpu.make_async_copy(source, target, r.keep.at[i])
        for i, (source, target) in enumerate(zip((r.q0, r.k0, r.v0, r.o0, r.p0), values))
    ]
    for copy in early[:2] + loads[2:] + early[2:] + loads[:2]:
        copy.start()
    spare = r.normed.shape[0] - rows
    for ref in (r.normed, r.branch, r.dk, r.dv):
        ref[rows:] = jnp.zeros((spare, ref.shape[1]), BF)
    r.total[rows:] = jnp.zeros((spare, model), F32)
    early[0].wait()
    early[1].wait()

    norm_into(r.third, r.norm.at[2], r.normed)
    flip_into(r.normed, r.normed_t)
    va = r.va.at[0]
    round_into(r.grad, r.branch, va, 8)
    flip_into(r.branch, r.branch_t)
    r.total[0:rows] = r.third[...] + r.db[...]
    r.gn[...] = jnp.zeros(r.gn.shape, F32)
    loads[2].wait()
    loads[3].wait()
    pl.semaphore_wait(barrier, 16)
    red = Reduction(r, where, x, y, k, z, r.own.shape[1], r.own.shape[2])
    size = r.ub.shape[2]
    halves = r.own.shape[2] // size

    def mlp(i, carry):
        t = (3 * i) % 4
        for half in range(halves):
            j = t * halves + half
            columns = pl.ds(pl.multiple_of(j * size, 128), size)
            up = r.w[2, :, columns]
            down = r.w[3, :, columns]
            hidden = nn(r.normed[...], up) + r.ub[j]
            cdf = 0.5 + 0.5 * lax.erf(hidden * (2.0**-0.5))
            active = (hidden * cdf).astype(BF)
            slope = cdf + hidden * (jnp.exp(-0.5 * hidden * hidden) * ((2.0 * jnp.pi) ** -0.5))
            rounded = (nn(r.branch[...], down) * slope).astype(BF)
            r.ups[j] = jnp.sum(rounded.astype(F32), axis=0, keepdims=True)
            r.total[...] += nt(active, down)
            r.gn[...] += nt(rounded, up)
            r.w[3, :, columns] = nn(r.branch_t[...], active).astype(BF)
            r.w[2, :, columns] = nn(r.normed_t[...], rounded).astype(BF)
        for s in (2 * i, 2 * i + 1):
            red.start(s)
        for s in (2 * i, 2 * i + 1):
            red.tick(s)
        return carry

    lax.fori_loop(0, 4, mlp, 0)

    by_frame(r.total.at[pl.ds(0, rows)], r.y_send, r.mix)
    outs = []
    for d in range(1, 4):
        peer = (c + d) % 4
        copy = pltpu.make_async_remote_copy(
            src_ref=r.y_send.at[pl.ds(peer * 4, 4)], dst_ref=r.y_home.at[c],
            send_sem=r.ys.at[d], recv_sem=r.yq.at[d], device_id=(x, peer, z), device_id_type=MESH,
        )
        copy.start()
        outs.append(copy)
    y_own = pltpu.make_async_copy(r.y_send.at[pl.ds(c * 4, 4)], r.y_home.at[c], r.ys.at[0])
    y_own.start()

    norm_back_into(r.third, r.norm.at[2], r.gn, r.grad, va, 6)
    for copy in early[2:]:
        copy.wait()
    loads[1].wait()
    for t in range(4):
        r.o[t, rows:] = jnp.zeros((spare, r.o.shape[2]), BF)
    group = TG * frames
    att = Attention(
        share // TG, group, None, r.w.at[1], None,
        *(ref.at[:, pl.ds(0, rows)] for ref in (r.q, r.k, r.v)), r.o, small_probs(r.p, group),
    )

    def each(first):
        def after(i):
            red.start(first + i)
            maybe(i > 0 if first == 12 else None, lambda: red.tick(first + i))

        return after

    attention_back(
        att, frames_in, r.grad, r.norm.at[1], r.normed, r.normed_t, r.branch, r.branch_t,
        r.dk, r.dv, r.gn, r.w.at[1], r.bias1, va, 3, each(8),
    )
    for copy in kept:
        copy.start()
    by_frame(r.grad, r.g_send, r.mix)

    def to_frame(d):
        peer = (me + d) % 16
        return pltpu.make_async_remote_copy(
            src_ref=r.g_send.at[peer], dst_ref=r.g_recv.at[me],
            send_sem=r.gs.at[d], recv_sem=r.gq.at[d], device_id=(x, peer // 4, peer % 4), device_id_type=MESH,
        )

    def go(d, carry):
        to_frame(d).start()
        return carry

    lax.fori_loop(1, 16, go, 0)
    r.g_recv[me] = r.g_send[me]
    red.tick(12)
    for copy in kept:
        copy.wait()
    loads[0].wait()
    srows = clips * SP
    for clip in range(clips):
        for zz in range(4):
            row = clip * SP + zz * home_places
            r.rows_in[row : row + home_places] = r.x[zz, clip].astype(F32)
        r.rows_in[pl.ds(clip * SP + places, SP - places)] = jnp.zeros((SP - places, model), F32)
        r.total[pl.ds(clip * SP + places, SP - places)] = jnp.zeros((SP - places, model), F32)

    def come(d, carry):
        to_frame(d).wait()
        return carry

    lax.fori_loop(1, 16, come, 0)
    for cc in range(4):
        for zz in range(4):
            r.third[0:share] = r.g_recv[cc * 4 + zz].astype(F32)
            for start, count, clip, place in pair_segments(cc, share, clips, home_places):
                row = clip * SP + zz * home_places + place
                r.total[row : row + count] = r.third[start : start + count]

    att = Attention(clips, SP, None, r.w.at[0], None, r.q, r.k, r.v, r.o, spatial_probs(r.p))
    attention_back(
        att, r.rows_in, r.total, r.norm.at[0], r.normed, r.normed_t, r.branch, r.branch_t, r.dk, r.dv, r.gn,
        r.w.at[0], r.bias0, va, 0, each(12),
    )
    for zz in range(4):
        for clip in range(clips):
            row = clip * SP + zz * home_places
            r.third[0:home_places] = r.total[row : row + home_places]
            r.home_send[zz, clip] = r.third[0:home_places].astype(BF)
    for d in range(1, 4):
        peer = (z + d) % 4
        copy = pltpu.make_async_remote_copy(
            src_ref=r.home_send.at[peer], dst_ref=r.g_home.at[z],
            send_sem=r.hs.at[d], recv_sem=r.hq.at[d], device_id=(x, c, peer), device_id_type=MESH,
        )
        copy.start()
        outs.append(copy)
    g_own = pltpu.make_async_copy(r.home_send.at[z], r.g_home.at[z], r.hs.at[0])
    g_own.start()

    for j in range(r.ups.shape[0]):
        va[9 + j // halves : 10 + j // halves, (j % halves) * size : (j % halves + 1) * size] = r.ups[j]
    for i, ref in enumerate((r.bias0, r.bias1)):
        for t in range(4):
            va[16 + i * 8 + t * 2 : 18 + i * 8 + t * 2, 0:256] = ref[t]
    sides = ("core", "x", "y", "z1", "z2")

    def v_copy(j):
        return red.remote(r.va.at[j], r.vr.at[j], r.vs.at[j], r.vq.at[j], sides[j])

    v_copy(0).start()

    def rest(n, carry):
        red.tick(n)
        for j in range(5):

            @pl.when(n == STEPS + j)
            def _():
                v_copy(j).wait()
                if j < 4:
                    r.va[j + 1] = r.va[j] + r.vr[j]
                    v_copy(j + 1).start()
                else:
                    r.vectors[...] = r.va[j] + r.vr[j]

        return carry

    lax.fori_loop(STEPS, STEPS + 13, rest, 0)
    red.finish()
    for copy in outs:
        copy.wait()
    y_own.wait()
    g_own.wait()


def backward(x, rows_in, third, grad, whole, kept, norm, up_bias, down_bias, own_rows, width, frames):
    _, clips, home_places, model = x.shape
    rows, srows = third.shape[0], clips * SP
    places, share = home_places * 4, rows // frames
    size = 384
    anywhere, vmem = pl.BlockSpec(memory_space=pl.ANY), pl.BlockSpec(memory_space=pltpu.VMEM)
    args = (x, rows_in, third, grad, whole, *kept, norm, up_bias.reshape(-1, 1, size), down_bias)
    in_specs = [vmem] + [anywhere] * 14 + [vmem] * 3
    sub = (own_rows, width)
    big = max(rows, srows)

    def v(*dims, dtype=BF):
        return pltpu.VMEM(dims, dtype)

    def f(*dims):
        return pltpu.VMEM(dims, F32)

    dma = pltpu.SemaphoreType.DMA
    scratch = (
        [v(*whole.shape)]
        + [v(4, big, 256)] * 4
        + [v(4, clips, 3 * SP, SP)]
        + [f(big, model), f(big, model), f(rows, model), f(rows, model), f(big, model)]
        + [f(model // 128, rows, 128)]
        + [v(big, model), v(model, big), v(big, model), v(model, big), v(big, 256), v(big, 256)]
        + [v(frames, share, model), v(frames, share, model), v(frames, share, model)]
        + [v(4, clips, places // 4, model), f(4, 2, 256), f(4, 2, 256), f(up_bias.shape[0] // size, 1, size)]
        + [v(STEPS, 2, 2, *sub)]
        + [v(STEPS, *sub)] * 4
        + [v(PIECES, *sub)]
        + [f(5, 32, model)] * 2
        + [dma((4,))]
        + [dma((STEPS, 2, 2))] * 2
        + [dma((STEPS,))] * 9
        + [dma((5,))] * 2
        + [dma((4,))] * 2
        + [dma((16,))] * 2
        + [dma((4,))] * 2
        + [dma((5,))]
        + [dma((8,))]
    )
    return pl.pallas_call(
        back_kernel,
        out_shape=(
            shape(4, frames // 4, share, model),
            shape(4, clips, places // 4, model),
            shape(PIECES, *sub, dtype=F32),
            shape(32, model, dtype=F32),
        ),
        in_specs=in_specs,
        out_specs=[anywhere, anywhere, vmem, vmem],
        scratch_shapes=scratch,
        compiler_params=pltpu.CompilerParams(
            collective_id=2, has_side_effects=True, vmem_limit_bytes=67043328
        ),
        name="backward",
    )(*args)


def local(
    inputs,
    cotangent,
    norm_gain,
    norm_bias,
    attn_weight,
    attn_bias,
    out_weight,
    out_bias,
    up_weight,
    up_bias,
    down_weight,
    down_bias,
):
    ranks_c = lax.axis_size("ctx")
    tp_rank = lax.axis_index("tp")
    clips, frames, places, model = inputs.shape
    width = attn_weight.shape[3]

    shard = jnp.concatenate(
        [
            jnp.concatenate(
                [
                    attn_weight.transpose(0, 2, 1, 3).reshape(2, attn_weight.shape[2], 3 * width),
                    out_weight.transpose(0, 2, 1),
                ],
                axis=2,
            ),
            up_weight[None],
            down_weight.T[None],
        ]
    )
    norm = jnp.stack([norm_gain, norm_bias], axis=1)

    pairs = clips * places
    share = -(-pairs // ranks_c)
    share += -share % TG

    def home_to_spatial(values):
        return lax.all_to_all(values, "tp", split_axis=1, concat_axis=2, tiled=True)

    def spatial_to_home(values):
        return lax.all_to_all(values, "tp", split_axis=2, concat_axis=1, tiled=True)

    def home_to_temporal(values):
        rows = values.transpose(1, 0, 2, 3).reshape(frames, pairs, model)
        rows = jnp.pad(rows, ((0, 0), (0, share * ranks_c - pairs), (0, 0)))
        return lax.all_to_all(rows, "ctx", split_axis=1, concat_axis=0, tiled=True)

    def temporal_to_home(values):
        rows = lax.all_to_all(values, "ctx", split_axis=0, concat_axis=1, tiled=True)[:, :pairs]
        return rows.reshape(frames, clips, places, model).transpose(1, 0, 2, 3)

    ups = up_bias.shape[0] // model
    bias = jnp.pad(attn_bias, ((0, 0), (0, 6), (0, 256 - width)))
    if lax.axis_size("fsdp") == 2 and (ranks_c, lax.axis_size("tp")) == (4, 4):
        frames *= ranks_c
        whole, first, *kept = forward(shard, bias, inputs, cotangent, norm, out_bias, frames, share)
        kept, rows = kept[5:10] + kept[:5], kept[10:]
        home, grad_home, own, vectors = backward(
            first, *rows, whole, kept, norm, up_bias, down_bias[None], attn_weight.shape[2] // 4, up_weight.shape[1], frames
        )
        frames //= ranks_c
        outputs = home.transpose(1, 0, 2, 3).reshape(frames, -1, model)[:, :pairs]
        outputs = outputs.reshape(frames, clips, places, model).transpose(1, 0, 2, 3)
        input_grad = grad_home.transpose(1, 0, 2, 3)
        sums = vectors[16:, :256].reshape(2, 4, 2, 256)[..., :width].transpose(0, 2, 1, 3)
        attn_bias_sums = sums.reshape(2, 2, model)
    else:
        whole, bias = gather(shard, bias)
        bias = bias[:, :, :2].transpose(1, 0, 2, 3)
        first = home_to_spatial(inputs)
        spatial_shape = first.shape
        first = first.reshape((-1,) + first.shape[2:])
        second, *kept = spatial_forward(first, whole, bias[0], norm[0], out_bias[0:1])
        second = home_to_temporal(spatial_to_home(second.reshape(spatial_shape)))
        grad_out = home_to_temporal(cotangent)
        result, grad_second, grad_attn1, grad_up, grad_down, bias1, vec1, vec2, grad_up_bias = temporal(
            second, grad_out, whole, bias[1], norm[1], norm[2], out_bias[1:2], up_bias, down_bias[None]
        )
        outputs = temporal_to_home(result)
        grad_second = home_to_spatial(temporal_to_home(grad_second)).reshape(first.shape)
        grad_first, grad_attn0, bias0, vec0 = spatial_back(first, grad_second, whole, norm[0], kept)
        input_grad = spatial_to_home(grad_first.reshape(spatial_shape))
        bias_sums = jnp.stack([bias0, bias1])[..., :width].transpose(0, 2, 1, 3)
        lines = [vec0, vec1, vec2, grad_up_bias, bias_sums]
        flat = jnp.concatenate([line.reshape(-1, model) for line in lines])
        vectors = jnp.pad(flat, ((0, -flat.shape[0] % 8), (0, 0)))
        own, vectors = scatter([grad_attn0, grad_attn1, grad_up, grad_down], vectors)
        attn_bias_sums = vectors[9 + ups : 13 + ups].reshape(2, 2, model)
    triples = vectors[:9].reshape(3, 3, model)
    attn = own[:2].reshape(2, own.shape[1], 4, width)
    return (
        outputs,
        input_grad,
        triples[:, 0],
        triples[:, 1],
        attn[:, :, :3].transpose(0, 2, 1, 3),
        lax.dynamic_slice_in_dim(attn_bias_sums, tp_rank * width, width, 2),
        attn[:, :, 3].transpose(0, 2, 1),
        triples[:2, 2],
        own[2],
        vectors[9 : 9 + ups].reshape(-1),
        own[3].T,
        triples[2, 2],
    )


def solution(mesh):
    return jax.shard_map(
        local,
        mesh=mesh,
        in_specs=(
            P("fsdp", "ctx", "tp", None),
            P("fsdp", "ctx", "tp", None),
            P(),
            P(),
            P(None, None, "fsdp", "tp"),
            P(None, None, "tp"),
            P(None, "tp", "fsdp"),
            P(),
            P("fsdp", "tp"),
            P(),
            P("tp", "fsdp"),
            P(),
        ),
        out_specs=(
            P("fsdp", "ctx", "tp", None),
            P("fsdp", "ctx", "tp", None),
            P(),
            P(),
            P(None, None, ("fsdp", "ctx"), "tp"),
            P(None, None, "tp"),
            P(None, "tp", ("fsdp", "ctx")),
            P(),
            P(("fsdp", "ctx"), "tp"),
            P(),
            P("tp", ("fsdp", "ctx")),
            P(),
        ),
        check_vma=False,
    )
```

```python
import jax
import jax.numpy as jnp
from jax import lax
from jax.experimental import pallas as pl
from jax.experimental.pallas import tpu as pltpu
from jax.sharding import PartitionSpec as P

HEAD = 64
EPSILON = 1e-06
BF = jnp.bfloat16
F32 = jnp.float32
MESH = pl.DeviceIdType.MESH
PIECES = 4
ALL = ("fsdp", "ctx", "tp")


def places_of(x, y, k, z):
    return {
        "x": (1 - x, y * 2 + k, z),
        "y": (x, (1 - y) * 2 + k, z),
        "core": (x, y * 2 + 1 - k, z),
        "up": (x, y * 2 + k, z + 1),
        "down": (x, y * 2 + k, z - 1),
        "z1": (x, y * 2 + k, (z // 2) * 2 + 1 - z % 2),
        "z2": (x, y * 2 + k, (z + 2) % 4),
    }


def maybe(when, action):
    if when is None:
        action()
    else:
        pl.when(when)(action)


def gather(shard, bias):
    part = shard.shape[1] // lax.axis_size("ctx")
    mine = lax.dynamic_slice_in_dim(shard, lax.axis_index("ctx") * part, part, 1)
    tall = lax.all_gather(mine, ("fsdp", "ctx"), axis=1, tiled=True)
    return lax.all_gather(tall, "tp", axis=2, tiled=True), lax.all_gather(bias, "tp")


def scatter(grads, vectors):
    tall = lax.psum_scatter(jnp.concatenate(grads), ("fsdp", "ctx"), scatter_dimension=1, tiled=True)
    own = lax.psum_scatter(tall, "tp", scatter_dimension=2, tiled=True)
    return own.astype(F32), lax.psum(vectors, ALL)


def nn(a, b):
    return lax.dot_general(a, b, (((1,), (0,)), ((), ())), preferred_element_type=F32)


def nt(a, b):
    return lax.dot_general(a, b, (((1,), (1,)), ((), ())), preferred_element_type=F32)


def tn(a, b):
    return lax.dot_general(a, b, (((0,), (0,)), ((), ())), preferred_element_type=F32)


def normalise(rows):
    centre = rows - jnp.mean(rows, axis=-1, keepdims=True)
    scale = lax.rsqrt(jnp.mean(centre * centre, axis=-1, keepdims=True) + EPSILON)
    return centre * scale, scale


def chunks(count):
    size = 80 if count % 80 == 0 else 208
    return size, count // size


def norm_into(source, norm, target):
    size, number = chunks(source.shape[0])

    def body(i, carry):
        span = pl.ds(pl.multiple_of(i * size, 16), size)
        unit, _ = normalise(source[span])
        target[span] = (unit * norm[0:1] + norm[1:2]).astype(BF)
        return carry

    lax.fori_loop(0, number, body, 0)


def norm_back_into(source, norm, grad, total, vec, line):
    size, number = chunks(source.shape[0])
    vec[line : line + 2] = jnp.zeros((2, source.shape[1]), F32)

    def body(i, carry):
        span = pl.ds(pl.multiple_of(i * size, 16), size)
        back, gain, shift = norm_back(source[span], norm[0:1], grad[span])
        total[span] += back
        vec[line : line + 1] += gain
        vec[line + 1 : line + 2] += shift
        return carry

    lax.fori_loop(0, number, body, 0)


def round_into(source, target, vec, line):
    size, number = chunks(source.shape[0])
    vec[line : line + 1] = jnp.zeros((1, source.shape[1]), F32)

    def body(i, carry):
        span = pl.ds(pl.multiple_of(i * size, 16), size)
        rounded = source[span].astype(BF)
        target[span] = rounded
        vec[line : line + 1] += jnp.sum(rounded.astype(F32), axis=0, keepdims=True)
        return carry

    lax.fori_loop(0, number, body, 0)


def flip_into(source, target):
    rows = source.shape[0]
    for low in range(0, rows, 128):
        high = min(rows, low + 128)
        target[:, low:high] = source[low:high].T


def norm_back(rows, gain, grad):
    unit, scale = normalise(rows)
    inner = grad * gain
    mean = jnp.mean(inner, axis=-1, keepdims=True)
    along = jnp.mean(inner * unit, axis=-1, keepdims=True)
    return scale * (inner - mean - unit * along), jnp.sum(grad * unit, axis=0, keepdims=True), jnp.sum(
        grad, axis=0, keepdims=True
    )


def lanes_in(low, high):
    lane = lax.broadcasted_iota(jnp.int32, (1, 256), 1)
    return jnp.where((lane >= low) & (lane < high), 1.0, 0.0)


def stack_heads(values):
    return jnp.concatenate(
        [values * lanes_in(i * HEAD, i * HEAD + HEAD).astype(BF) for i in range(3)], axis=0
    )


def pick_heads(stacked):
    rows = stacked.shape[0] // 3
    return sum(
        stacked[i * rows : (i + 1) * rows] * lanes_in(i * HEAD, i * HEAD + HEAD) for i in range(3)
    )


def shifted(values):
    return pltpu.roll(values, 64, axis=1)


def unshifted(values):
    return pltpu.roll(values, 192, axis=1)


def block(w_ref, t, start, size):
    return w_ref[:, pl.ds(pl.multiple_of(t * (w_ref.shape[1] // 4) + start, 128), size)]


def spatial_probs(ref):
    return lambda t, g: ref.at[t, g]


def small_probs(ref, size):
    def find(t, g):
        row, lane = ((g % 2) * 3 * size, 0) if g < 4 else (0, 128)
        return ref.at[t, g // 2 % 2, pl.ds(row, 3 * size), pl.ds(lane, size)]

    return find


class Attention:
    def __init__(self, groups, rows, penalty, w, bias, q, k, v, o, p):
        self.groups, self.rows, self.penalty = groups, rows, penalty
        self.w, self.bias, self.q, self.k, self.v, self.o, self.p = w, bias, q, k, v, o, p

    def spans(self):
        return [(g, pl.ds(g * self.rows, self.rows)) for g in range(self.groups)]

    def forward(self, normed, total, after=lambda i: None):
        used = lanes_in(0, 192)

        def body(t, carry):
            mixed = nn(normed[...], block(self.w, t, 0, 640))
            self.q[t] = ((mixed[:, :256] + self.bias[t, 0:1]) * used).astype(BF)
            self.k[t] = (unshifted(mixed[:, 128:384]) * used).astype(BF)
            self.v[t] = ((mixed[:, 384:] + self.bias[t, 1:2]) * used).astype(BF)
            for g, span in self.spans():
                scores = nt(stack_heads(self.q[t, span]), self.k[t, span]) * 0.125 + self.penalty()
                weights = jnp.exp(scores - jnp.max(scores, axis=-1, keepdims=True))
                weights = weights * (1.0 / jnp.sum(weights, axis=-1, keepdims=True))
                weights = weights.astype(BF)
                self.p(t, g)[...] = weights
                out = pick_heads(nn(weights, self.v[t, span]))
                self.o[t, span] = shifted(out).astype(BF)
            total[...] += nt(self.o[t, pl.ds(0, self.groups * self.rows)], block(self.w, t, 512, 256))
            after(t)
            return carry

        lax.fori_loop(0, 4, body, 0)

    def backward(self, normed_t, branch, branch_t, dk, dv, grad_normed, grad_w, grad_bias, after):
        used = lanes_in(0, 192)

        def body(i, carry):
            t = (3 * i) % 4
            grad_o = (unshifted(nn(branch[...], block(self.w, t, 512, 256))) * used).astype(BF)
            dq = []
            for g, span in self.spans():
                stacked = stack_heads(grad_o[g * self.rows : (g + 1) * self.rows])
                weights = self.p(t, g)[...]
                probs = weights.astype(F32)
                grad_p = nt(stacked, self.v[t, span])
                inner = jnp.sum(probs * grad_p, axis=-1, keepdims=True)
                grad_s = (probs * (grad_p - inner)).astype(BF)
                dq.append((pick_heads(nn(grad_s, self.k[t, span])) * 0.125).astype(BF))
                dk[span] = shifted(tn(grad_s, stack_heads(self.q[t, span])) * 0.125).astype(BF)
                dv[span] = tn(weights, stacked).astype(BF)
            extra = normed_t.shape[1] - self.groups * self.rows
            if extra:
                dq.append(jnp.zeros((extra, 256), BF))
            dq = jnp.concatenate(dq, axis=0)
            grad_normed[...] += (
                nt(dq, block(self.w, t, 0, 256))
                + nt(dk[...], block(self.w, t, 128, 256))
                + nt(dv[...], block(self.w, t, 384, 256))
            )
            for start, low, high in (
                (0, nn(normed_t[...], dq), nn(normed_t[...], dk[...])),
                (384, nn(normed_t[...], dv[...]), nn(branch_t[...], self.o[t])),
            ):
                columns = pl.multiple_of(t * (self.w.shape[1] // 4) + start, 128)
                grad_w[:, pl.ds(columns, 128)] = low[:, :128].astype(BF)
                grad_w[:, pl.ds(columns + 128, 128)] = (low[:, 128:] + high[:, :128]).astype(BF)
                grad_w[:, pl.ds(columns + 256, 128)] = high[:, 128:].astype(BF)
            grad_bias[t, 0:1] = jnp.sum(dq.astype(F32), axis=0, keepdims=True)
            grad_bias[t, 1:2] = jnp.sum(dv[...].astype(F32), axis=0, keepdims=True)
            after(i)
            return carry

        lax.fori_loop(0, 4, body, 0)


SP = 208


def spatial_penalty(places):
    def penalty():
        lane = lax.broadcasted_iota(jnp.int32, (1, SP), 1)
        return jnp.where(lane < places, 0.0, -1e30)
    return penalty


def spatial_forward_kernel(x_ref, w_ref, bias_ref, norm_ref, ob_ref, h_out, q, k, v, o, p, total, normed):
    clips, places, model = x_ref.shape
    for g in range(clips):
        total[pl.ds(g * SP, places)] = x_ref[g].astype(F32)
        total[pl.ds(g * SP + places, SP - places)] = jnp.zeros((SP - places, model), F32)
        span = pl.ds(g * SP, SP)
        unit, _ = normalise(total[span])
        normed[span] = (unit * norm_ref[0:1] + norm_ref[1:2]).astype(BF)
        total[span] += ob_ref[...]
    att = Attention(clips, SP, spatial_penalty(places), w_ref.at[0], bias_ref, q, k, v, o, spatial_probs(p))
    att.forward(normed, total)
    for g in range(clips):
        h_out[g] = total[pl.ds(g * SP, places)].astype(BF)


def spatial_back_kernel(x_ref, g_ref, w_ref, norm_ref, q, k, v, o, p,
                        gx_out, gw, gbias, gvec, total, normed, normed_t, branch, branch_t, dk, dv, gn, rows_in):
    clips, places, model = x_ref.shape
    for g in range(clips):
        for ref, source in ((rows_in, x_ref), (total, g_ref)):
            ref[pl.ds(g * SP, places)] = source[g].astype(F32)
            ref[pl.ds(g * SP + places, SP - places)] = jnp.zeros((SP - places, model), F32)
    attention_back(Attention(clips, SP, None, w_ref.at[0], None, q, k, v, o, spatial_probs(p)),
                   rows_in, total, norm_ref, normed, normed_t, branch, branch_t, dk, dv, gn, gw.at[0], gbias, gvec, 0, lambda i: None)
    for g in range(clips):
        gx_out[g] = total[pl.ds(g * SP, places)].astype(BF)


def attention_back(
    att, rows_in, total, norm, normed, normed_t, branch, branch_t, dk, dv, gn, grad_w, gbias, vec, line, after
):
    round_into(total, branch, vec, line + 2)
    flip_into(branch, branch_t)
    norm_into(rows_in, norm, normed)
    flip_into(normed, normed_t)
    gn[...] = jnp.zeros(gn.shape, F32)
    att.backward(normed_t, branch, branch_t, dk, dv, gn, grad_w, gbias, after)
    norm_back_into(rows_in, norm, gn, total, vec, line)


def by_pair(source, target, mix):
    frames, pairs, model = source.shape
    for f in range(frames):
        values = source[f].astype(F32)
        for i in range(model // 128):
            mix[i, pl.ds(f, pairs, stride=frames)] = values[:, i * 128 : i * 128 + 128]
    for i in range(model // 128):
        target[:, i * 128 : i * 128 + 128] = mix[i]


def by_frame(source, target, mix):
    frames, pairs, model = target.shape
    for i in range(model // 128):
        mix[i] = source[:, i * 128 : i * 128 + 128]
    for f in range(frames):
        for i in range(model // 128):
            target[f, :, i * 128 : i * 128 + 128] = mix[i, pl.ds(f, pairs, stride=frames)].astype(BF)


TG = 5


def temporal_kernel(h_ref, g_ref, w_ref, u_ref, d_ref, bias_ref, norm_ref, norm2_ref, ob_ref, ub_ref, db_ref, pen_ref,
                    y_out, g_out, gw, gu, gd, gbias, gvec, gvec2, gub,
                    q, k, v, o, p, rows_in, total, third, grad, normed, normed_t, branch, branch_t, dk, dv, gn, mix):
    frames, pairs, model = h_ref.shape
    rows = frames * pairs
    by_pair(h_ref, rows_in, mix)
    by_pair(g_ref, grad, mix)
    unit, _ = normalise(rows_in[...])
    normed[...] = (unit * norm_ref[0:1] + norm_ref[1:2]).astype(BF)
    third[...] = rows_in[...] + ob_ref[...]
    group = TG * frames
    att = Attention(pairs // TG, group, lambda: pen_ref[...], w_ref.at[0], bias_ref, q, k, v, o, spatial_probs(p))
    att.forward(normed, third)
    unit, _ = normalise(third[...])
    n2 = unit * norm2_ref[0:1] + norm2_ref[1:2]
    normed[...] = n2.astype(BF)
    normed_t[...] = n2.T.astype(BF)
    branch[...] = grad[...].astype(BF)
    branch_t[...] = grad[...].T.astype(BF)
    gvec2[2:3] = jnp.sum(grad[...], axis=0, keepdims=True)
    total[...] = third[...] + db_ref[...]
    gn[...] = jnp.zeros_like(gn)
    size = 384
    def mlp(j, carry):
        columns = pl.ds(pl.multiple_of(j * size, 128), size)
        up = u_ref[0, :, columns]
        down = d_ref[0, :, columns]
        hidden = nn(normed[...], up) + ub_ref[j]
        half = 0.5 + 0.5 * lax.erf(hidden * (2.0 ** -0.5))
        active = (hidden * half).astype(BF)
        slope = half + hidden * (jnp.exp(-0.5 * hidden * hidden) * ((2.0 * jnp.pi) ** -0.5))
        grad_hidden = nn(branch[...], down) * slope
        rounded = grad_hidden.astype(BF)
        gub[j] = jnp.sum(rounded.astype(F32), axis=0, keepdims=True)
        total[...] += nt(active, down)
        gn[...] += nt(rounded, up)
        gd[0, :, columns] = nn(branch_t[...], active).astype(BF)
        gu[0, :, columns] = nn(normed_t[...], rounded).astype(BF)
        return carry
    lax.fori_loop(0, u_ref.shape[2] // size, mlp, 0)
    by_frame(total, y_out, mix)
    back, gain, shift = norm_back(third[...], norm2_ref[0:1], gn[...])
    grad[...] += back
    gvec2[0:1] = gain
    gvec2[1:2] = shift
    attention_back(att, rows_in, grad, norm_ref, normed, normed_t, branch, branch_t, dk, dv, gn, gw.at[0], gbias, gvec, 0, lambda i: None)
    by_frame(grad, g_out, mix)


def piece_spec(piece, whole):
    return pl.BlockSpec((1,) + whole.shape[1:], lambda i: (piece, 0, 0))


def full_spec(value):
    return pl.BlockSpec(value.shape, lambda i: (0,) * len(value.shape))


def run(kernel, args, specs, outs, scratch, name):
    return pl.pallas_call(
        kernel, grid=(1,),
        out_shape=outs, in_specs=specs, out_specs=[full_spec(out) for out in outs], scratch_shapes=scratch,
        compiler_params=pltpu.CompilerParams(vmem_limit_bytes=63 * 2**20),
        name=name,
    )(*args)


def shape(*size, dtype=BF):
    return jax.ShapeDtypeStruct(size, dtype)


def spatial_forward(x, whole, bias, norm, out_bias):
    clips, places, model = x.shape
    rows = clips * SP
    args = (x, whole, bias, norm, out_bias)
    specs = [full_spec(a) for a in args]
    specs[1] = piece_spec(0, whole)
    outs = [shape(clips, places, model)] + [shape(4, rows, 256)] * 4 + [shape(4, clips, 3 * SP, SP)]
    return run(spatial_forward_kernel, args, specs, outs,
               [pltpu.VMEM((rows, model), F32), pltpu.VMEM((rows, model), BF)], "spatial_forward")


def spatial_back(x, g, whole, norm, kept):
    clips, places, model = x.shape
    rows = clips * SP
    args = (x, g, whole, norm) + tuple(kept)
    specs = [full_spec(a) for a in args]
    specs[2] = piece_spec(0, whole)
    outs = [shape(clips, places, model), shape(1, *whole.shape[1:]), shape(4, 2, 256, dtype=F32), shape(3, model, dtype=F32)]
    scratch = [pltpu.VMEM((rows, model), F32), pltpu.VMEM((rows, model), BF), pltpu.VMEM((model, rows), BF), pltpu.VMEM((rows, model), BF),
               pltpu.VMEM((model, rows), BF), pltpu.VMEM((rows, 256), BF), pltpu.VMEM((rows, 256), BF),
               pltpu.VMEM((rows, model), F32), pltpu.VMEM((rows, model), F32)]
    return run(spatial_back_kernel, args, specs, outs, scratch, "spatial_back")


def temporal(h, g, whole, bias, norm, norm2, out_bias, up_bias, down_bias):
    frames, pairs, model = h.shape
    rows = frames * pairs
    group = TG * frames
    row = jnp.arange(3 * group)[:, None] % group // frames
    column = jnp.arange(group)[None] // frames
    penalty = jnp.where(row == column, 0.0, -1e30).astype(F32)
    args = (h, g, whole, whole, whole, bias, norm, norm2, out_bias, up_bias.reshape(-1, 1, 384), down_bias, penalty)
    specs = [full_spec(a) for a in args]
    for i, piece in ((2, 1), (3, 2), (4, 3)):
        specs[i] = piece_spec(piece, whole)
    hidden = whole.shape[2]
    outs = [shape(frames, pairs, model), shape(frames, pairs, model), shape(1, model, hidden), shape(1, model, hidden),
            shape(1, model, hidden), shape(4, 2, 256, dtype=F32), shape(3, model, dtype=F32), shape(3, model, dtype=F32),
            shape(hidden // 384, 1, 384, dtype=F32)]
    big = pltpu.VMEM((rows, model), F32)
    low = pltpu.VMEM((rows, model), BF)
    flip = pltpu.VMEM((model, rows), BF)
    part = pltpu.VMEM((rows, 256), BF)
    scratch = [pltpu.VMEM((4, rows, 256), BF)] * 4 + [pltpu.VMEM((4, pairs // TG, 3 * group, group), BF)] + [
        big, big, big, big, low, flip, low, flip, part, part, big, pltpu.VMEM((model // 128, rows, 128), F32)]
    return run(temporal_kernel, args, specs, outs, scratch, "temporal_and_mlp")


STEPS = 16


class Refs:
    def __init__(self, names, refs):
        for name, ref in zip(names, refs, strict=True):
            setattr(self, name, ref)


def pair_segments(index, share, clips, places):
    found = []
    for clip in range(clips):
        low = max(index * share, clip * places)
        high = min(index * share + share, clip * places + places)
        if low < high:
            found.append((low - index * share, high - low, clip, low - clip * places))
    return found


class Reduction:
    def __init__(self, r, places, x, y, k, z, rows, width):
        self.r, self.places, self.rows, self.width = r, places, rows, width
        self.x, self.y, self.k, self.z = x, y, k, z
        self.quads = [(f, yy) for f in range(2) for yy in range(2)]
        self.last = 3

    def piece_of(self, s):
        if isinstance(s, int):
            return 2 + s % 2 if s < 8 else 1 if s < 12 else 0
        early, middle = (s < 8).astype(jnp.int32), ((s >= 8) & (s < 12)).astype(jnp.int32)
        return early * (2 + s % 2) + middle

    def tp_of(self, s):
        if isinstance(s, int):
            return 3 * (s // 2 if s < 8 else s) % 4
        early = (s < 8).astype(jnp.int32)
        return (3 * (early * (s // 2) + (1 - early) * s)) % 4

    def spot(self, f, yy, kk, s):
        row = pl.multiple_of((f * 4 + yy * 2 + kk) * self.rows, 16)
        column = pl.multiple_of(self.tp_of(s) * self.width, 128)
        return self.r.w.at[self.piece_of(s), pl.ds(row, self.rows), pl.ds(column, self.width)]

    def remote(self, src, dst, send, recv, side):
        return pltpu.make_async_remote_copy(
            src_ref=src, dst_ref=dst, send_sem=send, recv_sem=recv,
            device_id=self.places[side], device_id_type=MESH,
        )

    def core_copy(self, s, f, yy):
        r = self.r
        return self.remote(
            self.spot(f, yy, 1 - self.k, s), r.r1.at[s, f, yy], r.s1.at[s, f, yy], r.q1s.at[s, f, yy], "core"
        )

    def diag_copy(self, s, side):
        r = self.r
        return self.remote(r.r1.at[s, 1 - self.x, 1 - self.y], r.r2.at[s], r.s2.at[s], r.q2.at[s], side)

    def x_copy(self, s):
        r = self.r
        return self.remote(r.r1.at[s, 1 - self.x, self.y], r.r3x.at[s], r.s3x.at[s], r.q3x.at[s], "x")

    def y_copy(self, s):
        r = self.r
        return self.remote(r.r1.at[s, self.x, 1 - self.y], r.r3y.at[s], r.s3y.at[s], r.q3y.at[s], "y")

    def up_copy(self, s):
        r = self.r
        return self.remote(r.r1.at[s, self.x, self.y], r.rz.at[s], r.sz.at[s], r.qup.at[s], "up")

    def down_copy(self, s, owner=False):
        r = self.r
        target = r.re.at[self.piece_of(s)] if owner else r.rz.at[s]
        return self.remote(r.r1.at[s, self.x, self.y], target, r.sz.at[s], r.qdn.at[s], "down")

    def start(self, s):
        for f, yy in self.quads:
            self.core_copy(s, f, yy).start()

    def even_odd(self, s, even, odd):
        if isinstance(s, int):
            (odd if s % 2 else even)()
        else:
            pl.when(s % 2 == 0)(even)
            pl.when(s % 2 == 1)(odd)

    def chip_sum(self, s):
        r1 = self.r.r1
        for f, yy in self.quads:
            self.core_copy(s, f, yy).wait_recv()
            r1[s, f, yy] = r1[s, f, yy] + self.spot(f, yy, self.k, s)[...]

        def even():
            self.diag_copy(s, "x").start()
            self.x_copy(s).start()

        def odd():
            self.diag_copy(s, "y").start()
            self.y_copy(s).start()

        self.even_odd(s, even, odd)

    def turn(self, s):
        r1, r2, x, y = self.r.r1, self.r.r2, self.x, self.y
        self.diag_copy(s, "x").wait_recv()

        def even():
            r1[s, x, 1 - y] = r1[s, x, 1 - y] + r2[s]
            self.y_copy(s).start()

        def odd():
            r1[s, 1 - x, y] = r1[s, 1 - x, y] + r2[s]
            self.x_copy(s).start()

        self.even_odd(s, even, odd)

    def plane_sum(self, s):
        r = self.r
        self.x_copy(s).wait_recv()
        self.y_copy(s).wait_recv()
        total = r.r1[s, self.x, self.y].astype(F32) + r.r3x[s].astype(F32) + r.r3y[s].astype(F32)
        r.r1[s, self.x, self.y] = total.astype(BF)

    def line(self, s, hop):
        r, x, y, z, last = self.r, self.x, self.y, self.z, self.last
        t = self.tp_of(s)

        @pl.when((z < t) & (z == hop))
        def _():
            if hop > 0:
                self.up_copy(s).wait_recv()
                r.r1[s, x, y] = r.r1[s, x, y] + r.rz[s]
            self.up_copy(s).start()

        @pl.when((z > t) & (last - z == hop))
        def _():
            if hop > 0:
                self.down_copy(s).wait_recv()
                r.r1[s, x, y] = r.r1[s, x, y] + r.rz[s]

            @pl.when(z - 1 == t)
            def _():
                self.down_copy(s, True).start()

            @pl.when(z - 1 != t)
            def _():
                self.down_copy(s).start()

        far = z + (last - 2 * z) * ((last - 2 * z) > 0).astype(jnp.int32)

        @pl.when((z == t) & (far == hop))
        def _():
            piece = self.piece_of(s)
            r.own[piece] = r.r1[s, x, y].astype(F32)

            @pl.when(z > 0)
            def _():
                self.up_copy(s).wait_recv()
                r.own[piece] = r.own[piece] + r.rz[s].astype(F32)

            @pl.when(z < last)
            def _():
                self.down_copy(s, True).wait_recv()
                r.own[piece] = r.own[piece] + r.re[piece].astype(F32)

    def guard(self, action, s, *rest):
        if isinstance(s, int):
            if 0 <= s < STEPS:
                action(s, *rest)
        else:

            @pl.when((s >= 0) & (s < STEPS))
            def _():
                action(s, *rest)

    def tick(self, n):
        self.guard(self.chip_sum, n - 1)
        self.guard(self.turn, n - 3)
        self.guard(self.plane_sum, n - 5)
        for hop in range(4):
            self.guard(self.line, n - 7 - 2 * hop, hop)

    def finish(self):
        def body(s, carry):
            for f, yy in self.quads:
                self.core_copy(s, f, yy).wait_send()
            self.diag_copy(s, "x").wait_send()
            self.x_copy(s).wait_send()
            self.y_copy(s).wait_send()

            @pl.when(self.z != self.tp_of(s))
            def _():
                self.up_copy(s).wait_send()

            return carry

        lax.fori_loop(0, STEPS, body, 0)


STAGES = 7
X_LAST = ()
WIDE = (3,)
FIRST = [[(0, 0), (1, 0)], [(0, 1)], [(0, 2), (1, 1)], [(0, 3), (1, 2), (2, 0), (0, 4), (1, 3), (3, 0), (0, 5), (1, 4), (2, 1), (0, 6)]]
WITH_SPATIAL = [[(1, 5)], [(3, 1)], [(1, 6)], [(2, 2)]]
WITH_EXCHANGE = [[(3, 2)], [(2, 3)], [(3, 3)]]
WITH_TEMPORAL = [[(2, 4)], [(3, 4)], [(2, 5)], [(3, 5)]]
AT_END = [(2, 6), (3, 6)]


class Gather:
    def __init__(self, r, places, x, y, k, z):
        self.r, self.places, self.x, self.k, self.z = r, places, x, k, z
        self.c = y * 2 + k
        self.rows, self.width = r.shard.shape[1] // 4, r.shard.shape[2]
        self.sends = []
        c, other_y, last = self.c, (1 - y) * 2 + k, 3
        self.stages = [[] for _ in range(STAGES)]

        def wait(stage, unit, when=None, use=None):
            self.stages[stage].append(("wait", unit, when, use))

        def send(stage, side, unit, when=None, mine=False, use=None):
            entry = (side, unit, when, mine, use, len(self.sends))
            self.sends.append(entry)
            self.stages[stage].append(("send",) + entry)

        def wide(piece):
            return piece in WIDE

        def narrow(piece):
            return piece not in WIDE

        def x_last(piece):
            return piece in X_LAST

        def y_last(piece):
            return piece not in X_LAST

        me, beside = (x, c, z), (x, other_y, z)
        send(0, "up", me, z < last, True)
        send(0, "down", me, z > 0, True)
        send(0, "x", me, None, True)
        send(0, "up", beside, z < last, True, wide)
        send(0, "down", beside, z > 0, True, wide)
        send(0, "x", beside, None, True)
        for d in (1, 2, 3):
            for sign in (-1, 1):
                t = z + sign * d
                have = (t >= 0) if sign < 0 else (t <= last)
                for unit, use in (((x, c, t), None), ((x, other_y, t), wide)):
                    wait(d, unit, have, use)
                    if d < last:
                        if sign < 0:
                            send(d, "up", unit, have & (z < last), use=use)
                        else:
                            send(d, "down", unit, have & (z > 0), use=use)
                for side in ("x", "y", "core"):
                    send(d, side, (x, c, t), have, use=narrow if side == "y" else None)
            if d == 1:
                wait(1, (1 - x, c, z))
                send(1, "core", (1 - x, c, z))
            if d == 2:
                wait(2, (1 - x, other_y, z))
                send(2, "core", (1 - x, other_y, z))
        for d in (1, 2, 3):
            for sign in (-1, 1):
                t = z + sign * d
                have = (t >= 0) if sign < 0 else (t <= last)
                wait(d + 1, (1 - x, c, t), have)
                send(d + 1, "y", (1 - x, c, t), have, use=y_last)
                send(d + 1, "core", (1 - x, c, t), have)
                wait(d + 1, (x, other_y, t), have, narrow)
                send(d + 1, "x", (x, other_y, t), have, use=x_last)
                send(d + 1, "core", (x, other_y, t), have)
                wait(d + 2, (1 - x, other_y, t), have)
                send(d + 2, "core", (1 - x, other_y, t), have)
                for f in (x, 1 - x):
                    for yy in (y, 1 - y):
                        wait(6, (f, yy * 2 + 1 - k, t), have)
        for yy in (y, 1 - y):
            wait(6, (1 - x, yy * 2 + 1 - k, z))

    def spot(self, piece, unit):
        f, cc, t = unit
        row = pl.multiple_of((f * 4 + cc) * self.rows, 16)
        return self.r.w.at[piece, pl.ds(row, self.rows), pl.ds(pl.multiple_of(t * self.width, 128), self.width)]

    def copy(self, piece, entry):
        side, unit, _, mine, _, number = entry
        f, cc, t = unit
        target = self.spot(piece, unit)
        source = self.r.shard.at[piece, pl.ds(pl.multiple_of(cc * self.rows, 16), self.rows)] if mine else target
        return pltpu.make_async_remote_copy(
            src_ref=source, dst_ref=target,
            send_sem=self.r.ws.at[number, piece], recv_sem=self.r.wq.at[(f * 4 + cc) * 4 + t, piece],
            device_id=self.places[side], device_id_type=MESH,
        )

    def own(self, piece):
        row = pl.multiple_of(self.x * self.rows * 4, 16)
        column = pl.multiple_of(self.z * self.width, 128)
        target = self.r.w.at[piece, pl.ds(row, self.rows * 4), pl.ds(column, self.width)]
        return pltpu.make_async_copy(self.r.shard.at[piece], target, self.r.wl.at[piece])

    def put(self, piece):
        return pltpu.make_async_copy(self.r.w.at[piece], self.r.whole.at[piece], self.r.wo.at[piece])

    def arrived(self, piece, unit):
        f, cc, t = unit
        ref = self.spot(piece, unit)
        pltpu.make_async_copy(ref, ref, self.r.wq.at[(f * 4 + cc) * 4 + t, piece]).wait()

    def stage(self, piece, number):
        if number == 0:
            self.own(piece).start()
        for kind, *rest in self.stages[number]:
            if kind == "wait":
                unit, when, use = rest
                if use is None or use(piece):
                    maybe(when, lambda: self.arrived(piece, unit))
            elif rest[4] is None or rest[4](piece):
                maybe(rest[2], lambda: self.copy(piece, rest).start())
        if number == STAGES - 1:
            self.own(piece).wait()
            self.put(piece).start()

    def run(self, items):
        for piece, number in items:
            self.stage(piece, number)

    def beside(self, plan):
        def after(i):
            for step, items in enumerate(plan):
                pl.when(i == step)(lambda: self.run(items))

        return after

    def finish(self):
        always = [entry for entry in self.sends if entry[4] is None]

        def body(piece, carry):
            for entry in always:
                maybe(entry[2], lambda: self.copy(piece, entry).wait_send())
            self.put(piece).wait()
            return carry

        lax.fori_loop(0, PIECES, body, 0)
        for piece in range(PIECES):
            for entry in self.sends:
                if entry[4] is not None and entry[4](piece):
                    maybe(entry[2], lambda: self.copy(piece, entry).wait_send())


FORWARD_NAMES = [
    "shard", "bias", "x_in", "g_in", "norm", "ob", "penalty",
    "whole", "x_out", "q0", "k0", "v0", "o0", "p0", "q1", "k1", "v1", "o1", "p1", "rows_out", "third_out", "grad_out",
    "w", "bias_all", "q", "k", "v", "o", "p", "total", "normed", "rows_in", "third", "grad", "mix",
    "x_recv", "g_send", "g_recv", "h_send", "h_recv",
    "ws", "wq", "wl", "wo", "bs", "bq", "xs", "xq", "cs", "cq", "hs", "hq", "keep",
]


def forward_kernel(*refs):
    r = Refs(FORWARD_NAMES, refs)
    x, c, z = lax.axis_index("fsdp"), lax.axis_index("ctx"), lax.axis_index("tp")
    y, k = c // 2, c % 2
    clips, home_places = r.x_in.shape[0], r.x_in.shape[2]
    model = r.x_in.shape[3]
    places = home_places * 4
    frames, share = r.h_recv.shape[:2]
    rows = frames * share
    me = c * 4 + z
    where = places_of(x, y, k, z)

    barrier = pltpu.get_barrier_semaphore()
    pl.semaphore_signal(barrier, inc=1, device_id=where["x"], device_id_type=MESH)

    def greet(d, carry):
        peer = (me + d) % 16
        pl.semaphore_signal(barrier, inc=1, device_id=(x, peer // 4, peer % 4), device_id_type=MESH)
        return carry

    lax.fori_loop(1, 16, greet, 0)
    pl.semaphore_wait(barrier, 16)

    def remote(src, dst, send, recv, place):
        return pltpu.make_async_remote_copy(
            src_ref=src, dst_ref=dst, send_sem=send, recv_sem=recv, device_id=place, device_id_type=MESH
        )

    gather = Gather(r, where, x, y, k, z)
    early = []
    for d in range(1, 4):
        to = (z + d) % 4
        place = (x, c, to)
        early.append(remote(r.x_in.at[:, to], r.x_recv.at[z], r.xs.at[d], r.xq.at[d], place))
        early.append(remote(r.bias, r.bias_all.at[z], r.bs.at[d], r.bq.at[d], place))
    early.append(pltpu.make_async_copy(r.x_in.at[:, z], r.x_recv.at[z], r.xs.at[0]))
    early.append(pltpu.make_async_copy(r.bias, r.bias_all.at[z], r.bs.at[0]))
    for copy in early:
        copy.start()
    gather.run(FIRST[0])

    def share_out(f, carry):
        for clip in range(clips):
            r.third[64 * clip + 64 : 64 * clip + 64 + home_places] = r.g_in[clip, f].astype(F32)
        for to in range(4):
            used = 0
            for start, count, clip, place in pair_segments(to, share, clips, home_places):
                low = 64 * clip + 64 + place
                r.third[start : start + count] = r.third[low : low + count]
                used = start + count
            if used < share:
                r.third[used:share] = jnp.zeros((share - used, model), F32)
            r.g_send[to * 4 + f] = r.third[0:share].astype(BF)
        return carry

    lax.fori_loop(0, 4, share_out, 0)
    gather.run(FIRST[1])
    shares = []
    for d in range(1, 4):
        to = (c + d) % 4
        shares.append(
            remote(r.g_send.at[pl.ds(to * 4, 4)], r.g_recv.at[pl.ds(c * 4, 4)], r.cs.at[d], r.cq.at[d], (x, to, z))
        )
    shares.append(
        pltpu.make_async_copy(r.g_send.at[pl.ds(c * 4, 4)], r.g_recv.at[pl.ds(c * 4, 4)], r.cs.at[0])
    )
    for copy in shares:
        copy.start()
    gather.run(FIRST[2])

    for copy in early:
        copy.wait()
    keep_x = pltpu.make_async_copy(r.x_recv, r.x_out, r.keep.at[0])
    keep_x.start()
    for clip in range(clips):
        for zz in range(4):
            row = clip * SP + zz * home_places
            r.total[row : row + home_places] = r.x_recv[zz, clip].astype(F32)
        r.total[clip * SP + places : clip * SP + SP] = jnp.zeros((SP - places, model), F32)
    norm_into(r.total, r.norm.at[0], r.normed)
    r.total[...] += r.ob[0:1]
    gather.run(FIRST[3])
    att = Attention(clips, SP, spatial_penalty(places), r.w.at[0], r.bias_all.at[:, 0], r.q, r.k, r.v, r.o, spatial_probs(r.p))
    att.forward(r.normed, r.total, gather.beside(WITH_SPATIAL))
    values = (r.q, r.k, r.v, r.o, r.p)
    kept = [
        pltpu.make_async_copy(source, target, r.keep.at[1 + i])
        for i, (source, target) in enumerate(zip(values, (r.q0, r.k0, r.v0, r.o0, r.p0)))
    ]
    for copy in kept:
        copy.start()
    for cc in range(4):
        for zz in range(4):
            used = 0
            for start, count, clip, place in pair_segments(cc, share, clips, home_places):
                row = clip * SP + zz * home_places + place
                r.third[start : start + count] = r.total[row : row + count]
                used = start + count
            if used < share:
                r.third[used:share] = jnp.zeros((share - used, model), F32)
            r.h_send[cc * 4 + zz] = r.third[0:share].astype(BF)

    def to_column(d):
        peer = (me + d) % 16
        return remote(
            r.h_send.at[peer], r.h_recv.at[me], r.hs.at[d], r.hq.at[d], (x, peer // 4, peer % 4)
        )

    def go(d, carry):
        to_column(d).start()
        return carry

    lax.fori_loop(1, 16, go, 0)
    r.h_recv[me] = r.h_send[me]
    for copy in shares:
        copy.wait()
    gather.run(WITH_EXCHANGE[0])
    by_pair(r.g_recv, r.grad, r.mix)
    gather.run(WITH_EXCHANGE[1])

    def come(d, carry):
        to_column(d).wait()
        return carry

    lax.fori_loop(1, 16, come, 0)

    by_pair(r.h_recv, r.rows_in, r.mix)
    normed = r.normed.at[pl.ds(0, rows)]
    norm_into(r.rows_in, r.norm.at[1], normed)
    r.third[...] = r.rows_in[...] + r.ob[1:2]
    for copy in kept:
        copy.wait()
    group = TG * frames
    att = Attention(
        share // TG, group, lambda: r.penalty[...], r.w.at[1], r.bias_all.at[:, 1],
        *(ref.at[:, pl.ds(0, rows)] for ref in (r.q, r.k, r.v)), r.o, small_probs(r.p, group),
    )
    gather.run(WITH_EXCHANGE[2])
    att.forward(normed, r.third, gather.beside(WITH_TEMPORAL))
    gather.run(AT_END)
    kept = [
        pltpu.make_async_copy(source, target, r.keep.at[1 + i])
        for i, (source, target) in enumerate(
            zip(
                values + (r.rows_in, r.third, r.grad),
                (r.q1, r.k1, r.v1, r.o1, r.p1, r.rows_out, r.third_out, r.grad_out),
            )
        )
    ]
    for copy in kept:
        copy.start()
    gather.finish()
    for copy in kept:
        copy.wait()
    keep_x.wait()


def whole_penalty(group, frames):
    row = jnp.arange(3 * group)[:, None] % group // frames
    column = jnp.arange(group)[None] // frames
    return jnp.where(row == column, 0.0, -1e30).astype(F32)


def forward(shard, bias, inputs, cotangent, norm, out_bias, frames, share):
    clips, _, home_places, model = inputs.shape
    rows, srows = frames * share, clips * SP
    args = (shard, bias, inputs, cotangent, norm, out_bias, whole_penalty(TG * frames, frames))
    anywhere, vmem = pl.BlockSpec(memory_space=pl.ANY), pl.BlockSpec(memory_space=pltpu.VMEM)
    whole = (PIECES, shard.shape[1] * 2, shard.shape[2] * 4)
    blocks = (4, clips, home_places, model)
    part, probs = (4, srows, 256), (4, clips, 3 * SP, SP)
    attention = [part] * 4 + [probs]
    outs = [shape(*whole), shape(*blocks)] + [shape(*size) for size in attention * 2]
    outs += [shape(rows, model, dtype=F32)] * 3
    dma = pltpu.SemaphoreType.DMA
    sends = 68
    scratch = (
        [pltpu.VMEM(whole, BF), pltpu.VMEM((4,) + bias.shape, F32)]
        + [pltpu.VMEM(size, BF) for size in attention]
        + [pltpu.VMEM((srows, model), F32), pltpu.VMEM((srows, model), BF)]
        + [pltpu.VMEM((rows, model), F32)] * 3
        + [pltpu.VMEM((model // 128, rows, 128), F32), pltpu.VMEM(blocks, BF)]
        + [pltpu.VMEM((frames, share, model), BF)] * 4
        + [dma((sends, PIECES)), dma((32, PIECES)), dma((PIECES,)), dma((PIECES,))]
        + [dma((4,))] * 6
        + [dma((16,))] * 2
        + [dma((9,))]
    )
    return pl.pallas_call(
        forward_kernel,
        out_shape=outs,
        in_specs=[vmem, vmem, anywhere, vmem, vmem, vmem, vmem],
        out_specs=[anywhere] * len(outs),
        scratch_shapes=scratch,
        compiler_params=pltpu.CompilerParams(
            collective_id=0, has_side_effects=True, vmem_limit_bytes=67043328
        ),
        name="forward",
    )(*args)


BACK_NAMES = [
    "x", "rows_from", "third_from", "grad_from", "whole", "q1", "k1", "v1", "o1", "p1", "q0", "k0", "v0", "o0", "p0",
    "norm", "ub", "db", "y_home", "g_home", "own", "vectors", "w", "q", "k", "v", "o", "p", "rows_in", "total",
    "third", "grad", "gn", "mix", "normed", "normed_t", "branch", "branch_t", "dk", "dv", "y_send",
    "g_send", "g_recv", "home_send", "bias1", "bias0", "ups", "r1", "r2", "r3x", "r3y", "rz", "re", "va",
    "vr", "load", "s1", "q1s", "s2", "q2", "s3x", "s3y", "q3x", "q3y", "sz", "qup", "qdn", "vs", "vq", "ys",
    "yq", "gs", "gq", "hs", "hq", "keep", "early",
]


def back_kernel(*refs):
    r = Refs(BACK_NAMES, refs)
    x, c, z = lax.axis_index("fsdp"), lax.axis_index("ctx"), lax.axis_index("tp")
    y, k = c // 2, c % 2
    _, clips, home_places, model = r.x.shape
    frames, share = r.y_send.shape[:2]
    rows = frames * share
    places = home_places * 4
    me = c * 4 + z
    where = places_of(x, y, k, z)

    barrier = pltpu.get_barrier_semaphore()
    pl.semaphore_signal(barrier, inc=1, device_id=where["x"], device_id_type=MESH)

    def greet(d, carry):
        peer = (me + d) % 16
        pl.semaphore_signal(barrier, inc=1, device_id=(x, peer // 4, peer % 4), device_id_type=MESH)
        return carry

    lax.fori_loop(1, 16, greet, 0)

    loads = [pltpu.make_async_copy(r.whole.at[i], r.w.at[i], r.load.at[i]) for i in range(4)]
    frames_in = r.rows_in.at[pl.ds(0, rows)]
    values = (r.q, r.k, r.v, r.o, r.p)
    early = [
        pltpu.make_async_copy(source, target, r.early.at[i])
        for i, (source, target) in enumerate(
            zip(
                (r.third_from, r.grad_from, r.rows_from, r.q1, r.k1, r.v1, r.o1, r.p1),
                (r.third, r.grad, frames_in) + values,
            )
        )
    ]
    kept = [
        pltpu.make_async_copy(source, target, r.keep.at[i])
        for i, (source, target) in enumerate(zip((r.q0, r.k0, r.v0, r.o0, r.p0), values))
    ]
    for copy in early[:2] + loads[2:] + early[2:] + loads[:2]:
        copy.start()
    spare = r.normed.shape[0] - rows
    for ref in (r.normed, r.branch, r.dk, r.dv):
        ref[rows:] = jnp.zeros((spare, ref.shape[1]), BF)
    r.total[rows:] = jnp.zeros((spare, model), F32)
    early[0].wait()
    early[1].wait()

    norm_into(r.third, r.norm.at[2], r.normed)
    flip_into(r.normed, r.normed_t)
    va = r.va.at[0]
    round_into(r.grad, r.branch, va, 8)
    flip_into(r.branch, r.branch_t)
    r.total[0:rows] = r.third[...] + r.db[...]
    r.gn[...] = jnp.zeros(r.gn.shape, F32)
    loads[2].wait()
    loads[3].wait()
    pl.semaphore_wait(barrier, 16)
    red = Reduction(r, where, x, y, k, z, r.own.shape[1], r.own.shape[2])
    size = r.ub.shape[2]
    halves = r.own.shape[2] // size

    def mlp(i, carry):
        t = (3 * i) % 4
        for half in range(halves):
            j = t * halves + half
            columns = pl.ds(pl.multiple_of(j * size, 128), size)
            up = r.w[2, :, columns]
            down = r.w[3, :, columns]
            hidden = nn(r.normed[...], up) + r.ub[j]
            cdf = 0.5 + 0.5 * lax.erf(hidden * (2.0**-0.5))
            active = (hidden * cdf).astype(BF)
            slope = cdf + hidden * (jnp.exp(-0.5 * hidden * hidden) * ((2.0 * jnp.pi) ** -0.5))
            rounded = (nn(r.branch[...], down) * slope).astype(BF)
            r.ups[j] = jnp.sum(rounded.astype(F32), axis=0, keepdims=True)
            r.total[...] += nt(active, down)
            r.gn[...] += nt(rounded, up)
            r.w[3, :, columns] = nn(r.branch_t[...], active).astype(BF)
            r.w[2, :, columns] = nn(r.normed_t[...], rounded).astype(BF)
        for s in (2 * i, 2 * i + 1):
            red.start(s)
        for s in (2 * i, 2 * i + 1):
            red.tick(s)
        return carry

    lax.fori_loop(0, 4, mlp, 0)

    by_frame(r.total.at[pl.ds(0, rows)], r.y_send, r.mix)
    outs = []
    for d in range(1, 4):
        peer = (c + d) % 4
        copy = pltpu.make_async_remote_copy(
            src_ref=r.y_send.at[pl.ds(peer * 4, 4)], dst_ref=r.y_home.at[c],
            send_sem=r.ys.at[d], recv_sem=r.yq.at[d], device_id=(x, peer, z), device_id_type=MESH,
        )
        copy.start()
        outs.append(copy)
    y_own = pltpu.make_async_copy(r.y_send.at[pl.ds(c * 4, 4)], r.y_home.at[c], r.ys.at[0])
    y_own.start()

    norm_back_into(r.third, r.norm.at[2], r.gn, r.grad, va, 6)
    for copy in early[2:]:
        copy.wait()
    loads[1].wait()
    for t in range(4):
        r.o[t, rows:] = jnp.zeros((spare, r.o.shape[2]), BF)
    group = TG * frames
    att = Attention(
        share // TG, group, None, r.w.at[1], None,
        *(ref.at[:, pl.ds(0, rows)] for ref in (r.q, r.k, r.v)), r.o, small_probs(r.p, group),
    )

    def each(first):
        def after(i):
            red.start(first + i)
            maybe(i > 0 if first == 12 else None, lambda: red.tick(first + i))

        return after

    attention_back(
        att, frames_in, r.grad, r.norm.at[1], r.normed, r.normed_t, r.branch, r.branch_t,
        r.dk, r.dv, r.gn, r.w.at[1], r.bias1, va, 3, each(8),
    )
    for copy in kept:
        copy.start()
    by_frame(r.grad, r.g_send, r.mix)

    def to_frame(d):
        peer = (me + d) % 16
        return pltpu.make_async_remote_copy(
            src_ref=r.g_send.at[peer], dst_ref=r.g_recv.at[me],
            send_sem=r.gs.at[d], recv_sem=r.gq.at[d], device_id=(x, peer // 4, peer % 4), device_id_type=MESH,
        )

    def go(d, carry):
        to_frame(d).start()
        return carry

    lax.fori_loop(1, 16, go, 0)
    r.g_recv[me] = r.g_send[me]
    red.tick(12)
    for copy in kept:
        copy.wait()
    loads[0].wait()
    srows = clips * SP
    for clip in range(clips):
        for zz in range(4):
            row = clip * SP + zz * home_places
            r.rows_in[row : row + home_places] = r.x[zz, clip].astype(F32)
        r.rows_in[pl.ds(clip * SP + places, SP - places)] = jnp.zeros((SP - places, model), F32)
        r.total[pl.ds(clip * SP + places, SP - places)] = jnp.zeros((SP - places, model), F32)

    def come(d, carry):
        to_frame(d).wait()
        return carry

    lax.fori_loop(1, 16, come, 0)
    for cc in range(4):
        for zz in range(4):
            r.third[0:share] = r.g_recv[cc * 4 + zz].astype(F32)
            for start, count, clip, place in pair_segments(cc, share, clips, home_places):
                row = clip * SP + zz * home_places + place
                r.total[row : row + count] = r.third[start : start + count]

    att = Attention(clips, SP, None, r.w.at[0], None, r.q, r.k, r.v, r.o, spatial_probs(r.p))
    attention_back(
        att, r.rows_in, r.total, r.norm.at[0], r.normed, r.normed_t, r.branch, r.branch_t, r.dk, r.dv, r.gn,
        r.w.at[0], r.bias0, va, 0, each(12),
    )
    for zz in range(4):
        for clip in range(clips):
            row = clip * SP + zz * home_places
            r.third[0:home_places] = r.total[row : row + home_places]
            r.home_send[zz, clip] = r.third[0:home_places].astype(BF)
    for d in range(1, 4):
        peer = (z + d) % 4
        copy = pltpu.make_async_remote_copy(
            src_ref=r.home_send.at[peer], dst_ref=r.g_home.at[z],
            send_sem=r.hs.at[d], recv_sem=r.hq.at[d], device_id=(x, c, peer), device_id_type=MESH,
        )
        copy.start()
        outs.append(copy)
    g_own = pltpu.make_async_copy(r.home_send.at[z], r.g_home.at[z], r.hs.at[0])
    g_own.start()

    for j in range(r.ups.shape[0]):
        va[9 + j // halves : 10 + j // halves, (j % halves) * size : (j % halves + 1) * size] = r.ups[j]
    for i, ref in enumerate((r.bias0, r.bias1)):
        for t in range(4):
            va[16 + i * 8 + t * 2 : 18 + i * 8 + t * 2, 0:256] = ref[t]
    sides = ("core", "x", "y", "z1", "z2")

    def v_copy(j):
        return red.remote(r.va.at[j], r.vr.at[j], r.vs.at[j], r.vq.at[j], sides[j])

    v_copy(0).start()

    def rest(n, carry):
        red.tick(n)
        for j in range(5):

            @pl.when(n == STEPS + j)
            def _():
                v_copy(j).wait()
                if j < 4:
                    r.va[j + 1] = r.va[j] + r.vr[j]
                    v_copy(j + 1).start()
                else:
                    r.vectors[...] = r.va[j] + r.vr[j]

        return carry

    lax.fori_loop(STEPS, STEPS + 13, rest, 0)
    red.finish()
    for copy in outs:
        copy.wait()
    y_own.wait()
    g_own.wait()


def backward(x, rows_in, third, grad, whole, kept, norm, up_bias, down_bias, own_rows, width, frames):
    _, clips, home_places, model = x.shape
    rows, srows = third.shape[0], clips * SP
    places, share = home_places * 4, rows // frames
    size = 384
    anywhere, vmem = pl.BlockSpec(memory_space=pl.ANY), pl.BlockSpec(memory_space=pltpu.VMEM)
    args = (x, rows_in, third, grad, whole, *kept, norm, up_bias.reshape(-1, 1, size), down_bias)
    in_specs = [vmem] + [anywhere] * 14 + [vmem] * 3
    sub = (own_rows, width)
    big = max(rows, srows)

    def v(*dims, dtype=BF):
        return pltpu.VMEM(dims, dtype)

    def f(*dims):
        return pltpu.VMEM(dims, F32)

    dma = pltpu.SemaphoreType.DMA
    scratch = (
        [v(*whole.shape)]
        + [v(4, big, 256)] * 4
        + [v(4, clips, 3 * SP, SP)]
        + [f(big, model), f(big, model), f(rows, model), f(rows, model), f(big, model)]
        + [f(model // 128, rows, 128)]
        + [v(big, model), v(model, big), v(big, model), v(model, big), v(big, 256), v(big, 256)]
        + [v(frames, share, model), v(frames, share, model), v(frames, share, model)]
        + [v(4, clips, places // 4, model), f(4, 2, 256), f(4, 2, 256), f(up_bias.shape[0] // size, 1, size)]
        + [v(STEPS, 2, 2, *sub)]
        + [v(STEPS, *sub)] * 4
        + [v(PIECES, *sub)]
        + [f(5, 32, model)] * 2
        + [dma((4,))]
        + [dma((STEPS, 2, 2))] * 2
        + [dma((STEPS,))] * 9
        + [dma((5,))] * 2
        + [dma((4,))] * 2
        + [dma((16,))] * 2
        + [dma((4,))] * 2
        + [dma((5,))]
        + [dma((8,))]
    )
    return pl.pallas_call(
        back_kernel,
        out_shape=(
            shape(4, frames // 4, share, model),
            shape(4, clips, places // 4, model),
            shape(PIECES, *sub, dtype=F32),
            shape(32, model, dtype=F32),
        ),
        in_specs=in_specs,
        out_specs=[anywhere, anywhere, vmem, vmem],
        scratch_shapes=scratch,
        compiler_params=pltpu.CompilerParams(
            collective_id=2, has_side_effects=True, vmem_limit_bytes=67043328
        ),
        name="backward",
    )(*args)


def local(
    inputs,
    cotangent,
    norm_gain,
    norm_bias,
    attn_weight,
    attn_bias,
    out_weight,
    out_bias,
    up_weight,
    up_bias,
    down_weight,
    down_bias,
):
    ranks_c = lax.axis_size("ctx")
    tp_rank = lax.axis_index("tp")
    clips, frames, places, model = inputs.shape
    width = attn_weight.shape[3]

    shard = jnp.concatenate(
        [
            jnp.concatenate(
                [
                    attn_weight.transpose(0, 2, 1, 3).reshape(2, attn_weight.shape[2], 3 * width),
                    out_weight.transpose(0, 2, 1),
                ],
                axis=2,
            ),
            up_weight[None],
            down_weight.T[None],
        ]
    )
    norm = jnp.stack([norm_gain, norm_bias], axis=1)

    pairs = clips * places
    share = -(-pairs // ranks_c)
    share += -share % TG

    def home_to_spatial(values):
        return lax.all_to_all(values, "tp", split_axis=1, concat_axis=2, tiled=True)

    def spatial_to_home(values):
        return lax.all_to_all(values, "tp", split_axis=2, concat_axis=1, tiled=True)

    def home_to_temporal(values):
        rows = values.transpose(1, 0, 2, 3).reshape(frames, pairs, model)
        rows = jnp.pad(rows, ((0, 0), (0, share * ranks_c - pairs), (0, 0)))
        return lax.all_to_all(rows, "ctx", split_axis=1, concat_axis=0, tiled=True)

    def temporal_to_home(values):
        rows = lax.all_to_all(values, "ctx", split_axis=0, concat_axis=1, tiled=True)[:, :pairs]
        return rows.reshape(frames, clips, places, model).transpose(1, 0, 2, 3)

    ups = up_bias.shape[0] // model
    bias = jnp.pad(attn_bias, ((0, 0), (0, 6), (0, 256 - width)))
    if lax.axis_size("fsdp") == 2 and (ranks_c, lax.axis_size("tp")) == (4, 4):
        frames *= ranks_c
        whole, first, *kept = forward(shard, bias, inputs, cotangent, norm, out_bias, frames, share)
        kept, rows = kept[5:10] + kept[:5], kept[10:]
        home, grad_home, own, vectors = backward(
            first, *rows, whole, kept, norm, up_bias, down_bias[None], attn_weight.shape[2] // 4, up_weight.shape[1], frames
        )
        frames //= ranks_c
        outputs = home.transpose(1, 0, 2, 3).reshape(frames, -1, model)[:, :pairs]
        outputs = outputs.reshape(frames, clips, places, model).transpose(1, 0, 2, 3)
        input_grad = grad_home.transpose(1, 0, 2, 3)
        sums = vectors[16:, :256].reshape(2, 4, 2, 256)[..., :width].transpose(0, 2, 1, 3)
        attn_bias_sums = sums.reshape(2, 2, model)
    else:
        whole, bias = gather(shard, bias)
        bias = bias[:, :, :2].transpose(1, 0, 2, 3)
        first = home_to_spatial(inputs)
        spatial_shape = first.shape
        first = first.reshape((-1,) + first.shape[2:])
        second, *kept = spatial_forward(first, whole, bias[0], norm[0], out_bias[0:1])
        second = home_to_temporal(spatial_to_home(second.reshape(spatial_shape)))
        grad_out = home_to_temporal(cotangent)
        result, grad_second, grad_attn1, grad_up, grad_down, bias1, vec1, vec2, grad_up_bias = temporal(
            second, grad_out, whole, bias[1], norm[1], norm[2], out_bias[1:2], up_bias, down_bias[None]
        )
        outputs = temporal_to_home(result)
        grad_second = home_to_spatial(temporal_to_home(grad_second)).reshape(first.shape)
        grad_first, grad_attn0, bias0, vec0 = spatial_back(first, grad_second, whole, norm[0], kept)
        input_grad = spatial_to_home(grad_first.reshape(spatial_shape))
        bias_sums = jnp.stack([bias0, bias1])[..., :width].transpose(0, 2, 1, 3)
        lines = [vec0, vec1, vec2, grad_up_bias, bias_sums]
        flat = jnp.concatenate([line.reshape(-1, model) for line in lines])
        vectors = jnp.pad(flat, ((0, -flat.shape[0] % 8), (0, 0)))
        own, vectors = scatter([grad_attn0, grad_attn1, grad_up, grad_down], vectors)
        attn_bias_sums = vectors[9 + ups : 13 + ups].reshape(2, 2, model)
    triples = vectors[:9].reshape(3, 3, model)
    attn = own[:2].reshape(2, own.shape[1], 4, width)
    return (
        outputs,
        input_grad,
        triples[:, 0],
        triples[:, 1],
        attn[:, :, :3].transpose(0, 2, 1, 3),
        lax.dynamic_slice_in_dim(attn_bias_sums, tp_rank * width, width, 2),
        attn[:, :, 3].transpose(0, 2, 1),
        triples[:2, 2],
        own[2],
        vectors[9 : 9 + ups].reshape(-1),
        own[3].T,
        triples[2, 2],
    )


def solution(mesh):
    return jax.shard_map(
        local,
        mesh=mesh,
        in_specs=(
            P("fsdp", "ctx", "tp", None),
            P("fsdp", "ctx", "tp", None),
            P(),
            P(),
            P(None, None, "fsdp", "tp"),
            P(None, None, "tp"),
            P(None, "tp", "fsdp"),
            P(),
            P("fsdp", "tp"),
            P(),
            P("tp", "fsdp"),
            P(),
        ),
        out_specs=(
            P("fsdp", "ctx", "tp", None),
            P("fsdp", "ctx", "tp", None),
            P(),
            P(),
            P(None, None, ("fsdp", "ctx"), "tp"),
            P(None, None, "tp"),
            P(None, "tp", ("fsdp", "ctx")),
            P(),
            P(("fsdp", "ctx"), "tp"),
            P(),
            P("tp", ("fsdp", "ctx")),
            P(),
        ),
        check_vma=False,
    )
```
